32 devices in a mesh: block: 4 (over y, x), tok: 8 (over z, core).
Axes of the slice: x: 2, y: 2, z: 4, core: 2. Of those that a mesh axis runs over, the one named last changes fastest.
Arguments:
- queries: float32 [4096, 256], P(('block', 'tok')), may hold values from -6 to 6
- keys: float32 [4096, 256], P(('block', 'tok')), may hold values from -6 to 6
- values: float32 [4096, 256], P(('block', 'tok')), may hold values from -6 to 6
- rates: float32 [4096], P(('block', 'tok')), may hold values from 0.0001 to 0.001
- states: float32 [4, 3, 256, 256], P('block', None, 'tok'), may hold values from -0.375 to 0.375
- out_cot: float32 [4096, 256], P(('block', 'tok')), may hold values from -6 to 6
- final_cot: float32 [3, 256, 256], P(None, 'tok'), may hold values from -6 to 6
Outputs:
- d_queries: float32 [4096, 256], P(('block', 'tok'))
- d_keys: float32 [4096, 256], P(('block', 'tok'))
- d_values: float32 [4096, 256], P(('block', 'tok'))
- d_rates: float32 [4096], P(('block', 'tok'))
- d_states: float32 [4, 3, 256, 256], P('block', None, 'tok')
The draws below stay inside these ranges and needn't reach their ends.
All inputs are finite; a program needn't handle non-finite values.
Results may differ from the reference program's by a relative error of at most 0.00029.
Values sent between devices are 32-bit elements; how exact they have to be, the bound alone decides.
No kernel may reach another device: no remote copies, remote signals or barrier semaphores. Data moves between devices by JAX's collectives and lax.ppermute only.
A program may use at most 64 MiB of HBM per device.

```python
import math
import jax
import jax.numpy as jnp
from jax import lax

D = 256
TOKENS = 4096
N_BLOCK = 4


def block_levels(key, dims, pieces, low, largest):
    gain, own = 1.0, jax.random.fold_in(key, 6)
    for dim, parts in pieces:
        heights = jnp.exp(jax.random.uniform(jax.random.fold_in(own, dim), (parts,), jnp.float32, low / len(pieces), largest / len(pieces)))
        gain = gain * jnp.repeat(heights, dims[dim] // parts).reshape([-1 if axis == dim else 1 for axis in range(len(dims))])
    return gain


def bell_draw(key, extent, scale, bound, cuts=(), dtype=jnp.bfloat16):
    gain = block_levels(key, extent, cuts, -0.22, 0.18) if cuts else 1.0
    entries = jax.random.normal(key, extent, jnp.float32) * scale * gain
    return jnp.minimum(jnp.maximum(entries, -bound), bound).astype(dtype)


def setup_inputs(seed: int = 0) -> dict:
    key_list = jax.random.split(jax.random.key(seed), 8)
    queries = bell_draw(key_list[0], (TOKENS, D), 1.0, 6.0, ((0, 32),), jnp.float32)
    keys = bell_draw(key_list[1], (TOKENS, D), 1.0, 6.0, ((0, 32),), jnp.float32)
    values = bell_draw(key_list[2], (TOKENS, D), 1.0, 6.0, ((0, 32),), jnp.float32)
    rates = jnp.clip(jnp.exp(math.log(0.001) - 2.3025852 * jax.random.uniform(key_list[3], (TOKENS,), jnp.float32) ** block_levels(key_list[3], (TOKENS,), ((0, 32),), -0.2, 0.2)), 0.0001, 0.001)
    states = bell_draw(key_list[4], (N_BLOCK, 3, D, D), D ** -0.5, 0.375, ((0, 4), (2, 8)), jnp.float32)
    out_cot = bell_draw(key_list[5], (TOKENS, D), 1.0, 6.0, ((0, 32),), jnp.float32)
    final_cot = bell_draw(key_list[6], (3, D, D), 1.0, 6.0, ((1, 8),), jnp.float32)
    return dict(queries=queries, keys=keys, values=values, rates=rates, states=states, out_cot=out_cot, final_cot=final_cot)


EPS = 1e-06
HIGH = lax.Precision.HIGHEST

def apply_fast(weights, inputs):
    first = jnp.dot(inputs, weights[0], precision=HIGH, preferred_element_type=jnp.float32)
    gate = jnp.dot(inputs, weights[1], precision=HIGH, preferred_element_type=jnp.float32)
    mixed = jax.nn.silu(first) * gate
    return jnp.dot(mixed, weights[2], precision=HIGH, preferred_element_type=jnp.float32)

def update_grad(weights, keys, values, rates):

    def loss(current):
        return -jnp.sum(rates[:, None] * apply_fast(current, keys) * values)
    return jax.grad(loss)(weights)

def renorm(weights, grads):
    shifted = weights - grads
    row_norm = jnp.sqrt(lax.optimization_barrier(jnp.sum(weights * weights, axis=-1, keepdims=True)) + EPS)
    new_norm = jnp.sqrt(lax.optimization_barrier(jnp.sum(shifted * shifted, axis=-1, keepdims=True)) + EPS)
    return shifted * (row_norm / new_norm)

def block_map(weights, queries, keys, values, rates):
    return (apply_fast(weights, queries), renorm(weights, update_grad(weights, keys, values, rates)))

def reference(queries, keys, values, rates, states, out_cot, final_cot):
    length = queries.shape[0] // N_BLOCK
    incoming = final_cot
    grad_q = [None] * N_BLOCK
    grad_k = [None] * N_BLOCK
    grad_v = [None] * N_BLOCK
    grad_r = [None] * N_BLOCK
    grad_s = [None] * N_BLOCK
    for index in range(N_BLOCK - 1, -1, -1):
        start = index * length
        stop = start + length
        _, backward = jax.vjp(block_map, states[index], queries[start:stop], keys[start:stop], values[start:stop], rates[start:stop])
        d_weights, d_q, d_k, d_v, d_r = backward((out_cot[start:stop], incoming))
        grad_q[index] = d_q
        grad_k[index] = d_k
        grad_v[index] = d_v
        grad_r[index] = d_r
        grad_s[index] = d_weights
        incoming = d_weights
    return (jnp.concatenate(grad_q, axis=0), jnp.concatenate(grad_k, axis=0), jnp.concatenate(grad_v, axis=0), jnp.concatenate(grad_r, axis=0), jnp.stack(grad_s, axis=0))
```

```python
import jax
import jax.numpy as jnp
from jax import lax
from jax.sharding import PartitionSpec as P

EPS = 1e-06
HIGH = lax.Precision.HIGHEST


def mm(left, right):
    return lax.dot_general(left, right, (((1,), (0,)), ((), ())), precision=HIGH, preferred_element_type=jnp.float32)


def mm_nt(left, right):
    return lax.dot_general(left, right, (((1,), (1,)), ((), ())), precision=HIGH, preferred_element_type=jnp.float32)


def mm_tn(left, right):
    return lax.dot_general(left, right, (((0,), (0,)), ((), ())), precision=HIGH, preferred_element_type=jnp.float32)


def silu_parts(first):
    sig = 1.0 / (1.0 + jnp.exp(-first))
    slope = sig * (1.0 - sig)
    value = first * sig
    d_one = sig + first * slope
    d_two = slope * (2.0 + first * (1.0 - 2.0 * sig))
    return value, d_one, d_two


def direct(size):
    return size % 2 == 0 and size <= 16


def chip_shift(array, by):
    size = lax.axis_size("tok")
    return lax.ppermute(array, "tok", [(j, (j + 2 * by) % size) for j in range(size)])


def core_swap(array):
    size = lax.axis_size("tok")
    return lax.ppermute(array, "tok", [(j, j ^ 1) for j in range(size)])


def gather_pieces(array):
    size = lax.axis_size("tok")
    if not direct(size):
        return lax.all_gather(array, "tok")
    mine = jnp.stack([array] + [chip_shift(array, by) for by in range(1, size // 2)])
    return jnp.concatenate([mine, core_swap(mine)])


def spread_sum(pieces):
    size = lax.axis_size("tok")
    if not direct(size):
        return lax.psum_scatter(pieces, "tok")
    half = size // 2
    mine = pieces[:half] + core_swap(pieces[half:])
    total = mine[0]
    for by in range(1, half):
        total = total + chip_shift(mine[by], -by)
    return total


def sum_all(array):
    size = lax.axis_size("tok")
    if not direct(size):
        return jnp.sum(lax.all_gather(array, "tok"), axis=0)
    array = array + core_swap(array)
    total = array
    for by in range(1, size // 2):
        total = total + chip_shift(array, by)
    return total


def rows_to_hidden(rows):
    size = lax.axis_size("tok")
    count, depth, width = rows.shape
    parts = rows.reshape(count, depth, size, width // size).transpose(2, 0, 3, 1)
    parts = lax.all_to_all(parts, "tok", 0, 0)
    return parts.transpose(1, 2, 0, 3).reshape(count, width // size, depth * size)


def hidden_to_rows(slices):
    size = lax.axis_size("tok")
    count, depth, width = slices.shape
    parts = slices.reshape(count, depth, size, width // size).transpose(2, 0, 1, 3)
    parts = lax.all_to_all(parts, "tok", 0, 0)
    return parts.transpose(1, 3, 0, 2).reshape(count, width // size, depth * size)


def to_block(array, source, target, by=0):
    size = lax.axis_size("tok")
    pairs = [(source * size + j, target * size + (j + by) % size) for j in range(size)]
    return lax.ppermute(array, ("block", "tok"), pairs)


def up_one(array):
    groups = lax.axis_size("block")
    return lax.ppermute(array, "block", [(i, i + 1) for i in range(groups - 1)])


def slice_forward(weights, keys, scaled):
    first, gate = mm_nt(weights[0], keys), mm_nt(weights[1], keys)
    value, d_one, d_two = silu_parts(first)
    d_mixed = mm_nt(weights[2], scaled)
    mixed = value * gate
    d_gate = d_mixed * value
    d_first = d_mixed * gate * d_one
    grads = jnp.stack([mm(d_first, keys), mm(d_gate, keys), mm(mixed, scaled)])
    return grads, (gate, value, d_one, d_two, d_mixed)


def slice_adjoint(cot, kept, keys, scaled):
    gate, value, d_one, d_two, d_mixed = kept
    t_first, t_gate, p_mixed = mm_nt(cot[0], keys), mm_nt(cot[1], keys), mm_nt(cot[2], scaled)
    t_mixed = d_one * t_first * gate + value * t_gate
    c_gate = p_mixed * value + d_mixed * d_one * t_first
    c_first = p_mixed * gate * d_one + d_mixed * (d_two * t_first * gate + d_one * t_gate)
    return jnp.stack([mm(c_first, keys), mm(c_gate, keys), mm(t_mixed, scaled)])


def query_adjoint(weights, queries, out_cot):
    first, gate = mm_nt(queries, weights[0]), mm_nt(queries, weights[1])
    value, d_one, _ = silu_parts(first)
    d_mixed = mm_nt(out_cot, weights[2])
    d_gate = d_mixed * value
    d_first = d_mixed * gate * d_one
    d_queries = mm(d_first, weights[0]) + mm(d_gate, weights[1])
    d_weights = jnp.stack([mm_tn(d_first, queries), mm_tn(d_gate, queries), mm_tn(value * gate, out_cot)])
    return d_queries, d_weights


def token_adjoint(weights, cot, keys, scaled):
    first, gate = mm_nt(keys, weights[0]), mm_nt(keys, weights[1])
    value, d_one, d_two = silu_parts(first)
    d_mixed = mm_nt(scaled, weights[2])
    mixed = value * gate
    d_gate = d_mixed * value
    d_first = d_mixed * gate * d_one
    t_first, t_gate, p_mixed = mm_nt(keys, cot[0]), mm_nt(keys, cot[1]), mm_nt(scaled, cot[2])
    t_mixed = d_one * t_first * gate + value * t_gate
    c_gate = p_mixed * value + d_mixed * d_one * t_first
    c_first = p_mixed * gate * d_one + d_mixed * (d_two * t_first * gate + d_one * t_gate)
    d_keys = mm(c_first, weights[0]) + mm(c_gate, weights[1]) + mm(d_first, cot[0]) + mm(d_gate, cot[1])
    t_out = mm(t_mixed, weights[2]) + mm(mixed, cot[2])
    return d_keys, t_out


def over_hidden(array):
    return jnp.sum(array[:2], axis=1)


def per_device(queries, keys, values, rates, states, out_cot, final_cot):
    groups, size = lax.axis_size("block"), lax.axis_size("tok")
    position = lax.axis_index("block")
    own_rows = states[0]
    scaled = -rates[:, None] * values
    both = gather_pieces(jnp.stack([keys, scaled]))
    width = keys.shape[1]
    all_keys = both[:, 0].reshape(-1, width)
    all_scaled = both[:, 1].reshape(-1, width)
    split = rows_to_hidden(jnp.concatenate([own_rows[:2], final_cot[:2]]))
    own = jnp.concatenate([split[:2], own_rows[2:]])
    last = jnp.concatenate([split[2:], final_cot[2:]])
    grads, kept = slice_forward(own, all_keys, all_scaled)
    shifted = own - grads
    earlier = up_one(shifted[:2])
    sums = sum_all(jnp.concatenate([over_hidden(own * own), over_hidden(shifted * shifted), over_hidden(last * shifted)]))
    row_norm = [jnp.sqrt(sums[0:2, None, :] + EPS), jnp.sqrt(jnp.sum(own[2:] ** 2, axis=-1, keepdims=True) + EPS)]
    new_norm = [jnp.sqrt(sums[2:4, None, :] + EPS), jnp.sqrt(jnp.sum(shifted[2:] ** 2, axis=-1, keepdims=True) + EPS)]

    pieces = gather_pieces(own)
    whole = pieces.transpose(1, 0, 2, 3).reshape(3, -1, width)
    d_queries, d_weights = query_adjoint(whole, queries, out_cot)
    apply_state = spread_sum(d_weights.reshape(3, size, -1, width).transpose(1, 0, 2, 3))

    is_last = position == groups - 1
    incoming = jnp.where(is_last, last, 0.0)
    inner = jnp.where(is_last, sums[4:6], 0.0)
    for section in range(groups):
        inners = [inner[:, None, :], jnp.sum(incoming[2:] * shifted[2:], axis=-1, keepdims=True)]
        cots, straights = [], []
        for part, dot, old, new in zip((slice(0, 2), slice(2, 3)), inners, row_norm, new_norm):
            d_shifted = old / new * incoming[part] - old * dot / (new * new * new) * shifted[part]
            cots.append(-d_shifted)
            straights.append(d_shifted + dot / new * own[part] / old)
        cot = jnp.concatenate(cots)
        straight = jnp.concatenate(straights)
        rows_now = slice_adjoint(cot, kept, all_keys, all_scaled) + apply_state + straight
        if section + 1 < groups:
            source = groups - 1 - section
            partial = over_hidden(rows_now[:2] * earlier)
            incoming = incoming + to_block(rows_now, source, source - 1)
            if direct(size):
                for by in range(size):
                    inner = inner + to_block(partial, source, source - 1, by)
            else:
                inner = inner + to_block(sum_all(partial), source, source - 1)
    cot_pieces = gather_pieces(cot)
    whole_cot = cot_pieces.transpose(1, 0, 2, 3).reshape(3, -1, width)
    d_keys, t_out = token_adjoint(whole, whole_cot, keys, scaled)
    d_values = -rates[:, None] * t_out
    d_rates = -jnp.sum(values * t_out, axis=-1)
    d_rows = jnp.concatenate([hidden_to_rows(rows_now[:2]), rows_now[2:]])
    return (d_queries, d_keys, d_values, d_rates, d_rows[None])


def solution(mesh):
    return jax.shard_map(
        per_device,
        mesh=mesh,
        in_specs=(
            P(("block", "tok"), None),
            P(("block", "tok"), None),
            P(("block", "tok"), None),
            P(("block", "tok")),
            P("block", None, "tok", None),
            P(("block", "tok"), None),
            P(None, "tok", None),
        ),
        out_specs=(
            P(("block", "tok"), None),
            P(("block", "tok"), None),
            P(("block", "tok"), None),
            P(("block", "tok")),
            P("block", None, "tok", None),
        ),
        check_vma=False,
    )
```

```python
import jax
import jax.numpy as jnp
from jax import lax
from jax.experimental import pallas as pl
from jax.experimental.pallas import tpu as pltpu
from jax.sharding import PartitionSpec as P

EPS = 1e-06
HIGH = lax.Precision.HIGHEST


def mm(left, right):
    return lax.dot_general(left, right, (((1,), (0,)), ((), ())), precision=HIGH, preferred_element_type=jnp.float32)


def mm_nt(left, right):
    return lax.dot_general(left, right, (((1,), (1,)), ((), ())), precision=HIGH, preferred_element_type=jnp.float32)


def mm_tn(left, right):
    return lax.dot_general(left, right, (((0,), (0,)), ((), ())), precision=HIGH, preferred_element_type=jnp.float32)


def silu_parts(first):
    sig = 1.0 / (1.0 + jnp.exp(-first))
    slope = sig * (1.0 - sig)
    value = first * sig
    d_one = sig + first * slope
    d_two = slope * (2.0 + first * (1.0 - 2.0 * sig))
    return value, d_one, d_two


def direct(size):
    return size % 2 == 0 and size <= 16


def chip_shift(array, by):
    size = lax.axis_size("tok")
    return lax.ppermute(array, "tok", [(j, (j + 2 * by) % size) for j in range(size)])


def core_swap(array):
    size = lax.axis_size("tok")
    return lax.ppermute(array, "tok", [(j, j ^ 1) for j in range(size)])


def gather_pieces(array):
    size = lax.axis_size("tok")
    if not direct(size):
        return lax.all_gather(array, "tok")
    mine = jnp.stack([array] + [chip_shift(array, by) for by in range(1, size // 2)])
    return jnp.concatenate([mine, core_swap(mine)])


def spread_sum(pieces):
    size = lax.axis_size("tok")
    if not direct(size):
        return lax.psum_scatter(pieces, "tok")
    half = size // 2
    mine = pieces[:half] + core_swap(pieces[half:])
    total = mine[0]
    for by in range(1, half):
        total = total + chip_shift(mine[by], -by)
    return total


def sum_all(array):
    size = lax.axis_size("tok")
    if not direct(size):
        return jnp.sum(lax.all_gather(array, "tok"), axis=0)
    array = array + core_swap(array)
    total = array
    for by in range(1, size // 2):
        total = total + chip_shift(array, by)
    return total


def rows_to_hidden(rows):
    size = lax.axis_size("tok")
    count, depth, width = rows.shape
    parts = rows.reshape(count, depth, size, width // size).transpose(2, 0, 3, 1)
    parts = lax.all_to_all(parts, "tok", 0, 0)
    return parts.transpose(1, 2, 0, 3).reshape(count, width // size, depth * size)


def hidden_to_rows(slices):
    size = lax.axis_size("tok")
    count, depth, width = slices.shape
    parts = slices.reshape(count, depth, size, width // size).transpose(2, 0, 1, 3)
    parts = lax.all_to_all(parts, "tok", 0, 0)
    return parts.transpose(1, 3, 0, 2).reshape(count, width // size, depth * size)


def to_block(array, source, target, by=0):
    size = lax.axis_size("tok")
    pairs = [(source * size + j, target * size + (j + by) % size) for j in range(size)]
    return lax.ppermute(array, ("block", "tok"), pairs)


def up_one(array):
    groups = lax.axis_size("block")
    return lax.ppermute(array, "block", [(i, i + 1) for i in range(groups - 1)])


def slice_forward(weights, keys, scaled):
    first, gate = mm_nt(weights[0], keys), mm_nt(weights[1], keys)
    value, d_one, d_two = silu_parts(first)
    d_mixed = mm_nt(weights[2], scaled)
    mixed = value * gate
    d_gate = d_mixed * value
    d_first = d_mixed * gate * d_one
    grads = jnp.stack([mm(d_first, keys), mm(d_gate, keys), mm(mixed, scaled)])
    return grads, (gate, value, d_one, d_two, d_mixed)


def slice_adjoint(cot, kept, keys, scaled):
    gate, value, d_one, d_two, d_mixed = kept
    t_first, t_gate, p_mixed = mm_nt(cot[0], keys), mm_nt(cot[1], keys), mm_nt(cot[2], scaled)
    t_mixed = d_one * t_first * gate + value * t_gate
    c_gate = p_mixed * value + d_mixed * d_one * t_first
    c_first = p_mixed * gate * d_one + d_mixed * (d_two * t_first * gate + d_one * t_gate)
    return jnp.stack([mm(c_first, keys), mm(c_gate, keys), mm(t_mixed, scaled)])


def query_adjoint(weights, queries, out_cot):
    first, gate = mm_nt(queries, weights[0]), mm_nt(queries, weights[1])
    value, d_one, _ = silu_parts(first)
    d_mixed = mm_nt(out_cot, weights[2])
    d_gate = d_mixed * value
    d_first = d_mixed * gate * d_one
    d_queries = mm(d_first, weights[0]) + mm(d_gate, weights[1])
    d_weights = jnp.stack([mm_tn(d_first, queries), mm_tn(d_gate, queries), mm_tn(value * gate, out_cot)])
    return d_queries, d_weights


def token_adjoint(weights, cot, keys, scaled):
    first, gate = mm_nt(keys, weights[0]), mm_nt(keys, weights[1])
    value, d_one, d_two = silu_parts(first)
    d_mixed = mm_nt(scaled, weights[2])
    mixed = value * gate
    d_gate = d_mixed * value
    d_first = d_mixed * gate * d_one
    t_first, t_gate, p_mixed = mm_nt(keys, cot[0]), mm_nt(keys, cot[1]), mm_nt(scaled, cot[2])
    t_mixed = d_one * t_first * gate + value * t_gate
    c_gate = p_mixed * value + d_mixed * d_one * t_first
    c_first = p_mixed * gate * d_one + d_mixed * (d_two * t_first * gate + d_one * t_gate)
    d_keys = mm(c_first, weights[0]) + mm(c_gate, weights[1]) + mm(d_first, cot[0]) + mm(d_gate, cot[1])
    t_out = mm(t_mixed, weights[2]) + mm(mixed, cot[2])
    return d_keys, t_out


def over_hidden(array):
    return jnp.sum(array[:2], axis=1)


def per_device_general(queries, keys, values, rates, states, out_cot, final_cot):
    groups, size = lax.axis_size("block"), lax.axis_size("tok")
    position = lax.axis_index("block")
    own_rows = states[0]
    scaled = -rates[:, None] * values
    both = gather_pieces(jnp.stack([keys, scaled]))
    width = keys.shape[1]
    all_keys = both[:, 0].reshape(-1, width)
    all_scaled = both[:, 1].reshape(-1, width)
    split = rows_to_hidden(jnp.concatenate([own_rows[:2], final_cot[:2]]))
    own = jnp.concatenate([split[:2], own_rows[2:]])
    last = jnp.concatenate([split[2:], final_cot[2:]])
    grads, kept = slice_forward(own, all_keys, all_scaled)
    shifted = own - grads
    earlier = up_one(shifted[:2])
    sums = sum_all(jnp.concatenate([over_hidden(own * own), over_hidden(shifted * shifted), over_hidden(last * shifted)]))
    row_norm = [jnp.sqrt(sums[0:2, None, :] + EPS), jnp.sqrt(jnp.sum(own[2:] ** 2, axis=-1, keepdims=True) + EPS)]
    new_norm = [jnp.sqrt(sums[2:4, None, :] + EPS), jnp.sqrt(jnp.sum(shifted[2:] ** 2, axis=-1, keepdims=True) + EPS)]

    pieces = gather_pieces(own)
    whole = pieces.transpose(1, 0, 2, 3).reshape(3, -1, width)
    d_queries, d_weights = query_adjoint(whole, queries, out_cot)
    apply_state = spread_sum(d_weights.reshape(3, size, -1, width).transpose(1, 0, 2, 3))

    is_last = position == groups - 1
    incoming = jnp.where(is_last, last, 0.0)
    inner = jnp.where(is_last, sums[4:6], 0.0)
    for section in range(groups):
        inners = [inner[:, None, :], jnp.sum(incoming[2:] * shifted[2:], axis=-1, keepdims=True)]
        cots, straights = [], []
        for part, dot, old, new in zip((slice(0, 2), slice(2, 3)), inners, row_norm, new_norm):
            d_shifted = old / new * incoming[part] - old * dot / (new * new * new) * shifted[part]
            cots.append(-d_shifted)
            straights.append(d_shifted + dot / new * own[part] / old)
        cot = jnp.concatenate(cots)
        straight = jnp.concatenate(straights)
        rows_now = slice_adjoint(cot, kept, all_keys, all_scaled) + apply_state + straight
        if section + 1 < groups:
            source = groups - 1 - section
            partial = over_hidden(rows_now[:2] * earlier)
            incoming = incoming + to_block(rows_now, source, source - 1)
            if direct(size):
                for by in range(size):
                    inner = inner + to_block(partial, source, source - 1, by)
            else:
                inner = inner + to_block(sum_all(partial), source, source - 1)
    cot_pieces = gather_pieces(cot)
    whole_cot = cot_pieces.transpose(1, 0, 2, 3).reshape(3, -1, width)
    d_keys, t_out = token_adjoint(whole, whole_cot, keys, scaled)
    d_values = -rates[:, None] * t_out
    d_rates = -jnp.sum(values * t_out, axis=-1)
    d_rows = jnp.concatenate([hidden_to_rows(rows_now[:2]), rows_now[2:]])
    return (d_queries, d_keys, d_values, d_rates, d_rows[None])


def halves(array):
    upper = array.astype(jnp.bfloat16)
    return upper, (array - upper.astype(jnp.float32)).astype(jnp.bfloat16)


def product(left, right, contract):
    def one(a, b):
        return lax.dot_general(a, b, (((1,), (contract,)), ((), ())), preferred_element_type=jnp.float32)

    return one(left[0], right[0]) + (one(left[0], right[1]) + one(left[1], right[0]))


def nn(left, right):
    return product(left, right, 0)


def nt(left, right):
    return product(left, right, 1)


def kernel_call(body, name, outs, *operands, flag=None):
    specs = [pl.BlockSpec(memory_space=pltpu.VMEM) for _ in operands]
    if flag is not None:
        specs = [pl.BlockSpec(memory_space=pltpu.SMEM)] + specs
        operands = (flag,) + operands
    return pl.pallas_call(
        body,
        name=name,
        in_specs=specs,
        out_specs=[pl.BlockSpec(memory_space=pltpu.VMEM) for _ in outs],
        out_shape=[jax.ShapeDtypeStruct(shape, dtype) for shape, dtype in outs],
    )(*operands)


def f32(*shape):
    return shape, jnp.float32


def bf16(*shape):
    return shape, jnp.bfloat16


def column(row, width):
    block = jnp.broadcast_to(row, (128, row.shape[1])).T
    return jnp.concatenate([block] * (width // 128), axis=1)


def pack_body(values, rates, rows, final, scaled, packed):
    scaled[...] = -column(rates[...], values.shape[1]) * values[...]
    depth, width = rows.shape[1:]
    count = packed.shape[0] // depth
    span = width // count
    for peer in range(count):
        cut = slice(peer * span, (peer + 1) * span)
        parts = [rows[0, :, cut], rows[1, :, cut], final[0, :, cut], final[1, :, cut]]
        packed[peer * depth : (peer + 1) * depth, :] = jnp.concatenate(parts, axis=1)


def unpack_body(flag, arrived, rows, final, own, last):
    span = own.shape[1]
    turned = arrived[...].T
    own[0] = turned[:span]
    own[1] = turned[span : 2 * span]
    own[2] = rows[2]
    keep = jnp.where(flag[0] != 0, 1.0, 0.0)
    last[0] = turned[2 * span : 3 * span] * keep
    last[1] = turned[3 * span :] * keep
    last[2] = final[2] * keep


CHUNK = 256


def forward_body(own, last, *refs):
    pieces = (len(refs) - 7) // 2
    keys, scaled = refs[:pieces], refs[pieces : 2 * pieces]
    key_high, key_low, scaled_high, scaled_low, kept, shifted, sums = refs[2 * pieces :]
    depth = keys[0].shape[0]
    for index in range(pieces):
        cut = slice(index * depth, (index + 1) * depth)
        key_high[cut, :], key_low[cut, :] = halves(keys[index][...])
        scaled_high[cut, :], scaled_low[cut, :] = halves(scaled[index][...])
    span = own.shape[1]
    pair = halves(jnp.concatenate([own[0], own[1]]))
    second = halves(own[2])
    grad_pair, grad_second = 0.0, 0.0
    for start in range(0, pieces * depth, CHUNK):
        cut = slice(start, start + CHUNK)
        key_cut = key_high[cut, :], key_low[cut, :]
        scaled_cut = scaled_high[cut, :], scaled_low[cut, :]
        both = nt(pair, key_cut)
        d_mixed = nt(second, scaled_cut)
        first, gate = both[:span], both[span:]
        value, d_one, d_two = silu_parts(first)
        for place, array in enumerate((gate, value, d_one, d_two, d_mixed)):
            kept[place, :, cut] = array
        d_pair = jnp.concatenate([d_mixed * gate * d_one, d_mixed * value])
        grad_pair += nn(halves(d_pair), key_cut)
        grad_second += nn(halves(value * gate), scaled_cut)
    moved = own[0] - grad_pair[:span], own[1] - grad_pair[span:], own[2] - grad_second
    rows = []
    for left, right in ((own, own), (moved, moved), (last, moved)):
        rows += [jnp.sum(left[m] * right[m], axis=0, keepdims=True) for m in range(2)]
    sums[...] = jnp.concatenate(rows + [jnp.zeros((2, own.shape[2]), jnp.float32)])
    for m in range(3):
        shifted[m] = moved[m]


def state_terms(own, shifted, last, sums, inners, arrived):
    span = own.shape[1]
    total = sums[0][...] + sums[1][...]
    inner = total[4:6]
    for array in inners:
        inner = inner + array[0:2]
    cots, straights = [], []
    for m in range(3):
        incoming = last[m]
        for array in arrived:
            incoming = incoming + array[m * span : (m + 1) * span, :]
        if m < 2:
            dot, old, new = inner[m : m + 1], jnp.sqrt(total[m : m + 1] + EPS), jnp.sqrt(total[m + 2 : m + 3] + EPS)
        else:
            dot = jnp.sum(incoming * shifted[m], axis=-1, keepdims=True)
            old = jnp.sqrt(jnp.sum(own[m] * own[m], axis=-1, keepdims=True) + EPS)
            new = jnp.sqrt(jnp.sum(shifted[m] * shifted[m], axis=-1, keepdims=True) + EPS)
        d_shifted = old / new * incoming - old * dot / (new * new * new) * shifted[m]
        cots.append(-d_shifted)
        straights.append(d_shifted + dot / new * own[m] / old)
    return cots, straights


def terms_body(count, *refs):
    own, shifted, last, sum_a, sum_b = refs[:5]
    inners, arrived = refs[5 : 5 + 2 * count], refs[5 + 2 * count : 5 + 3 * count]
    cot = refs[-1]
    cots, _ = state_terms(own, shifted, last, (sum_a, sum_b), inners, arrived)
    for m in range(3):
        cot[m] = cots[m]


def section_body(count, final, flag, *refs):
    own, shifted, last, sum_a, sum_b, earlier = refs[:6]
    key_high, key_low, scaled_high, scaled_low, kept = refs[6:11]
    refs = refs[11:]
    inners, arrived, refs = refs[: 2 * count], refs[2 * count : 3 * count], refs[3 * count :]
    applied, outs = refs[:-2], refs[-2:]
    span = own.shape[1]

    @pl.when(flag[0] != 0)
    def _():
        cots, straights = state_terms(own, shifted, last, (sum_a, sum_b), inners, arrived)
        pair = halves(jnp.concatenate(cots[:2]))
        second = halves(cots[2])
        d_pair, d_second = 0.0, 0.0
        for start in range(0, key_high.shape[0], CHUNK):
            cut = slice(start, start + CHUNK)
            key_cut = key_high[cut, :], key_low[cut, :]
            scaled_cut = scaled_high[cut, :], scaled_low[cut, :]
            gate, value, d_one, d_two, d_mixed = [kept[place, :, cut] for place in range(5)]
            both = nt(pair, key_cut)
            p_mixed = nt(second, scaled_cut)
            t_first, t_gate = both[:span], both[span:]
            lift = d_one * t_first
            t_mixed = lift * gate + value * t_gate
            c_gate = p_mixed * value + d_mixed * lift
            c_first = p_mixed * gate * d_one + d_mixed * (d_two * t_first * gate + d_one * t_gate)
            d_pair += nn(halves(jnp.concatenate([c_first, c_gate])), key_cut)
            d_second += nn(halves(t_mixed), scaled_cut)
        rows = [d_pair[:span] + straights[0], d_pair[span:] + straights[1], d_second + straights[2]]
        for array in applied:
            rows = [row + array[m * span : (m + 1) * span, :] for m, row in enumerate(rows)]
        width = own.shape[2]
        if final:
            out_pair, out_second = outs
            out_pair[...] = jnp.concatenate([rows[0], rows[1], jnp.zeros((128 - 2 * span, width), jnp.float32)]).T
            out_second[...] = rows[2]
        else:
            payload, partial = outs
            sums = [jnp.sum(rows[m] * earlier[m], axis=0, keepdims=True) for m in range(2)]
            tail = jnp.concatenate(sums + [jnp.zeros((6, width), jnp.float32)])
            partial[...] = tail
            payload[...] = jnp.concatenate(rows + [tail])


def load_halves(pieces, part):
    return halves(jnp.concatenate([piece[part] for piece in pieces]))


def query_body(queries, out_cot, *refs):
    size = (len(refs) - 1) // 2
    pieces, d_queries, outs = refs[:size], refs[size], refs[size + 1 :]
    span = pieces[0].shape[1]
    one, three, two = [load_halves(pieces, part) for part in range(3)]
    query, cot = halves(queries[...]), halves(out_cot[...])
    first, gate = nt(query, one), nt(query, three)
    value, d_one, _ = silu_parts(first)
    d_mixed = nt(cot, two)
    d_gate = d_mixed * value
    d_first = d_mixed * gate * d_one
    d_queries[...] = nn(halves(d_first), one) + nn(halves(d_gate), three)
    parts = nn(halves(d_first.T), query), nn(halves(d_gate.T), query), nn(halves((value * gate).T), cot)
    for index, out in enumerate(outs):
        out[...] = jnp.concatenate([part[index * span : (index + 1) * span] for part in parts])


def token_body(keys, values, rates, arrived, second, *refs):
    size = (len(refs) - 4) // 2
    weights, cots = refs[:size], refs[size : 2 * size]
    d_keys, d_values, d_rates, d_rows = refs[2 * size :]
    width = keys.shape[1]
    one, three, two = [load_halves(weights, part) for part in range(3)]
    c_one, c_three, c_two = [load_halves(cots, part) for part in range(3)]
    rate = column(rates[...], width)
    key, scaled = halves(keys[...]), halves(-rate * values[...])
    first, gate = nt(key, one), nt(key, three)
    value, d_one, d_two = silu_parts(first)
    d_mixed = nt(scaled, two)
    t_first, t_gate, p_mixed = nt(key, c_one), nt(key, c_three), nt(scaled, c_two)
    mixed = value * gate
    d_gate = d_mixed * value
    d_first = d_mixed * gate * d_one
    lift = d_one * t_first
    t_mixed = lift * gate + value * t_gate
    c_gate = p_mixed * value + d_mixed * lift
    c_first = p_mixed * gate * d_one + d_mixed * (d_two * t_first * gate + d_one * t_gate)
    d_keys[...] = nn(halves(c_first), one) + nn(halves(c_gate), three) + nn(halves(d_first), c_one) + nn(halves(d_gate), c_three)
    t_out = nn(halves(t_mixed), two) + nn(halves(mixed), c_two)
    d_values[...] = -rate * t_out
    d_rates[...] = -jnp.sum((values[...] * t_out).T, axis=0, keepdims=True)
    depth, span = d_rows.shape[1], weights[0].shape[1]
    for m in range(2):
        parts = [arrived[j * depth : (j + 1) * depth, m * span : (m + 1) * span] for j in range(size)]
        d_rows[m] = jnp.concatenate(parts, axis=1)
    d_rows[2] = second[...]


def gather_list(array):
    size = lax.axis_size("tok")
    mine = [array] + [chip_shift(array, by) for by in range(1, size // 2)]
    return mine + [core_swap(piece) for piece in mine]


def per_device(queries, keys, values, rates, states, out_cot, final_cot):
    groups, size = lax.axis_size("block"), lax.axis_size("tok")
    depth, width = keys.shape
    span = width // size
    rows = states.shape[2]
    if not (direct(size) and 4 * span == 128 and depth % 128 == 0 and width % 128 == 0):
        return per_device_general(queries, keys, values, rates, states, out_cot, final_cot)
    tokens = depth * size
    position = lax.axis_index("block")
    own_rows = states[0]
    rates_row = rates.reshape(1, depth)
    scaled, packed = kernel_call(
        pack_body, "pack", [f32(depth, width), f32(width, 4 * span)], values, rates_row, own_rows, final_cot
    )
    turned = lax.all_to_all(packed, "tok", 0, 0, tiled=True)
    key_pieces = gather_list(keys)
    scaled_pieces = gather_list(scaled)
    is_last = (position == groups - 1).astype(jnp.int32).reshape(1)
    state = f32(3, span, width)
    own, last = kernel_call(unpack_body, "unpack", [state, state], turned, own_rows, final_cot, flag=is_last)
    half = bf16(tokens, width)
    *halved, kept, shifted, sums = kernel_call(
        forward_body,
        "forward",
        [half, half, half, half, f32(5, span, tokens), state, f32(8, width)],
        own,
        last,
        *key_pieces,
        *scaled_pieces,
    )
    earlier = up_one(shifted[:2])
    sum_a = sums
    for by in range(1, size // 2):
        sum_a = sum_a + chip_shift(sums, by)
    sum_b = core_swap(sum_a)

    pieces = gather_list(own)
    piece = f32(3 * span, width)
    d_queries, *parts = kernel_call(query_body, "query", [f32(depth, width)] + [piece] * size, queries, out_cot, *pieces)
    near, far = parts[: size // 2], parts[size // 2 :]
    mine = [a + core_swap(b) for a, b in zip(near, far)]
    applied = [mine[0]] + [chip_shift(mine[by], -by) for by in range(1, size // 2)]

    inners, arrived = [], []
    common = [own, shifted, last, sum_a, sum_b]
    for section in range(groups - 1):
        source = groups - 1 - section
        active = (position == source).astype(jnp.int32).reshape(1)

        def body(*refs, count=section):
            section_body(count, False, *refs)

        payload, partial = kernel_call(
            body,
            "section",
            [f32(3 * span + 8, width), f32(8, width)],
            *common,
            earlier,
            *halved,
            kept,
            *inners,
            *arrived,
            *applied,
            flag=active,
        )
        got = to_block(payload, source, source - 1)
        inner = got[3 * span :]
        for by in range(1, size // 2):
            inner = inner + to_block(partial, source, source - 1, 2 * by)
        arrived = arrived + [got]
        inners = inners + [inner, core_swap(inner)]

    def terms(*refs):
        terms_body(groups - 1, *refs)

    def body(*refs):
        section_body(groups - 1, True, *refs)

    (cot,) = kernel_call(terms, "terms", [state], *common, *inners, *arrived)
    cot_pieces = gather_list(cot)
    always = jnp.ones((1,), jnp.int32)
    pair, second = kernel_call(
        body,
        "final",
        [f32(width, 128), f32(span, width)],
        *common,
        earlier,
        *halved,
        kept,
        *inners,
        *arrived,
        *applied,
        flag=always,
    )
    turned = lax.all_to_all(pair, "tok", 0, 0, tiled=True)
    d_keys, d_values, d_rates, d_rows = kernel_call(
        token_body,
        "token",
        [f32(depth, width), f32(depth, width), f32(1, depth), f32(3, rows, width)],
        keys,
        values,
        rates_row,
        turned,
        second,
        *pieces,
        *cot_pieces,
    )
    return (d_queries, d_keys, d_values, d_rates.reshape(depth), d_rows[None])


def solution(mesh):
    return jax.shard_map(
        per_device,
        mesh=mesh,
        in_specs=(
            P(("block", "tok"), None),
            P(("block", "tok"), None),
            P(("block", "tok"), None),
            P(("block", "tok")),
            P("block", None, "tok", None),
            P(("block", "tok"), None),
            P(None, "tok", None),
        ),
        out_specs=(
            P(("block", "tok"), None),
            P(("block", "tok"), None),
            P(("block", "tok"), None),
            P(("block", "tok")),
            P("block", None, "tok", None),
        ),
        check_vma=False,
    )
```

```python
import jax
import jax.numpy as jnp
from jax import lax
from jax.experimental import pallas as pl
from jax.experimental.pallas import tpu as pltpu
from jax.sharding import PartitionSpec as P

EPS = 1e-06
HIGH = lax.Precision.HIGHEST


def mm(left, right):
    return lax.dot_general(left, right, (((1,), (0,)), ((), ())), precision=HIGH, preferred_element_type=jnp.float32)


def mm_nt(left, right):
    return lax.dot_general(left, right, (((1,), (1,)), ((), ())), precision=HIGH, preferred_element_type=jnp.float32)


def mm_tn(left, right):
    return lax.dot_general(left, right, (((0,), (0,)), ((), ())), precision=HIGH, preferred_element_type=jnp.float32)


def silu_parts(first):
    sig = 1.0 / (1.0 + jnp.exp(-first))
    slope = sig * (1.0 - sig)
    value = first * sig
    d_one = sig + first * slope
    d_two = slope * (2.0 + first * (1.0 - 2.0 * sig))
    return value, d_one, d_two


def direct(size):
    return size % 2 == 0 and size <= 16


def chip_shift(array, by):
    size = lax.axis_size("tok")
    return lax.ppermute(array, "tok", [(j, (j + 2 * by) % size) for j in range(size)])


def core_swap(array):
    size = lax.axis_size("tok")
    return lax.ppermute(array, "tok", [(j, j ^ 1) for j in range(size)])


def gather_pieces(array):
    size = lax.axis_size("tok")
    if not direct(size):
        return lax.all_gather(array, "tok")
    mine = jnp.stack([array] + [chip_shift(array, by) for by in range(1, size // 2)])
    return jnp.concatenate([mine, core_swap(mine)])


def spread_sum(pieces):
    size = lax.axis_size("tok")
    if not direct(size):
        return lax.psum_scatter(pieces, "tok")
    half = size // 2
    mine = pieces[:half] + core_swap(pieces[half:])
    total = mine[0]
    for by in range(1, half):
        total = total + chip_shift(mine[by], -by)
    return total


def sum_all(array):
    size = lax.axis_size("tok")
    if not direct(size):
        return jnp.sum(lax.all_gather(array, "tok"), axis=0)
    array = array + core_swap(array)
    total = array
    for by in range(1, size // 2):
        total = total + chip_shift(array, by)
    return total


def rows_to_hidden(rows):
    size = lax.axis_size("tok")
    count, depth, width = rows.shape
    parts = rows.reshape(count, depth, size, width // size).transpose(2, 0, 3, 1)
    parts = lax.all_to_all(parts, "tok", 0, 0)
    return parts.transpose(1, 2, 0, 3).reshape(count, width // size, depth * size)


def hidden_to_rows(slices):
    size = lax.axis_size("tok")
    count, depth, width = slices.shape
    parts = slices.reshape(count, depth, size, width // size).transpose(2, 0, 1, 3)
    parts = lax.all_to_all(parts, "tok", 0, 0)
    return parts.transpose(1, 3, 0, 2).reshape(count, width // size, depth * size)


def to_block(array, source, target, by=0):
    size = lax.axis_size("tok")
    pairs = [(source * size + j, target * size + (j + by) % size) for j in range(size)]
    return lax.ppermute(array, ("block", "tok"), pairs)


def up_one(array):
    groups = lax.axis_size("block")
    return lax.ppermute(array, "block", [(i, i + 1) for i in range(groups - 1)])


def slice_forward(weights, keys, scaled):
    first, gate = mm_nt(weights[0], keys), mm_nt(weights[1], keys)
    value, d_one, d_two = silu_parts(first)
    d_mixed = mm_nt(weights[2], scaled)
    mixed = value * gate
    d_gate = d_mixed * value
    d_first = d_mixed * gate * d_one
    grads = jnp.stack([mm(d_first, keys), mm(d_gate, keys), mm(mixed, scaled)])
    return grads, (gate, value, d_one, d_two, d_mixed)


def slice_adjoint(cot, kept, keys, scaled):
    gate, value, d_one, d_two, d_mixed = kept
    t_first, t_gate, p_mixed = mm_nt(cot[0], keys), mm_nt(cot[1], keys), mm_nt(cot[2], scaled)
    t_mixed = d_one * t_first * gate + value * t_gate
    c_gate = p_mixed * value + d_mixed * d_one * t_first
    c_first = p_mixed * gate * d_one + d_mixed * (d_two * t_first * gate + d_one * t_gate)
    return jnp.stack([mm(c_first, keys), mm(c_gate, keys), mm(t_mixed, scaled)])


def query_adjoint(weights, queries, out_cot):
    first, gate = mm_nt(queries, weights[0]), mm_nt(queries, weights[1])
    value, d_one, _ = silu_parts(first)
    d_mixed = mm_nt(out_cot, weights[2])
    d_gate = d_mixed * value
    d_first = d_mixed * gate * d_one
    d_queries = mm(d_first, weights[0]) + mm(d_gate, weights[1])
    d_weights = jnp.stack([mm_tn(d_first, queries), mm_tn(d_gate, queries), mm_tn(value * gate, out_cot)])
    return d_queries, d_weights


def token_adjoint(weights, cot, keys, scaled):
    first, gate = mm_nt(keys, weights[0]), mm_nt(keys, weights[1])
    value, d_one, d_two = silu_parts(first)
    d_mixed = mm_nt(scaled, weights[2])
    mixed = value * gate
    d_gate = d_mixed * value
    d_first = d_mixed * gate * d_one
    t_first, t_gate, p_mixed = mm_nt(keys, cot[0]), mm_nt(keys, cot[1]), mm_nt(scaled, cot[2])
    t_mixed = d_one * t_first * gate + value * t_gate
    c_gate = p_mixed * value + d_mixed * d_one * t_first
    c_first = p_mixed * gate * d_one + d_mixed * (d_two * t_first * gate + d_one * t_gate)
    d_keys = mm(c_first, weights[0]) + mm(c_gate, weights[1]) + mm(d_first, cot[0]) + mm(d_gate, cot[1])
    t_out = mm(t_mixed, weights[2]) + mm(mixed, cot[2])
    return d_keys, t_out


def over_hidden(array):
    return jnp.sum(array[:2], axis=1)


def per_device_general(queries, keys, values, rates, states, out_cot, final_cot):
    groups, size = lax.axis_size("block"), lax.axis_size("tok")
    position = lax.axis_index("block")
    own_rows = states[0]
    scaled = -rates[:, None] * values
    both = gather_pieces(jnp.stack([keys, scaled]))
    width = keys.shape[1]
    all_keys = both[:, 0].reshape(-1, width)
    all_scaled = both[:, 1].reshape(-1, width)
    split = rows_to_hidden(jnp.concatenate([own_rows[:2], final_cot[:2]]))
    own = jnp.concatenate([split[:2], own_rows[2:]])
    last = jnp.concatenate([split[2:], final_cot[2:]])
    grads, kept = slice_forward(own, all_keys, all_scaled)
    shifted = own - grads
    earlier = up_one(shifted[:2])
    sums = sum_all(jnp.concatenate([over_hidden(own * own), over_hidden(shifted * shifted), over_hidden(last * shifted)]))
    row_norm = [jnp.sqrt(sums[0:2, None, :] + EPS), jnp.sqrt(jnp.sum(own[2:] ** 2, axis=-1, keepdims=True) + EPS)]
    new_norm = [jnp.sqrt(sums[2:4, None, :] + EPS), jnp.sqrt(jnp.sum(shifted[2:] ** 2, axis=-1, keepdims=True) + EPS)]

    pieces = gather_pieces(own)
    whole = pieces.transpose(1, 0, 2, 3).reshape(3, -1, width)
    d_queries, d_weights = query_adjoint(whole, queries, out_cot)
    apply_state = spread_sum(d_weights.reshape(3, size, -1, width).transpose(1, 0, 2, 3))

    is_last = position == groups - 1
    incoming = jnp.where(is_last, last, 0.0)
    inner = jnp.where(is_last, sums[4:6], 0.0)
    for section in range(groups):
        inners = [inner[:, None, :], jnp.sum(incoming[2:] * shifted[2:], axis=-1, keepdims=True)]
        cots, straights = [], []
        for part, dot, old, new in zip((slice(0, 2), slice(2, 3)), inners, row_norm, new_norm):
            d_shifted = old / new * incoming[part] - old * dot / (new * new * new) * shifted[part]
            cots.append(-d_shifted)
            straights.append(d_shifted + dot / new * own[part] / old)
        cot = jnp.concatenate(cots)
        straight = jnp.concatenate(straights)
        rows_now = slice_adjoint(cot, kept, all_keys, all_scaled) + apply_state + straight
        if section + 1 < groups:
            source = groups - 1 - section
            partial = over_hidden(rows_now[:2] * earlier)
            incoming = incoming + to_block(rows_now, source, source - 1)
            if direct(size):
                for by in range(size):
                    inner = inner + to_block(partial, source, source - 1, by)
            else:
                inner = inner + to_block(sum_all(partial), source, source - 1)
    cot_pieces = gather_pieces(cot)
    whole_cot = cot_pieces.transpose(1, 0, 2, 3).reshape(3, -1, width)
    d_keys, t_out = token_adjoint(whole, whole_cot, keys, scaled)
    d_values = -rates[:, None] * t_out
    d_rates = -jnp.sum(values * t_out, axis=-1)
    d_rows = jnp.concatenate([hidden_to_rows(rows_now[:2]), rows_now[2:]])
    return (d_queries, d_keys, d_values, d_rates, d_rows[None])


def halves(array):
    upper = array.astype(jnp.bfloat16)
    return upper, (array - upper.astype(jnp.float32)).astype(jnp.bfloat16)


def product(left, right, contract):
    def one(a, b):
        return lax.dot_general(a, b, (((1,), (contract,)), ((), ())), preferred_element_type=jnp.float32)

    return one(left[0], right[0]) + (one(left[0], right[1]) + one(left[1], right[0]))


def nn(left, right):
    return product(left, right, 0)


def nt(left, right):
    return product(left, right, 1)


def kernel_call(body, name, outs, *operands, flags=None, keep=False, scratch=()):
    specs = [pl.BlockSpec(memory_space=pltpu.VMEM) for _ in operands]
    if flags is not None:
        specs = [pl.BlockSpec(memory_space=pltpu.SMEM)] + specs
        operands = (flags,) + operands
    return pl.pallas_call(
        body,
        name=name,
        in_specs=specs,
        out_specs=[pl.BlockSpec(memory_space=pltpu.VMEM) for _ in outs],
        out_shape=[(pltpu.VMEM if keep else jax.ShapeDtypeStruct)(shape, dtype) for shape, dtype in outs],
        scratch_shapes=list(scratch),
        compiler_params=pltpu.CompilerParams(vmem_limit_bytes=32 * 1024 * 1024),
    )(*operands)


def f32(*shape):
    return shape, jnp.float32


def bf16(*shape):
    return shape, jnp.bfloat16


def column(row, width):
    block = jnp.broadcast_to(row, (128, row.shape[1])).T
    return jnp.concatenate([block] * (width // 128), axis=1)


CHIPS = 4
LOW, HIGH_CHIP = 1, 2
CHUNK = 256


def rows_at(start, count):
    return pl.ds(pl.multiple_of(start, count), count)


def pack_body(flags, values, rates, rows, final, scaled, *packs):
    scaled[...] = -column(rates[...], values.shape[1]) * values[...]
    depth = rows.shape[1]
    sides = []
    for side in range(2):
        parts = []
        for core in range(2):
            lanes = []
            for source in (rows, final):
                for m in range(2):
                    for i in range(2):
                        start = (4 * side + 2 * i + core) * depth
                        lanes.append(source[m, :, start : start + depth])
            parts.append(jnp.concatenate(lanes, axis=1))
        sides.append(jnp.concatenate(parts))
    for by, pack in enumerate(packs):
        low = lax.rem(flags[0] - by + CHIPS, CHIPS) == LOW
        pack[: 2 * depth] = jnp.where(low, sides[0], sides[1])
        pack[2 * depth : 3 * depth] = rows[2]
        pack[3 * depth :] = final[2]


def unpack_body(flags, *refs):
    packs, mates = refs[:CHIPS], refs[CHIPS : 2 * CHIPS]
    own, last, table = refs[2 * CHIPS :]
    depth = packs[0].shape[0] // 4
    span = own.shape[1]
    chip, core = flags[0], flags[1]

    @pl.when(flags[2] == 0)
    def _():
        own[...] = jnp.zeros(own.shape, jnp.float32)
        last[...] = jnp.zeros(last.shape, jnp.float32)

    @pl.when(flags[2] != 0)
    def _():
        for by in range(CHIPS):
            source = lax.rem(chip + by, CHIPS)
            mine = rows_at(core * depth, depth)
            table[rows_at((2 * source + core) * depth, depth), :] = packs[by][mine, :]
            table[rows_at((2 * source + 1 - core) * depth, depth), :] = mates[by][mine, :]
        turned = table[...].T
        keep = jnp.where(flags[3] != 0, 1.0, 0.0)
        own[0], own[1] = turned[:span], turned[span : 2 * span]
        last[0], last[1] = turned[2 * span : 3 * span] * keep, turned[3 * span :] * keep
        low = chip == LOW
        for place, out, scale in ((2 * depth, own, 1.0), (3 * depth, last, keep)):
            cut = slice(place, place + depth)
            out[2, :depth] = jnp.where(low, packs[3][cut, :], packs[0][cut, :]) * scale
            out[2, depth:] = jnp.where(low, packs[0][cut, :], packs[1][cut, :]) * scale


def forward_body(flags, own, last, *refs):
    pieces = (len(refs) - 7) // 2
    keys, scaled = refs[:pieces], refs[pieces : 2 * pieces]
    key_high, key_low, scaled_high, scaled_low, kept, shifted, sums = refs[2 * pieces :]
    depth = keys[0].shape[0]
    span = own.shape[1]

    @pl.when(flags[2] == 0)
    def _():
        shifted[...] = jnp.zeros(shifted.shape, jnp.float32)
        sums[...] = jnp.zeros(sums.shape, jnp.float32)

    @pl.when(flags[2] != 0)
    def _():
        for index in range(pieces):
            cut = slice(index * depth, (index + 1) * depth)
            key_high[cut, :], key_low[cut, :] = halves(keys[index][...])
            scaled_high[cut, :], scaled_low[cut, :] = halves(scaled[index][...])
        pair = halves(jnp.concatenate([own[0], own[1]]))
        second = halves(own[2])
        grad_pair, grad_second = 0.0, 0.0
        for start in range(0, pieces * depth, CHUNK):
            cut = slice(start, start + CHUNK)
            key_cut = key_high[cut, :], key_low[cut, :]
            scaled_cut = scaled_high[cut, :], scaled_low[cut, :]
            both = nt(pair, key_cut)
            d_mixed = nt(second, scaled_cut)
            first, gate = both[:span], both[span:]
            value, d_one, d_two = silu_parts(first)
            for place, array in enumerate((gate, value, d_one, d_two, d_mixed)):
                kept[place, :, cut] = array
            d_pair = jnp.concatenate([d_mixed * gate * d_one, d_mixed * value])
            grad_pair += nn(halves(d_pair), key_cut)
            grad_second += nn(halves(value * gate), scaled_cut)
        moved = own[0] - grad_pair[:span], own[1] - grad_pair[span:], own[2] - grad_second
        rows = []
        for left, right in ((own, own), (moved, moved), (last, moved)):
            rows += [jnp.sum(left[m] * right[m], axis=0, keepdims=True) for m in range(2)]
        sums[...] = jnp.concatenate(rows + [jnp.zeros((2, own.shape[2]), jnp.float32)])
        for m in range(3):
            shifted[m] = moved[m]


def apply_body(flags, own, *refs):
    pieces = (len(refs) - 1) // 2
    queries, cots, applied = refs[:pieces], refs[pieces : 2 * pieces], refs[-1]
    span = own.shape[1]

    @pl.when(flags[2] != 0)
    def _():
        pair = halves(jnp.concatenate([own[0], own[1]]))
        second = halves(own[2])
        out_pair, out_second = 0.0, 0.0
        for index in range(0, pieces, 2):
            query = halves(jnp.concatenate([queries[index][...], queries[index + 1][...]]))
            cot = halves(jnp.concatenate([cots[index][...], cots[index + 1][...]]))
            both = nt(pair, query)
            d_mixed = nt(second, cot)
            first, gate = both[:span], both[span:]
            value, d_one, _ = silu_parts(first)
            out_pair += nn(halves(jnp.concatenate([d_mixed * gate * d_one, d_mixed * value])), query)
            out_second += nn(halves(value * gate), cot)
        applied[: 2 * span] = out_pair
        applied[2 * span :] = out_second


def state_terms(own, shifted, last, sums, inners, arrived):
    span = own.shape[1]
    total = sums[0][...] + sums[1][...] + (sums[2][...] + sums[3][...])
    inner = total[4:6]
    for array in inners:
        inner = inner + array[0:2]
    for array in arrived:
        inner = inner + array[3 * span : 3 * span + 2]
    cots, straights = [], []
    for m in range(3):
        incoming = last[m]
        for array in arrived:
            incoming = incoming + array[m * span : (m + 1) * span, :]
        if m < 2:
            dot, old, new = inner[m : m + 1], jnp.sqrt(total[m : m + 1] + EPS), jnp.sqrt(total[m + 2 : m + 3] + EPS)
        else:
            dot = jnp.sum(incoming * shifted[m], axis=-1, keepdims=True)
            old = jnp.sqrt(jnp.sum(own[m] * own[m], axis=-1, keepdims=True) + EPS)
            new = jnp.sqrt(jnp.sum(shifted[m] * shifted[m], axis=-1, keepdims=True) + EPS)
        d_shifted = old / new * incoming - old * dot / (new * new * new) * shifted[m]
        cots.append(-d_shifted)
        straights.append(d_shifted + dot / new * own[m] / old)
    return cots, straights


def terms_body(count, flags, *refs):
    own, shifted, last = refs[:3]
    sums, inners, arrived, cot = refs[3:7], refs[7 : 7 + 3 * count], refs[7 + 3 * count : -1], refs[-1]

    @pl.when(flags[2] == 0)
    def _():
        cot[...] = jnp.zeros(cot.shape, jnp.float32)

    @pl.when(flags[2] != 0)
    def _():
        cots, _ = state_terms(own, shifted, last, sums, inners, arrived)
        for m in range(3):
            cot[m] = cots[m]


def section_rows(count, refs):
    own, shifted, last = refs[:3]
    sums, inners, arrived = refs[3:7], refs[7 : 7 + 3 * count], refs[7 + 3 * count : 7 + 4 * count]
    key_high, key_low, scaled_high, scaled_low, kept, applied = refs[7 + 4 * count : 13 + 4 * count]
    span = own.shape[1]
    cots, straights = state_terms(own, shifted, last, sums, inners, arrived)
    pair = halves(jnp.concatenate(cots[:2]))
    second = halves(cots[2])
    d_pair, d_second = 0.0, 0.0
    for start in range(0, key_high.shape[0], CHUNK):
        cut = slice(start, start + CHUNK)
        key_cut = key_high[cut, :], key_low[cut, :]
        scaled_cut = scaled_high[cut, :], scaled_low[cut, :]
        gate, value, d_one, d_two, d_mixed = [kept[place, :, cut] for place in range(5)]
        both = nt(pair, key_cut)
        p_mixed = nt(second, scaled_cut)
        t_first, t_gate = both[:span], both[span:]
        lift = d_one * t_first
        t_mixed = lift * gate + value * t_gate
        c_gate = p_mixed * value + d_mixed * lift
        c_first = p_mixed * gate * d_one + d_mixed * (d_two * t_first * gate + d_one * t_gate)
        d_pair += nn(halves(jnp.concatenate([c_first, c_gate])), key_cut)
        d_second += nn(halves(t_mixed), scaled_cut)
    rows = [d_pair[:span] + straights[0], d_pair[span:] + straights[1], d_second + straights[2]]
    return [row + applied[m * span : (m + 1) * span, :] for m, row in enumerate(rows)]


def section_body(count, flags, *refs):
    earlier, payload, partial = refs[-3:]

    @pl.when(flags[4] != 0)
    def _():
        rows = section_rows(count, refs)
        sums = [jnp.sum(rows[m] * earlier[m], axis=0, keepdims=True) for m in range(2)]
        tail = jnp.concatenate(sums + [jnp.zeros((6, rows[0].shape[1]), jnp.float32)])
        partial[...] = tail
        payload[...] = jnp.concatenate(rows + [tail])


def final_body(count, flags, *refs):
    outs, table = refs[-5:-1], refs[-1]
    depth = outs[0].shape[0] // 2
    chip = flags[0]

    @pl.when(flags[2] == 0)
    def _():
        for out in outs:
            out[...] = jnp.zeros(out.shape, jnp.float32)

    @pl.when(flags[2] != 0)
    def _():
        rows = section_rows(count, refs)
        table[...] = jnp.concatenate(rows[:2]).T
        low = chip == LOW
        upper, lower = rows[2][:depth], rows[2][depth:]
        places = (chip, jnp.where(low, 0, CHIPS - 1), LOW + HIGH_CHIP - chip, jnp.where(low, CHIPS - 1, 0))
        picks = (jnp.where(low, lower, upper), jnp.where(low, upper, lower), upper, upper)
        for out, place, pick in zip(outs, places, picks):
            out[:, :128] = table[rows_at(place * 2 * depth, 2 * depth), :]
            out[:depth, 128:] = pick[:, :128]
            out[depth:, 128:] = pick[:, 128:]


def joined(refs):
    return [refs[0][...] + refs[1][...], refs[2][...] + refs[3][...], refs[4][...] + refs[5][...], refs[6][...] + refs[7][...]]


def load_halves(pieces, part):
    return halves(jnp.concatenate([piece[part] for piece in pieces]))


def query_body(queries, out_cot, *refs):
    pieces, d_queries = joined(refs[:8]), refs[8]
    one, three, two = [load_halves(pieces, part) for part in range(3)]
    query, cot = halves(queries[...]), halves(out_cot[...])
    first, gate = nt(query, one), nt(query, three)
    value, d_one, _ = silu_parts(first)
    d_mixed = nt(cot, two)
    d_gate = d_mixed * value
    d_first = d_mixed * gate * d_one
    d_queries[...] = nn(halves(d_first), one) + nn(halves(d_gate), three)


def token_body(flags, keys, values, rates, *refs):
    weights, cots, ends = joined(refs[:8]), joined(refs[8:16]), joined(refs[16:24])
    d_keys, d_values, d_rates, d_rows = refs[24:]
    width = keys.shape[1]
    one, three, two = [load_halves(weights, part) for part in range(3)]
    c_one, c_three, c_two = [load_halves(cots, part) for part in range(3)]
    rate = column(rates[...], width)
    key, scaled = halves(keys[...]), halves(-rate * values[...])
    first, gate = nt(key, one), nt(key, three)
    value, d_one, d_two = silu_parts(first)
    d_mixed = nt(scaled, two)
    t_first, t_gate, p_mixed = nt(key, c_one), nt(key, c_three), nt(scaled, c_two)
    mixed = value * gate
    d_gate = d_mixed * value
    d_first = d_mixed * gate * d_one
    lift = d_one * t_first
    t_mixed = lift * gate + value * t_gate
    c_gate = p_mixed * value + d_mixed * lift
    c_first = p_mixed * gate * d_one + d_mixed * (d_two * t_first * gate + d_one * t_gate)
    d_keys[...] = nn(halves(c_first), one) + nn(halves(c_gate), three) + nn(halves(d_first), c_one) + nn(halves(d_gate), c_three)
    t_out = nn(halves(t_mixed), two) + nn(halves(mixed), c_two)
    d_values[...] = -rate * t_out
    d_rates[...] = -jnp.sum((values[...] * t_out).T, axis=0, keepdims=True)
    depth = d_rows.shape[1]
    low_side, upper_core = flags[0] <= LOW, flags[1] == 0
    sides = []
    for near, far in ((ends[0], ends[1]), (ends[2], ends[3])):
        pair = jnp.where(low_side, near, far), jnp.where(low_side, far, near)
        sides.append([jnp.where(upper_core, piece[:depth], piece[depth:]) for piece in pair])
    by_core = [[jnp.where(upper_core, a, b) for a, b in zip(*sides)], [jnp.where(upper_core, b, a) for a, b in zip(*sides)]]
    for m in range(2):
        parts = []
        for side in range(2):
            for i in range(2):
                for core in range(2):
                    start = (2 * m + i) * depth
                    parts.append(by_core[core][side][:, start : start + depth])
        d_rows[m] = jnp.concatenate(parts, axis=1)
    d_rows[2] = jnp.concatenate([ends[0][:depth, 128:], ends[0][depth:, 128:]], axis=1)


def chip_permute(array, pairs):
    return lax.ppermute(array, "tok", [(2 * a + core, 2 * b + core) for a, b in pairs for core in range(2)])


def to_chain(arrays):
    pieces = [arrays[0]] + [
        chip_permute(arrays[by], [((chip + by) % CHIPS, chip) for chip in (LOW, HIGH_CHIP)]) for by in range(1, CHIPS)
    ]
    return pieces + [core_swap(piece) for piece in pieces]


SWAP = ((LOW, HIGH_CHIP), (HIGH_CHIP, LOW))
OUTWARD = ((LOW, 0), (HIGH_CHIP, CHIPS - 1))
ACROSS = ((LOW, CHIPS - 1), (HIGH_CHIP, 0))


def spread_list(arrays):
    pieces = [arrays[0]] + [chip_permute(array, pairs) for array, pairs in zip(arrays[1:], (OUTWARD, SWAP, ACROSS))]
    return pieces + [core_swap(piece) for piece in pieces]


def chain_to_block(array, source, target, pairs):
    size = lax.axis_size("tok")
    moves = [(source * size + 2 * a + core, target * size + 2 * b + core) for a, b in pairs for core in range(2)]
    return lax.ppermute(array, ("block", "tok"), moves)


def per_device(queries, keys, values, rates, states, out_cot, final_cot):
    groups, size = lax.axis_size("block"), lax.axis_size("tok")
    depth, width = keys.shape
    own_rows = states[0]
    rows = own_rows.shape[1]
    if not (size == 2 * CHIPS and 4 * rows == 128 and depth == 128 and width == 8 * rows):
        return per_device_general(queries, keys, values, rates, states, out_cot, final_cot)
    span, tokens = 2 * rows, depth * size
    position, place = lax.axis_index("block"), lax.axis_index("tok")
    chip = place // 2
    in_chain = (chip == LOW) | (chip == HIGH_CHIP)

    def flags_of(active):
        return jnp.stack([chip, place % 2, in_chain, position == groups - 1, active & in_chain]).astype(jnp.int32)

    flags = flags_of(in_chain)
    rates_row = rates.reshape(1, depth)
    state, square = f32(3, span, width), f32(depth, width)
    scaled, *packs = kernel_call(pack_body, "pack", [square] * 5, values, rates_row, own_rows, final_cot, flags=flags)
    key_pieces = to_chain([keys] * CHIPS)
    arrived_packs = to_chain(packs)
    scaled_pieces = to_chain([scaled] * CHIPS)
    query_pieces = to_chain([queries] * CHIPS)
    cot_pieces = to_chain([out_cot] * CHIPS)
    table = pltpu.VMEM((width, 4 * span), jnp.float32)
    own, last = kernel_call(unpack_body, "unpack", [state, state], *arrived_packs, flags=flags, scratch=[table])
    half = bf16(tokens, width)
    *halved, kept, shifted, sums = kernel_call(
        forward_body,
        "forward",
        [half, half, half, half, f32(5, span, tokens), state, f32(8, width)],
        own,
        last,
        *key_pieces,
        *scaled_pieces,
        flags=flags,
        keep=True,
    )
    across = chip_permute(sums, SWAP)
    all_sums = [sums, core_swap(sums), across, core_swap(across)]
    earlier = up_one(shifted)
    weights = spread_list([own] * CHIPS)
    (applied,) = kernel_call(
        apply_body, "apply", [f32(3 * span, width)], own, *query_pieces, *cot_pieces, flags=flags, keep=True
    )

    inners, arrived = [], []
    common = [own, shifted, last, *all_sums]
    for section in range(groups - 1):
        source = groups - 1 - section

        def body(*refs, count=section):
            section_body(count, *refs)

        payload, partial = kernel_call(
            body,
            "section",
            [f32(3 * span + 8, width), f32(8, width)],
            *common,
            *inners,
            *arrived,
            *halved,
            kept,
            applied,
            earlier,
            flags=flags_of(position == source),
            keep=True,
        )
        straight = ((LOW, LOW), (HIGH_CHIP, HIGH_CHIP))
        got = chain_to_block(payload, source, source - 1, straight)
        cross = chain_to_block(partial, source, source - 1, SWAP)
        mate = chain_to_block(core_swap(partial), source, source - 1, straight)
        arrived = arrived + [got]
        inners = inners + [cross, core_swap(cross), mate]

    def terms(*refs):
        terms_body(groups - 1, *refs)

    def body(*refs):
        final_body(groups - 1, *refs)

    (cot,) = kernel_call(terms, "terms", [state], *common, *inners, *arrived, flags=flags)
    cots = spread_list([cot] * CHIPS)
    (d_queries,) = kernel_call(query_body, "query", [square], queries, out_cot, *weights)
    ends = kernel_call(
        body,
        "final",
        [f32(2 * rows, width)] * CHIPS,
        *common,
        *inners,
        *arrived,
        *halved,
        kept,
        applied,
        flags=flags,
        scratch=[pltpu.VMEM((width, 128), jnp.float32)],
    )
    end_pieces = spread_list(ends)
    d_keys, d_values, d_rates, d_rows = kernel_call(
        token_body,
        "token",
        [square, square, f32(1, depth), f32(3, rows, width)],
        keys,
        values,
        rates_row,
        *weights,
        *cots,
        *end_pieces,
        flags=flags,
    )
    return (d_queries, d_keys, d_values, d_rates.reshape(depth), d_rows[None])


def solution(mesh):
    return jax.shard_map(
        per_device,
        mesh=mesh,
        in_specs=(
            P(("block", "tok"), None),
            P(("block", "tok"), None),
            P(("block", "tok"), None),
            P(("block", "tok")),
            P("block", None, "tok", None),
            P(("block", "tok"), None),
            P(None, "tok", None),
        ),
        out_specs=(
            P(("block", "tok"), None),
            P(("block", "tok"), None),
            P(("block", "tok"), None),
            P(("block", "tok")),
            P("block", None, "tok", None),
        ),
        check_vma=False,
    )
```

```python
import functools

import jax
import jax.numpy as jnp
from jax import lax
from jax.experimental import pallas as pl
from jax.experimental.pallas import tpu as pltpu
from jax.sharding import PartitionSpec as P

EPS = 1e-06
HIGH = lax.Precision.HIGHEST


def mm(left, right):
    return lax.dot_general(left, right, (((1,), (0,)), ((), ())), precision=HIGH, preferred_element_type=jnp.float32)


def mm_nt(left, right):
    return lax.dot_general(left, right, (((1,), (1,)), ((), ())), precision=HIGH, preferred_element_type=jnp.float32)


def mm_tn(left, right):
    return lax.dot_general(left, right, (((0,), (0,)), ((), ())), precision=HIGH, preferred_element_type=jnp.float32)


def silu_parts(first):
    sig = 1.0 / (1.0 + jnp.exp(-first))
    slope = sig * (1.0 - sig)
    value = first * sig
    d_one = sig + first * slope
    d_two = slope * (2.0 + first * (1.0 - 2.0 * sig))
    return value, d_one, d_two


def direct(size):
    return size % 2 == 0 and size <= 16


def chip_shift(array, by):
    size = lax.axis_size("tok")
    return lax.ppermute(array, "tok", [(j, (j + 2 * by) % size) for j in range(size)])


def core_swap(array):
    size = lax.axis_size("tok")
    return lax.ppermute(array, "tok", [(j, j ^ 1) for j in range(size)])


def gather_pieces(array):
    size = lax.axis_size("tok")
    if not direct(size):
        return lax.all_gather(array, "tok")
    mine = jnp.stack([array] + [chip_shift(array, by) for by in range(1, size // 2)])
    return jnp.concatenate([mine, core_swap(mine)])


def spread_sum(pieces):
    size = lax.axis_size("tok")
    if not direct(size):
        return lax.psum_scatter(pieces, "tok")
    half = size // 2
    mine = pieces[:half] + core_swap(pieces[half:])
    total = mine[0]
    for by in range(1, half):
        total = total + chip_shift(mine[by], -by)
    return total


def sum_all(array):
    size = lax.axis_size("tok")
    if not direct(size):
        return jnp.sum(lax.all_gather(array, "tok"), axis=0)
    array = array + core_swap(array)
    total = array
    for by in range(1, size // 2):
        total = total + chip_shift(array, by)
    return total


def rows_to_hidden(rows):
    size = lax.axis_size("tok")
    count, depth, width = rows.shape
    parts = rows.reshape(count, depth, size, width // size).transpose(2, 0, 3, 1)
    parts = lax.all_to_all(parts, "tok", 0, 0)
    return parts.transpose(1, 2, 0, 3).reshape(count, width // size, depth * size)


def hidden_to_rows(slices):
    size = lax.axis_size("tok")
    count, depth, width = slices.shape
    parts = slices.reshape(count, depth, size, width // size).transpose(2, 0, 1, 3)
    parts = lax.all_to_all(parts, "tok", 0, 0)
    return parts.transpose(1, 3, 0, 2).reshape(count, width // size, depth * size)


def to_block(array, source, target, by=0):
    size = lax.axis_size("tok")
    pairs = [(source * size + j, target * size + (j + by) % size) for j in range(size)]
    return lax.ppermute(array, ("block", "tok"), pairs)


def up_one(array):
    groups = lax.axis_size("block")
    return lax.ppermute(array, "block", [(i, i + 1) for i in range(groups - 1)])


def slice_forward(weights, keys, scaled):
    first, gate = mm_nt(weights[0], keys), mm_nt(weights[1], keys)
    value, d_one, d_two = silu_parts(first)
    d_mixed = mm_nt(weights[2], scaled)
    mixed = value * gate
    d_gate = d_mixed * value
    d_first = d_mixed * gate * d_one
    grads = jnp.stack([mm(d_first, keys), mm(d_gate, keys), mm(mixed, scaled)])
    return grads, (gate, value, d_one, d_two, d_mixed)


def slice_adjoint(cot, kept, keys, scaled):
    gate, value, d_one, d_two, d_mixed = kept
    t_first, t_gate, p_mixed = mm_nt(cot[0], keys), mm_nt(cot[1], keys), mm_nt(cot[2], scaled)
    t_mixed = d_one * t_first * gate + value * t_gate
    c_gate = p_mixed * value + d_mixed * d_one * t_first
    c_first = p_mixed * gate * d_one + d_mixed * (d_two * t_first * gate + d_one * t_gate)
    return jnp.stack([mm(c_first, keys), mm(c_gate, keys), mm(t_mixed, scaled)])


def query_adjoint(weights, queries, out_cot):
    first, gate = mm_nt(queries, weights[0]), mm_nt(queries, weights[1])
    value, d_one, _ = silu_parts(first)
    d_mixed = mm_nt(out_cot, weights[2])
    d_gate = d_mixed * value
    d_first = d_mixed * gate * d_one
    d_queries = mm(d_first, weights[0]) + mm(d_gate, weights[1])
    d_weights = jnp.stack([mm_tn(d_first, queries), mm_tn(d_gate, queries), mm_tn(value * gate, out_cot)])
    return d_queries, d_weights


def token_adjoint(weights, cot, keys, scaled):
    first, gate = mm_nt(keys, weights[0]), mm_nt(keys, weights[1])
    value, d_one, d_two = silu_parts(first)
    d_mixed = mm_nt(scaled, weights[2])
    mixed = value * gate
    d_gate = d_mixed * value
    d_first = d_mixed * gate * d_one
    t_first, t_gate, p_mixed = mm_nt(keys, cot[0]), mm_nt(keys, cot[1]), mm_nt(scaled, cot[2])
    t_mixed = d_one * t_first * gate + value * t_gate
    c_gate = p_mixed * value + d_mixed * d_one * t_first
    c_first = p_mixed * gate * d_one + d_mixed * (d_two * t_first * gate + d_one * t_gate)
    d_keys = mm(c_first, weights[0]) + mm(c_gate, weights[1]) + mm(d_first, cot[0]) + mm(d_gate, cot[1])
    t_out = mm(t_mixed, weights[2]) + mm(mixed, cot[2])
    return d_keys, t_out


def over_hidden(array):
    return jnp.sum(array[:2], axis=1)


def per_device_general(queries, keys, values, rates, states, out_cot, final_cot):
    groups, size = lax.axis_size("block"), lax.axis_size("tok")
    position = lax.axis_index("block")
    own_rows = states[0]
    scaled = -rates[:, None] * values
    both = gather_pieces(jnp.stack([keys, scaled]))
    width = keys.shape[1]
    all_keys = both[:, 0].reshape(-1, width)
    all_scaled = both[:, 1].reshape(-1, width)
    split = rows_to_hidden(jnp.concatenate([own_rows[:2], final_cot[:2]]))
    own = jnp.concatenate([split[:2], own_rows[2:]])
    last = jnp.concatenate([split[2:], final_cot[2:]])
    grads, kept = slice_forward(own, all_keys, all_scaled)
    shifted = own - grads
    earlier = up_one(shifted[:2])
    sums = sum_all(jnp.concatenate([over_hidden(own * own), over_hidden(shifted * shifted), over_hidden(last * shifted)]))
    row_norm = [jnp.sqrt(sums[0:2, None, :] + EPS), jnp.sqrt(jnp.sum(own[2:] ** 2, axis=-1, keepdims=True) + EPS)]
    new_norm = [jnp.sqrt(sums[2:4, None, :] + EPS), jnp.sqrt(jnp.sum(shifted[2:] ** 2, axis=-1, keepdims=True) + EPS)]

    pieces = gather_pieces(own)
    whole = pieces.transpose(1, 0, 2, 3).reshape(3, -1, width)
    d_queries, d_weights = query_adjoint(whole, queries, out_cot)
    apply_state = spread_sum(d_weights.reshape(3, size, -1, width).transpose(1, 0, 2, 3))

    is_last = position == groups - 1
    incoming = jnp.where(is_last, last, 0.0)
    inner = jnp.where(is_last, sums[4:6], 0.0)
    for section in range(groups):
        inners = [inner[:, None, :], jnp.sum(incoming[2:] * shifted[2:], axis=-1, keepdims=True)]
        cots, straights = [], []
        for part, dot, old, new in zip((slice(0, 2), slice(2, 3)), inners, row_norm, new_norm):
            d_shifted = old / new * incoming[part] - old * dot / (new * new * new) * shifted[part]
            cots.append(-d_shifted)
            straights.append(d_shifted + dot / new * own[part] / old)
        cot = jnp.concatenate(cots)
        straight = jnp.concatenate(straights)
        rows_now = slice_adjoint(cot, kept, all_keys, all_scaled) + apply_state + straight
        if section + 1 < groups:
            source = groups - 1 - section
            partial = over_hidden(rows_now[:2] * earlier)
            incoming = incoming + to_block(rows_now, source, source - 1)
            if direct(size):
                for by in range(size):
                    inner = inner + to_block(partial, source, source - 1, by)
            else:
                inner = inner + to_block(sum_all(partial), source, source - 1)
    cot_pieces = gather_pieces(cot)
    whole_cot = cot_pieces.transpose(1, 0, 2, 3).reshape(3, -1, width)
    d_keys, t_out = token_adjoint(whole, whole_cot, keys, scaled)
    d_values = -rates[:, None] * t_out
    d_rates = -jnp.sum(values * t_out, axis=-1)
    d_rows = jnp.concatenate([hidden_to_rows(rows_now[:2]), rows_now[2:]])
    return (d_queries, d_keys, d_values, d_rates, d_rows[None])


def halves(array):
    upper = array.astype(jnp.bfloat16)
    return upper, (array - upper.astype(jnp.float32)).astype(jnp.bfloat16)


def product(left, right, contract):
    def one(a, b):
        return lax.dot_general(a, b, (((1,), (contract,)), ((), ())), preferred_element_type=jnp.float32)

    return one(left[0], right[0]) + (one(left[0], right[1]) + one(left[1], right[0]))


def nn(left, right):
    return product(left, right, 0)


def nt(left, right):
    return product(left, right, 1)


def kernel_call(body, name, outs, *operands, flags=None, scratch=(), raw=False):
    space = pltpu.MemorySpace.HBM if raw else pltpu.VMEM
    specs = [pl.BlockSpec(memory_space=space) for _ in operands]
    if flags is not None:
        specs = [pl.BlockSpec(memory_space=pltpu.SMEM)] + specs
        operands = (flags,) + operands
    return pl.pallas_call(
        body,
        name=name,
        in_specs=specs,
        out_specs=[pl.BlockSpec(memory_space=pltpu.VMEM) for _ in outs],
        out_shape=[pltpu.VMEM(shape, dtype) for shape, dtype in outs],
        scratch_shapes=list(scratch),
        compiler_params=pltpu.CompilerParams(vmem_limit_bytes=24 * 1024 * 1024),
    )(*operands)


def f32(*shape):
    return shape, jnp.float32


def bf16(*shape):
    return shape, jnp.bfloat16


def column(row, width):
    block = jnp.broadcast_to(row, (128, row.shape[1])).T
    return jnp.concatenate([block] * (width // 128), axis=1)


CHIPS = 4
LOW, HIGH_CHIP = 1, 2
CHUNK = 256


def rows_at(start, count):
    return pl.ds(pl.multiple_of(start, count), count)


def pack_body(flags, *refs):
    count = 7
    sources, outs = refs[:count], refs[count : count + CHIPS + 1]
    buffers, sems = refs[count + CHIPS + 1 : -1], refs[-1]
    copies = [pltpu.make_async_copy(a, b, sems.at[i]) for i, (a, b) in enumerate(zip(sources, buffers))]
    for copy in copies:
        copy.start()
    for copy in copies:
        copy.wait()
    keys, values, rates, rows, final, queries, cot = buffers
    packs, ahead = outs[:CHIPS], outs[CHIPS]
    tokens = keys.shape[0]
    depth = rows.shape[1]
    scaled = -column(rates[...], values.shape[1]) * values[...]
    sides = []
    for side in range(2):
        parts = []
        for core in range(2):
            lanes = []
            for source in (rows, final):
                for m in range(2):
                    for i in range(2):
                        start = (4 * side + 2 * i + core) * depth
                        lanes.append(source[m, :, start : start + depth])
            parts.append(jnp.concatenate(lanes, axis=1))
        sides.append(jnp.concatenate(parts))
    for by, pack in enumerate(packs):
        pack[:tokens] = keys[...]
        pack[tokens : 2 * tokens] = scaled
        low = jnp.bitwise_xor(flags[0], by) == LOW
        pack[2 * tokens : 2 * tokens + 2 * depth] = jnp.where(low, sides[0], sides[1])
        if by < 2:
            pack[2 * tokens + 2 * depth : 2 * tokens + 3 * depth] = rows[2]
            pack[2 * tokens + 3 * depth :] = final[2]
    ahead[:tokens] = queries[...]
    ahead[tokens:] = cot[...]


def unpack(flags, packs, mates, own, last, table):
    depth = own.shape[1] // 2
    base = packs[0].shape[0] - 4 * depth
    span = own.shape[1]
    chip, core = flags[0], flags[1]
    for by in range(CHIPS):
        source = jnp.bitwise_xor(chip, by)
        mine = rows_at(base + core * depth, depth)
        table[rows_at((2 * source + core) * depth, depth), :] = packs[by][mine, :]
        table[rows_at((2 * source + 1 - core) * depth, depth), :] = mates[by][mine, :]
    turned = table[...].T
    keep = jnp.where(flags[3] != 0, 1.0, 0.0)
    own[0], own[1] = turned[:span], turned[span : 2 * span]
    last[0], last[1] = turned[2 * span : 3 * span] * keep, turned[3 * span :] * keep
    low = chip == LOW
    for place, out, scale in ((2 * depth, own, 1.0), (3 * depth, last, keep)):
        cut = slice(base + place, base + place + depth)
        out[2, :depth] = jnp.where(low, packs[1][cut, :], packs[0][cut, :]) * scale
        out[2, depth:] = jnp.where(low, packs[0][cut, :], packs[1][cut, :]) * scale


def forward_body(flags, *refs):
    packs, mates = refs[:CHIPS], refs[CHIPS : 2 * CHIPS]
    own, last, key_high, key_low, scaled_high, scaled_low, kept, shifted, sums, table = refs[2 * CHIPS :]
    pieces = packs + mates
    depth = key_high.shape[0] // len(pieces)
    span = own.shape[1]

    @pl.when(flags[2] == 0)
    def _():
        for out in (own, shifted, sums):
            out[...] = jnp.zeros(out.shape, jnp.float32)

    @pl.when(flags[2] != 0)
    def _():
        unpack(flags, packs, mates, own, last, table)
        for index, piece in enumerate(pieces):
            cut = slice(index * depth, (index + 1) * depth)
            key_high[cut, :], key_low[cut, :] = halves(piece[:depth, :])
            scaled_high[cut, :], scaled_low[cut, :] = halves(piece[depth : 2 * depth, :])
        pair = halves(jnp.concatenate([own[0], own[1]]))
        second = halves(own[2])
        grad_pair, grad_second = 0.0, 0.0
        for start in range(0, key_high.shape[0], CHUNK):
            cut = slice(start, start + CHUNK)
            key_cut = key_high[cut, :], key_low[cut, :]
            scaled_cut = scaled_high[cut, :], scaled_low[cut, :]
            both = nt(pair, key_cut)
            d_mixed = nt(second, scaled_cut)
            first, gate = both[:span], both[span:]
            value, d_one, d_two = silu_parts(first)
            for place, array in enumerate((gate, value, d_one, d_two, d_mixed)):
                kept[place, :, cut] = array
            d_pair = jnp.concatenate([d_mixed * gate * d_one, d_mixed * value])
            grad_pair += nn(halves(d_pair), key_cut)
            grad_second += nn(halves(value * gate), scaled_cut)
        moved = own[0] - grad_pair[:span], own[1] - grad_pair[span:], own[2] - grad_second
        rows = []
        for left, right in ((own, own), (moved, moved), (last, moved)):
            rows += [jnp.sum(left[m] * right[m], axis=0, keepdims=True) for m in range(2)]
        sums[...] = jnp.concatenate(rows + [jnp.zeros((2, own.shape[2]), jnp.float32)])
        for m in range(3):
            shifted[m] = moved[m]


def apply_body(flags, own, *refs):
    pieces, applied = refs[:-1], refs[-1]
    span = own.shape[1]
    depth = pieces[0].shape[0] // 2

    @pl.when(flags[2] != 0)
    def _():
        pair = halves(jnp.concatenate([own[0], own[1]]))
        second = halves(own[2])
        out_pair, out_second = 0.0, 0.0
        for index in range(0, len(pieces), 2):
            one, two = pieces[index], pieces[index + 1]
            query = halves(jnp.concatenate([one[:depth, :], two[:depth, :]]))
            cot = halves(jnp.concatenate([one[depth:, :], two[depth:, :]]))
            both = nt(pair, query)
            d_mixed = nt(second, cot)
            first, gate = both[:span], both[span:]
            value, d_one, _ = silu_parts(first)
            out_pair += nn(halves(jnp.concatenate([d_mixed * gate * d_one, d_mixed * value])), query)
            out_second += nn(halves(value * gate), cot)
        applied[: 2 * span] = out_pair
        applied[2 * span :] = out_second


def state_terms(own, shifted, last, sums, inners, arrived):
    span = own.shape[1]
    total = sums[0][...] + sums[1][...] + (sums[2][...] + sums[3][...])
    inner = total[4:6]
    for array in inners:
        inner = inner + array[0:2]
    cots, straights = [], []
    for m in range(3):
        incoming = last[m]
        for array in arrived:
            incoming = incoming + array[m]
        if m < 2:
            dot, old, new = inner[m : m + 1], jnp.sqrt(total[m : m + 1] + EPS), jnp.sqrt(total[m + 2 : m + 3] + EPS)
        else:
            dot = jnp.sum(incoming * shifted[m], axis=-1, keepdims=True)
            old = jnp.sqrt(jnp.sum(own[m] * own[m], axis=-1, keepdims=True) + EPS)
            new = jnp.sqrt(jnp.sum(shifted[m] * shifted[m], axis=-1, keepdims=True) + EPS)
        d_shifted = old / new * incoming - old * dot / (new * new * new) * shifted[m]
        cots.append(-d_shifted)
        straights.append(d_shifted + dot / new * own[m] / old)
    return cots, straights


def section_rows(count, refs):
    own, shifted, last = refs[:3]
    sums, inners, arrived = refs[3:7], refs[7 : 7 + 4 * count], refs[7 + 4 * count : 7 + 5 * count]
    key_high, key_low, scaled_high, scaled_low, kept, applied = refs[7 + 5 * count : 13 + 5 * count]
    span = own.shape[1]
    cots, straights = state_terms(own, shifted, last, sums, inners, arrived)
    pair = halves(jnp.concatenate(cots[:2]))
    second = halves(cots[2])
    d_pair, d_second = 0.0, 0.0
    for start in range(0, key_high.shape[0], CHUNK):
        cut = slice(start, start + CHUNK)
        key_cut = key_high[cut, :], key_low[cut, :]
        scaled_cut = scaled_high[cut, :], scaled_low[cut, :]
        gate, value, d_one, d_two, d_mixed = [kept[place, :, cut] for place in range(5)]
        both = nt(pair, key_cut)
        p_mixed = nt(second, scaled_cut)
        t_first, t_gate = both[:span], both[span:]
        lift = d_one * t_first
        t_mixed = lift * gate + value * t_gate
        c_gate = p_mixed * value + d_mixed * lift
        c_first = p_mixed * gate * d_one + d_mixed * (d_two * t_first * gate + d_one * t_gate)
        d_pair += nn(halves(jnp.concatenate([c_first, c_gate])), key_cut)
        d_second += nn(halves(t_mixed), scaled_cut)
    rows = [d_pair[:span] + straights[0], d_pair[span:] + straights[1], d_second + straights[2]]
    return cots, [row + applied[m * span : (m + 1) * span, :] for m, row in enumerate(rows)]


def section_body(count, source, flags, *refs):
    earlier, payload, partial = refs[-3:]

    @pl.when((flags[4] != source) | (flags[2] == 0))
    def _():
        payload[...] = jnp.zeros(payload.shape, jnp.float32)
        partial[...] = jnp.zeros(partial.shape, jnp.float32)

    @pl.when((flags[4] == source) & (flags[2] != 0))
    def _():
        _, rows = section_rows(count, refs)
        sums = [jnp.sum(rows[m] * earlier[m], axis=0, keepdims=True) for m in range(2)]
        partial[...] = jnp.concatenate(sums + [jnp.zeros((6, rows[0].shape[1]), jnp.float32)])
        for m in range(3):
            payload[m] = rows[m]


def final_body(count, flags, *refs):
    outs, table = refs[-5:-1], refs[-1]
    span = refs[0].shape[1]
    depth = span // 2
    chip = flags[0]

    @pl.when(flags[2] == 0)
    def _():
        for out in outs:
            out[...] = jnp.zeros(out.shape, jnp.float32)

    @pl.when(flags[2] != 0)
    def _():
        cots, rows = section_rows(count, refs)
        for out in outs:
            for m in range(3):
                out[m * span : (m + 1) * span, :] = cots[m]
        table[...] = jnp.concatenate(rows[:2]).T
        low = chip == LOW
        upper, lower = rows[2][:depth], rows[2][depth:]
        picks = jnp.where(low, lower, upper), jnp.where(low, upper, lower), upper, upper
        for by, (out, pick) in enumerate(zip(outs, picks)):
            start = rows_at(jnp.bitwise_xor(chip, by) * 2 * depth, 2 * depth)
            out[3 * span :, :128] = table[start, :]
            out[3 * span : 3 * span + depth, 128:] = pick[:, :128]
            out[3 * span + depth :, 128:] = pick[:, 128:]


def joined(refs):
    return [[refs[i], refs[i + 1]] for i in range(0, 8, 2)]


def taken(pair, cut):
    return pair[0][cut, :] + pair[1][cut, :]


def load_halves(pieces, part, span):
    return halves(jnp.concatenate([taken(pair, slice(part * span, (part + 1) * span)) for pair in pieces]))


def query_body(queries, out_cot, *refs):
    pieces, d_queries = joined(refs[:8]), refs[8]
    span = queries.shape[1] // len(pieces)
    one, three, two = [load_halves(pieces, part, span) for part in range(3)]
    query, cot = halves(queries[...]), halves(out_cot[...])
    first, gate = nt(query, one), nt(query, three)
    value, d_one, _ = silu_parts(first)
    d_mixed = nt(cot, two)
    d_gate = d_mixed * value
    d_first = d_mixed * gate * d_one
    d_queries[...] = nn(halves(d_first), one) + nn(halves(d_gate), three)


def token_body(flags, keys, values, rates, *refs):
    weights, cots = joined(refs[:8]), joined(refs[8:16])
    d_keys, d_values, d_rates, d_rows = refs[16:]
    width = keys.shape[1]
    span = width // len(weights)
    one, three, two = [load_halves(weights, part, span) for part in range(3)]
    c_one, c_three, c_two = [load_halves(cots, part, span) for part in range(3)]
    ends = [taken(pair, slice(3 * span, None)) for pair in cots]
    rate = column(rates[...], width)
    key, scaled = halves(keys[...]), halves(-rate * values[...])
    first, gate = nt(key, one), nt(key, three)
    value, d_one, d_two = silu_parts(first)
    d_mixed = nt(scaled, two)
    t_first, t_gate, p_mixed = nt(key, c_one), nt(key, c_three), nt(scaled, c_two)
    mixed = value * gate
    d_gate = d_mixed * value
    d_first = d_mixed * gate * d_one
    lift = d_one * t_first
    t_mixed = lift * gate + value * t_gate
    c_gate = p_mixed * value + d_mixed * lift
    c_first = p_mixed * gate * d_one + d_mixed * (d_two * t_first * gate + d_one * t_gate)
    d_keys[...] = nn(halves(c_first), one) + nn(halves(c_gate), three) + nn(halves(d_first), c_one) + nn(halves(d_gate), c_three)
    t_out = nn(halves(t_mixed), two) + nn(halves(mixed), c_two)
    d_values[...] = -rate * t_out
    d_rates[...] = -jnp.sum((values[...] * t_out).T, axis=0, keepdims=True)
    depth = d_rows.shape[1]
    low_side, upper_core = flags[0] <= LOW, flags[1] == 0
    sides = []
    for near, far in ((ends[0], ends[1]), (ends[2], ends[3])):
        pair = jnp.where(low_side, near, far), jnp.where(low_side, far, near)
        sides.append([jnp.where(upper_core, piece[:depth], piece[depth:]) for piece in pair])
    by_core = [[jnp.where(upper_core, a, b) for a, b in zip(*sides)], [jnp.where(upper_core, b, a) for a, b in zip(*sides)]]
    for m in range(2):
        parts = []
        for side in range(2):
            for i in range(2):
                for core in range(2):
                    start = (2 * m + i) * depth
                    parts.append(by_core[core][side][:, start : start + depth])
        d_rows[m] = jnp.concatenate(parts, axis=1)
    d_rows[2] = jnp.concatenate([ends[0][:depth, 128:], ends[0][depth:, 128:]], axis=1)


def by_xor(array, by, chips=range(CHIPS)):
    return lax.ppermute(array, "tok", [(2 * a + core, 2 * (a ^ by) + core) for a in chips for core in range(2)])


def both_cores(pieces):
    return pieces + [core_swap(piece) for piece in pieces]


def to_chain(arrays):
    near = by_xor(arrays[1], 1)
    across = by_xor(arrays[3], 3, (LOW, HIGH_CHIP))
    far = by_xor(arrays[2], 2, (0, CHIPS - 1))
    return both_cores([arrays[0], near, far, across])


def from_chain(arrays):
    near = by_xor(arrays[1], 1)
    far = by_xor(arrays[2], 2, (LOW, HIGH_CHIP))
    across = by_xor(arrays[3], 3, (LOW, HIGH_CHIP))
    return both_cores([arrays[0], near, across, far])


def to_earlier(array, by):
    groups, size = lax.axis_size("block"), lax.axis_size("tok")
    moves = [
        (block * size + 2 * chip + core, ((block - 1) % groups) * size + 2 * (chip ^ by) + core)
        for block in range(groups)
        for chip in range(CHIPS)
        for core in range(2)
    ]
    return lax.ppermute(array, ("block", "tok"), moves)


def to_later(array):
    groups = lax.axis_size("block")
    return lax.ppermute(array, "block", [(i, (i + 1) % groups) for i in range(groups)])


def per_device(queries, keys, values, rates, states, out_cot, final_cot):
    groups, size = lax.axis_size("block"), lax.axis_size("tok")
    depth, width = keys.shape
    own_rows = states[0]
    rows = own_rows.shape[1]
    if not (size == 2 * CHIPS and 4 * rows == 128 and depth == 128 and width == 8 * rows):
        return per_device_general(queries, keys, values, rates, states, out_cot, final_cot)
    span, tokens = 2 * rows, depth * size
    position, place = lax.axis_index("block"), lax.axis_index("tok")
    chip = place // 2
    in_chain = (chip == LOW) | (chip == HIGH_CHIP)
    flags = jnp.stack([chip, place % 2, in_chain, position == groups - 1, position]).astype(jnp.int32)
    rates_row = rates.reshape(1, depth)
    state, square, wide = f32(3, span, width), f32(depth, width), f32(3 * span, width)
    sources = (keys, values, rates_row, own_rows, final_cot, queries, out_cot)
    longer, shorter = f32(2 * depth + 4 * rows, width), f32(2 * depth + 2 * rows, width)
    *packs, ahead = kernel_call(
        pack_body,
        "pack",
        [longer, longer, shorter, shorter, f32(2 * depth, width)],
        *sources,
        flags=flags,
        scratch=[pltpu.VMEM(array.shape, array.dtype) for array in sources] + [pltpu.SemaphoreType.DMA((len(sources),))],
        raw=True,
    )
    pieces = to_chain(packs)
    half = bf16(tokens, width)
    own, last, *halved, kept, shifted, sums = kernel_call(
        forward_body,
        "forward",
        [state, state, half, half, half, half, f32(5, span, tokens), state, f32(8, width)],
        *pieces,
        flags=flags,
        scratch=[pltpu.VMEM((width, 4 * span), jnp.float32)],
    )
    across = by_xor(sums, 3)
    all_sums = [sums, core_swap(sums), across, core_swap(across)]
    earlier = to_later(shifted)
    weights = from_chain([own.reshape(3 * span, width)] * CHIPS)
    (applied,) = kernel_call(apply_body, "apply", [wide], own, *to_chain([ahead] * CHIPS), flags=flags)

    inners, arrived = [], []
    common = [own, shifted, last, *all_sums]
    kept_arrays = [*halved, kept, applied]
    for section in range(groups - 1):
        source = groups - 1 - section
        body = functools.partial(section_body, min(section, 1), source)
        payload, partial = kernel_call(
            body,
            "section",
            [state, f32(8, width)],
            *common,
            *inners[-4:],
            *arrived[-1:],
            *kept_arrays,
            earlier,
            flags=flags,
        )
        straight, cross = to_earlier(partial, 0), to_earlier(partial, 3)
        arrived.append(to_earlier(payload, 0))
        inners += [straight, cross, core_swap(straight), core_swap(cross)]
    ends = kernel_call(
        functools.partial(final_body, groups - 1),
        "final",
        [f32(4 * span, width)] * CHIPS,
        *common,
        *inners,
        *arrived,
        *kept_arrays,
        flags=flags,
        scratch=[pltpu.VMEM((width, 128), jnp.float32)],
    )
    cots = from_chain(ends)
    (d_queries,) = kernel_call(query_body, "query", [square], queries, out_cot, *weights)
    d_keys, d_values, d_rates, d_rows = kernel_call(
        token_body,
        "token",
        [square, square, f32(1, depth), f32(3, rows, width)],
        keys,
        values,
        rates_row,
        *weights,
        *cots,
        flags=flags,
    )
    return (d_queries, d_keys, d_values, d_rates.reshape(depth), d_rows[None])


def solution(mesh):
    return jax.shard_map(
        per_device,
        mesh=mesh,
        in_specs=(
            P(("block", "tok"), None),
            P(("block", "tok"), None),
            P(("block", "tok"), None),
            P(("block", "tok")),
            P("block", None, "tok", None),
            P(("block", "tok"), None),
            P(None, "tok", None),
        ),
        out_specs=(
            P(("block", "tok"), None),
            P(("block", "tok"), None),
            P(("block", "tok"), None),
            P(("block", "tok")),
            P("block", None, "tok", None),
        ),
        check_vma=False,
    )
```

```python
import functools

import jax
import jax.numpy as jnp
from jax import lax
from jax.experimental import pallas as pl
from jax.experimental.pallas import tpu as pltpu
from jax.sharding import PartitionSpec as P


EPS = 1e-06
HIGH = lax.Precision.HIGHEST


def mm(left, right):
    return lax.dot_general(left, right, (((1,), (0,)), ((), ())), precision=HIGH, preferred_element_type=jnp.float32)


def mm_nt(left, right):
    return lax.dot_general(left, right, (((1,), (1,)), ((), ())), precision=HIGH, preferred_element_type=jnp.float32)


def mm_tn(left, right):
    return lax.dot_general(left, right, (((0,), (0,)), ((), ())), precision=HIGH, preferred_element_type=jnp.float32)


def silu_parts(first):
    sig = 1.0 / (1.0 + jnp.exp(-first))
    slope = sig * (1.0 - sig)
    value = first * sig
    d_one = sig + first * slope
    d_two = slope * (2.0 + first * (1.0 - 2.0 * sig))
    return value, d_one, d_two


def direct(size):
    return size % 2 == 0 and size <= 16


def chip_shift(array, by):
    size = lax.axis_size("tok")
    return lax.ppermute(array, "tok", [(j, (j + 2 * by) % size) for j in range(size)])


def core_swap(array):
    size = lax.axis_size("tok")
    return lax.ppermute(array, "tok", [(j, j ^ 1) for j in range(size)])


def gather_pieces(array):
    size = lax.axis_size("tok")
    if not direct(size):
        return lax.all_gather(array, "tok")
    mine = jnp.stack([array] + [chip_shift(array, by) for by in range(1, size // 2)])
    return jnp.concatenate([mine, core_swap(mine)])


def spread_sum(pieces):
    size = lax.axis_size("tok")
    if not direct(size):
        return lax.psum_scatter(pieces, "tok")
    half = size // 2
    mine = pieces[:half] + core_swap(pieces[half:])
    total = mine[0]
    for by in range(1, half):
        total = total + chip_shift(mine[by], -by)
    return total


def sum_all(array):
    size = lax.axis_size("tok")
    if not direct(size):
        return jnp.sum(lax.all_gather(array, "tok"), axis=0)
    array = array + core_swap(array)
    total = array
    for by in range(1, size // 2):
        total = total + chip_shift(array, by)
    return total


def rows_to_hidden(rows):
    size = lax.axis_size("tok")
    count, depth, width = rows.shape
    parts = rows.reshape(count, depth, size, width // size).transpose(2, 0, 3, 1)
    parts = lax.all_to_all(parts, "tok", 0, 0)
    return parts.transpose(1, 2, 0, 3).reshape(count, width // size, depth * size)


def hidden_to_rows(slices):
    size = lax.axis_size("tok")
    count, depth, width = slices.shape
    parts = slices.reshape(count, depth, size, width // size).transpose(2, 0, 1, 3)
    parts = lax.all_to_all(parts, "tok", 0, 0)
    return parts.transpose(1, 3, 0, 2).reshape(count, width // size, depth * size)


def to_block(array, source, target, by=0):
    size = lax.axis_size("tok")
    pairs = [(source * size + j, target * size + (j + by) % size) for j in range(size)]
    return lax.ppermute(array, ("block", "tok"), pairs)


def up_one(array):
    groups = lax.axis_size("block")
    return lax.ppermute(array, "block", [(i, i + 1) for i in range(groups - 1)])


def slice_forward(weights, keys, scaled):
    first, gate = mm_nt(weights[0], keys), mm_nt(weights[1], keys)
    value, d_one, d_two = silu_parts(first)
    d_mixed = mm_nt(weights[2], scaled)
    mixed = value * gate
    d_gate = d_mixed * value
    d_first = d_mixed * gate * d_one
    grads = jnp.stack([mm(d_first, keys), mm(d_gate, keys), mm(mixed, scaled)])
    return grads, (gate, value, d_one, d_two, d_mixed)


def slice_adjoint(cot, kept, keys, scaled):
    gate, value, d_one, d_two, d_mixed = kept
    t_first, t_gate, p_mixed = mm_nt(cot[0], keys), mm_nt(cot[1], keys), mm_nt(cot[2], scaled)
    t_mixed = d_one * t_first * gate + value * t_gate
    c_gate = p_mixed * value + d_mixed * d_one * t_first
    c_first = p_mixed * gate * d_one + d_mixed * (d_two * t_first * gate + d_one * t_gate)
    return jnp.stack([mm(c_first, keys), mm(c_gate, keys), mm(t_mixed, scaled)])


def query_adjoint(weights, queries, out_cot):
    first, gate = mm_nt(queries, weights[0]), mm_nt(queries, weights[1])
    value, d_one, _ = silu_parts(first)
    d_mixed = mm_nt(out_cot, weights[2])
    d_gate = d_mixed * value
    d_first = d_mixed * gate * d_one
    d_queries = mm(d_first, weights[0]) + mm(d_gate, weights[1])
    d_weights = jnp.stack([mm_tn(d_first, queries), mm_tn(d_gate, queries), mm_tn(value * gate, out_cot)])
    return d_queries, d_weights


def token_adjoint(weights, cot, keys, scaled):
    first, gate = mm_nt(keys, weights[0]), mm_nt(keys, weights[1])
    value, d_one, d_two = silu_parts(first)
    d_mixed = mm_nt(scaled, weights[2])
    mixed = value * gate
    d_gate = d_mixed * value
    d_first = d_mixed * gate * d_one
    t_first, t_gate, p_mixed = mm_nt(keys, cot[0]), mm_nt(keys, cot[1]), mm_nt(scaled, cot[2])
    t_mixed = d_one * t_first * gate + value * t_gate
    c_gate = p_mixed * value + d_mixed * d_one * t_first
    c_first = p_mixed * gate * d_one + d_mixed * (d_two * t_first * gate + d_one * t_gate)
    d_keys = mm(c_first, weights[0]) + mm(c_gate, weights[1]) + mm(d_first, cot[0]) + mm(d_gate, cot[1])
    t_out = mm(t_mixed, weights[2]) + mm(mixed, cot[2])
    return d_keys, t_out


def over_hidden(array):
    return jnp.sum(array[:2], axis=1)


def per_device_general(queries, keys, values, rates, states, out_cot, final_cot):
    groups, size = lax.axis_size("block"), lax.axis_size("tok")
    position = lax.axis_index("block")
    own_rows = states[0]
    scaled = -rates[:, None] * values
    both = gather_pieces(jnp.stack([keys, scaled]))
    width = keys.shape[1]
    all_keys = both[:, 0].reshape(-1, width)
    all_scaled = both[:, 1].reshape(-1, width)
    split = rows_to_hidden(jnp.concatenate([own_rows[:2], final_cot[:2]]))
    own = jnp.concatenate([split[:2], own_rows[2:]])
    last = jnp.concatenate([split[2:], final_cot[2:]])
    grads, kept = slice_forward(own, all_keys, all_scaled)
    shifted = own - grads
    earlier = up_one(shifted[:2])
    sums = sum_all(jnp.concatenate([over_hidden(own * own), over_hidden(shifted * shifted), over_hidden(last * shifted)]))
    row_norm = [jnp.sqrt(sums[0:2, None, :] + EPS), jnp.sqrt(jnp.sum(own[2:] ** 2, axis=-1, keepdims=True) + EPS)]
    new_norm = [jnp.sqrt(sums[2:4, None, :] + EPS), jnp.sqrt(jnp.sum(shifted[2:] ** 2, axis=-1, keepdims=True) + EPS)]

    pieces = gather_pieces(own)
    whole = pieces.transpose(1, 0, 2, 3).reshape(3, -1, width)
    d_queries, d_weights = query_adjoint(whole, queries, out_cot)
    apply_state = spread_sum(d_weights.reshape(3, size, -1, width).transpose(1, 0, 2, 3))

    is_last = position == groups - 1
    incoming = jnp.where(is_last, last, 0.0)
    inner = jnp.where(is_last, sums[4:6], 0.0)
    for section in range(groups):
        inners = [inner[:, None, :], jnp.sum(incoming[2:] * shifted[2:], axis=-1, keepdims=True)]
        cots, straights = [], []
        for part, dot, old, new in zip((slice(0, 2), slice(2, 3)), inners, row_norm, new_norm):
            d_shifted = old / new * incoming[part] - old * dot / (new * new * new) * shifted[part]
            cots.append(-d_shifted)
            straights.append(d_shifted + dot / new * own[part] / old)
        cot = jnp.concatenate(cots)
        straight = jnp.concatenate(straights)
        rows_now = slice_adjoint(cot, kept, all_keys, all_scaled) + apply_state + straight
        if section + 1 < groups:
            source = groups - 1 - section
            partial = over_hidden(rows_now[:2] * earlier)
            incoming = incoming + to_block(rows_now, source, source - 1)
            if direct(size):
                for by in range(size):
                    inner = inner + to_block(partial, source, source - 1, by)
            else:
                inner = inner + to_block(sum_all(partial), source, source - 1)
    cot_pieces = gather_pieces(cot)
    whole_cot = cot_pieces.transpose(1, 0, 2, 3).reshape(3, -1, width)
    d_keys, t_out = token_adjoint(whole, whole_cot, keys, scaled)
    d_values = -rates[:, None] * t_out
    d_rates = -jnp.sum(values * t_out, axis=-1)
    d_rows = jnp.concatenate([hidden_to_rows(rows_now[:2]), rows_now[2:]])
    return (d_queries, d_keys, d_values, d_rates, d_rows[None])


def halves(array):
    upper = array.astype(jnp.bfloat16)
    return upper, (array - upper.astype(jnp.float32)).astype(jnp.bfloat16)


def product(left, right, contract):
    def one(a, b):
        return lax.dot_general(a, b, (((1,), (contract,)), ((), ())), preferred_element_type=jnp.float32)

    return one(left[0], right[0]) + (one(left[0], right[1]) + one(left[1], right[0]))


def nn(left, right):
    return product(left, right, 0)


def nt(left, right):
    return product(left, right, 1)


def kernel_call(body, outs, *operands, flags=None, scratch=(), raw=False, spill=False, limit=24 * 1024 * 1024):
    space = pltpu.MemorySpace.HBM if raw else pltpu.VMEM
    specs = [pl.BlockSpec(memory_space=space) for _ in operands]
    if flags is not None:
        specs = [pl.BlockSpec(memory_space=pltpu.SMEM)] + specs
        operands = (flags,) + operands
    return pl.pallas_call(
        body,
        in_specs=specs,
        out_specs=[pl.BlockSpec(memory_space=pltpu.VMEM) for _ in outs],
        out_shape=[(jax.ShapeDtypeStruct if spill else pltpu.VMEM)(shape, dtype) for shape, dtype in outs],
        scratch_shapes=list(scratch),
        compiler_params=pltpu.CompilerParams(vmem_limit_bytes=limit),
    )(*operands)


def f32(*shape):
    return shape, jnp.float32


def bf16(*shape):
    return shape, jnp.bfloat16


def column(row, width):
    block = jnp.broadcast_to(row, (128, row.shape[1])).T
    return jnp.concatenate([block] * (width // 128), axis=1)


CHIPS = 4
LOW, HIGH_CHIP = 1, 2
CHUNK = 256
PACK_LIMIT = 61 * 1024 * 1024


def rows_at(start, count):
    return pl.ds(pl.multiple_of(start, count), count)


def pack_body(flags, *refs):
    count = 7
    sources, outs = refs[:count], refs[count : count + CHIPS + 1]
    buffers, sems = refs[count + CHIPS + 1 : -1], refs[-1]
    copies = [pltpu.make_async_copy(a, b, sems.at[i]) for i, (a, b) in enumerate(zip(sources, buffers))]
    for copy in copies:
        copy.start()
    for copy in copies:
        copy.wait()
    keys, values, rates, rows, final, queries, cot = buffers
    packs, ahead = outs[:CHIPS], outs[CHIPS]
    tokens = keys.shape[0]
    depth = rows.shape[1]
    scaled = -column(rates[...], values.shape[1]) * values[...]
    sides = []
    for side in range(2):
        parts = []
        for core in range(2):
            lanes = []
            for source in (rows, final):
                for m in range(2):
                    for i in range(2):
                        start = (4 * side + 2 * i + core) * depth
                        lanes.append(source[m, :, start : start + depth])
            parts.append(jnp.concatenate(lanes, axis=1))
        sides.append(jnp.concatenate(parts))
    for by, pack in enumerate(packs):
        pack[:tokens] = keys[...]
        pack[tokens : 2 * tokens] = scaled
        low = jnp.bitwise_xor(flags[0], by) == LOW
        pack[2 * tokens : 2 * tokens + 2 * depth] = jnp.where(low, sides[0], sides[1])
        if by < 2:
            pack[2 * tokens + 2 * depth : 2 * tokens + 3 * depth] = rows[2]
            pack[2 * tokens + 3 * depth :] = final[2]
    ahead[:tokens] = queries[...]
    ahead[tokens:] = cot[...]


def unpack(flags, packs, mates, own, last, table):
    depth = own.shape[1] // 2
    base = packs[0].shape[0] - 4 * depth
    span = own.shape[1]
    chip, core = flags[0], flags[1]
    for by in range(CHIPS):
        source = jnp.bitwise_xor(chip, by)
        mine = rows_at(base + core * depth, depth)
        table[rows_at((2 * source + core) * depth, depth), :] = packs[by][mine, :]
        table[rows_at((2 * source + 1 - core) * depth, depth), :] = mates[by][mine, :]
    turned = table[...].T
    keep = jnp.where(flags[3] != 0, 1.0, 0.0)
    own[0], own[1] = turned[:span], turned[span : 2 * span]
    last[0], last[1] = turned[2 * span : 3 * span] * keep, turned[3 * span :] * keep
    low = chip == LOW
    for place, out, scale in ((2 * depth, own, 1.0), (3 * depth, last, keep)):
        cut = slice(base + place, base + place + depth)
        out[2, :depth] = jnp.where(low, packs[1][cut, :], packs[0][cut, :]) * scale
        out[2, depth:] = jnp.where(low, packs[0][cut, :], packs[1][cut, :]) * scale


def forward_body(flags, *refs):
    packs, mates = refs[:CHIPS], refs[CHIPS : 2 * CHIPS]
    own, last, key_high, key_low, scaled_high, scaled_low, kept, shifted, sums, table = refs[2 * CHIPS :]
    pieces = packs + mates
    depth = key_high.shape[0] // len(pieces)
    span = own.shape[1]

    @pl.when(flags[2] == 0)
    def _():
        for out in (own, shifted, sums):
            out[...] = jnp.zeros(out.shape, jnp.float32)

    @pl.when(flags[2] != 0)
    def _():
        unpack(flags, packs, mates, own, last, table)
        for index, piece in enumerate(pieces):
            cut = slice(index * depth, (index + 1) * depth)
            key_high[cut, :], key_low[cut, :] = halves(piece[:depth, :])
            scaled_high[cut, :], scaled_low[cut, :] = halves(piece[depth : 2 * depth, :])
        pair = halves(jnp.concatenate([own[0], own[1]]))
        second = halves(own[2])
        grad_pair, grad_second = 0.0, 0.0
        for start in range(0, key_high.shape[0], CHUNK):
            cut = slice(start, start + CHUNK)
            key_cut = key_high[cut, :], key_low[cut, :]
            scaled_cut = scaled_high[cut, :], scaled_low[cut, :]
            both = nt(pair, key_cut)
            d_mixed = nt(second, scaled_cut)
            first, gate = both[:span], both[span:]
            value, d_one, d_two = silu_parts(first)
            for place, array in enumerate((gate, value, d_one, d_two, d_mixed)):
                kept[place, :, cut] = array
            d_pair = jnp.concatenate([d_mixed * gate * d_one, d_mixed * value])
            grad_pair += nn(halves(d_pair), key_cut)
            grad_second += nn(halves(value * gate), scaled_cut)
        moved = own[0] - grad_pair[:span], own[1] - grad_pair[span:], own[2] - grad_second
        rows = []
        for left, right in ((own, own), (moved, moved), (last, moved)):
            rows += [jnp.sum(left[m] * right[m], axis=0, keepdims=True) for m in range(2)]
        sums[...] = jnp.concatenate(rows + [jnp.zeros((2, own.shape[2]), jnp.float32)])
        for m in range(3):
            shifted[m] = moved[m]


def apply_body(flags, own, *refs):
    pieces, applied = refs[:-1], refs[-1]
    span = own.shape[1]
    depth = pieces[0].shape[0] // 2

    @pl.when(flags[2] != 0)
    def _():
        pair = halves(jnp.concatenate([own[0], own[1]]))
        second = halves(own[2])
        out_pair, out_second = 0.0, 0.0
        for index in range(0, len(pieces), 2):
            one, two = pieces[index], pieces[index + 1]
            query = halves(jnp.concatenate([one[:depth, :], two[:depth, :]]))
            cot = halves(jnp.concatenate([one[depth:, :], two[depth:, :]]))
            both = nt(pair, query)
            d_mixed = nt(second, cot)
            first, gate = both[:span], both[span:]
            value, d_one, _ = silu_parts(first)
            out_pair += nn(halves(jnp.concatenate([d_mixed * gate * d_one, d_mixed * value])), query)
            out_second += nn(halves(value * gate), cot)
        applied[: 2 * span] = out_pair
        applied[2 * span :] = out_second


def state_terms(own, shifted, last, sums, inners, arrived):
    total = sums[0][...] + sums[1][...] + (sums[2][...] + sums[3][...])
    inner = total[4:6]
    for array in inners:
        inner = inner + array[0:2]
    cots, straights = [], []
    for m in range(3):
        incoming = last[m]
        for array in arrived:
            incoming = incoming + array[m]
        if m < 2:
            dot, old, new = inner[m : m + 1], jnp.sqrt(total[m : m + 1] + EPS), jnp.sqrt(total[m + 2 : m + 3] + EPS)
        else:
            dot = jnp.sum(incoming * shifted[m], axis=-1, keepdims=True)
            old = jnp.sqrt(jnp.sum(own[m] * own[m], axis=-1, keepdims=True) + EPS)
            new = jnp.sqrt(jnp.sum(shifted[m] * shifted[m], axis=-1, keepdims=True) + EPS)
        d_shifted = old / new * incoming - old * dot / (new * new * new) * shifted[m]
        cots.append(-d_shifted)
        straights.append(d_shifted + dot / new * own[m] / old)
    return cots, straights


def section_rows(count, refs):
    own, shifted, last = refs[:3]
    sums, inners, arrived = refs[3:7], refs[7 : 7 + 4 * count], refs[7 + 4 * count : 7 + 5 * count]
    key_high, key_low, scaled_high, scaled_low, kept, applied = refs[7 + 5 * count : 13 + 5 * count]
    span = own.shape[1]
    cots, straights = state_terms(own, shifted, last, sums, inners, arrived)
    pair = halves(jnp.concatenate(cots[:2]))
    second = halves(cots[2])
    d_pair, d_second = 0.0, 0.0
    for start in range(0, key_high.shape[0], CHUNK):
        cut = slice(start, start + CHUNK)
        key_cut = key_high[cut, :], key_low[cut, :]
        scaled_cut = scaled_high[cut, :], scaled_low[cut, :]
        gate, value, d_one, d_two, d_mixed = [kept[place, :, cut] for place in range(5)]
        both = nt(pair, key_cut)
        p_mixed = nt(second, scaled_cut)
        t_first, t_gate = both[:span], both[span:]
        lift = d_one * t_first
        t_mixed = lift * gate + value * t_gate
        c_gate = p_mixed * value + d_mixed * lift
        c_first = p_mixed * gate * d_one + d_mixed * (d_two * t_first * gate + d_one * t_gate)
        d_pair += nn(halves(jnp.concatenate([c_first, c_gate])), key_cut)
        d_second += nn(halves(t_mixed), scaled_cut)
    rows = [d_pair[:span] + straights[0], d_pair[span:] + straights[1], d_second + straights[2]]
    return cots, [row + applied[m * span : (m + 1) * span, :] for m, row in enumerate(rows)]


def section_body(count, source, flags, *refs):
    earlier, payload, partial = refs[-3:]

    @pl.when((flags[4] != source) | (flags[2] == 0))
    def _():
        payload[...] = jnp.zeros(payload.shape, jnp.float32)
        partial[...] = jnp.zeros(partial.shape, jnp.float32)

    @pl.when((flags[4] == source) & (flags[2] != 0))
    def _():
        _, rows = section_rows(count, refs)
        sums = [jnp.sum(rows[m] * earlier[m], axis=0, keepdims=True) for m in range(2)]
        partial[...] = jnp.concatenate(sums + [jnp.zeros((6, rows[0].shape[1]), jnp.float32)])
        for m in range(3):
            payload[m] = rows[m]


def final_body(count, flags, *refs):
    outs, table = refs[-5:-1], refs[-1]
    span = refs[0].shape[1]
    depth = span // 2
    chip = flags[0]

    @pl.when(flags[2] == 0)
    def _():
        for out in outs:
            out[...] = jnp.zeros(out.shape, jnp.float32)

    @pl.when(flags[2] != 0)
    def _():
        cots, rows = section_rows(count, refs)
        for out in outs:
            for m in range(3):
                out[m * span : (m + 1) * span, :] = cots[m]
        table[...] = jnp.concatenate(rows[:2]).T
        low = chip == LOW
        upper, lower = rows[2][:depth], rows[2][depth:]
        picks = jnp.where(low, lower, upper), jnp.where(low, upper, lower), upper, upper
        for by, (out, pick) in enumerate(zip(outs, picks)):
            start = rows_at(jnp.bitwise_xor(chip, by) * 2 * depth, 2 * depth)
            out[3 * span :, :128] = table[start, :]
            out[3 * span : 3 * span + depth, 128:] = pick[:, :128]
            out[3 * span + depth :, 128:] = pick[:, 128:]


def joined(refs):
    return [[refs[i], refs[i + 1]] for i in range(0, 8, 2)]


def taken(pair, cut):
    return pair[0][cut, :] + pair[1][cut, :]


def load_halves(pieces, part, span):
    return halves(jnp.concatenate([taken(pair, slice(part * span, (part + 1) * span)) for pair in pieces]))


def query_body(queries, out_cot, *refs):
    pieces, d_queries = joined(refs[:8]), refs[8]
    span = queries.shape[1] // len(pieces)
    one, three, two = [load_halves(pieces, part, span) for part in range(3)]
    query, cot = halves(queries[...]), halves(out_cot[...])
    first, gate = nt(query, one), nt(query, three)
    value, d_one, _ = silu_parts(first)
    d_mixed = nt(cot, two)
    d_gate = d_mixed * value
    d_first = d_mixed * gate * d_one
    d_queries[...] = nn(halves(d_first), one) + nn(halves(d_gate), three)


def token_body(flags, keys, values, rates, *refs):
    weights, cots = joined(refs[:8]), joined(refs[8:16])
    d_keys, d_values, d_rates, d_rows = refs[16:]
    width = keys.shape[1]
    span = width // len(weights)
    one, three, two = [load_halves(weights, part, span) for part in range(3)]
    c_one, c_three, c_two = [load_halves(cots, part, span) for part in range(3)]
    ends = [taken(pair, slice(3 * span, None)) for pair in cots]
    rate = column(rates[...], width)
    key, scaled = halves(keys[...]), halves(-rate * values[...])
    first, gate = nt(key, one), nt(key, three)
    value, d_one, d_two = silu_parts(first)
    d_mixed = nt(scaled, two)
    t_first, t_gate, p_mixed = nt(key, c_one), nt(key, c_three), nt(scaled, c_two)
    mixed = value * gate
    d_gate = d_mixed * value
    d_first = d_mixed * gate * d_one
    lift = d_one * t_first
    t_mixed = lift * gate + value * t_gate
    c_gate = p_mixed * value + d_mixed * lift
    c_first = p_mixed * gate * d_one + d_mixed * (d_two * t_first * gate + d_one * t_gate)
    d_keys[...] = nn(halves(c_first), one) + nn(halves(c_gate), three) + nn(halves(d_first), c_one) + nn(halves(d_gate), c_three)
    t_out = nn(halves(t_mixed), two) + nn(halves(mixed), c_two)
    d_values[...] = -rate * t_out
    d_rates[...] = -jnp.sum((values[...] * t_out).T, axis=0, keepdims=True)
    depth = d_rows.shape[1]
    low_side, upper_core = flags[0] <= LOW, flags[1] == 0
    sides = []
    for near, far in ((ends[0], ends[1]), (ends[2], ends[3])):
        pair = jnp.where(low_side, near, far), jnp.where(low_side, far, near)
        sides.append([jnp.where(upper_core, piece[:depth], piece[depth:]) for piece in pair])
    by_core = [[jnp.where(upper_core, a, b) for a, b in zip(*sides)], [jnp.where(upper_core, b, a) for a, b in zip(*sides)]]
    for m in range(2):
        parts = []
        for side in range(2):
            for i in range(2):
                for core in range(2):
                    start = (2 * m + i) * depth
                    parts.append(by_core[core][side][:, start : start + depth])
        d_rows[m] = jnp.concatenate(parts, axis=1)
    d_rows[2] = jnp.concatenate([ends[0][:depth, 128:], ends[0][depth:, 128:]], axis=1)


def by_xor(array, by, chips=range(CHIPS)):
    return lax.ppermute(array, "tok", [(2 * a + core, 2 * (a ^ by) + core) for a in chips for core in range(2)])


def both_cores(pieces):
    swapped = [core_swap(pieces[0])]
    return pieces + swapped + [core_swap(piece) for piece in pieces[1:]]


def to_chain(arrays):
    near = by_xor(arrays[1], 1)
    across = by_xor(arrays[3], 3, (LOW, HIGH_CHIP))
    far = by_xor(arrays[2], 2, (0, CHIPS - 1))
    return both_cores([arrays[0], near, far, across])


def from_chain(arrays):
    near = by_xor(arrays[1], 1)
    far = by_xor(arrays[2], 2, (LOW, HIGH_CHIP))
    across = by_xor(arrays[3], 3, (LOW, HIGH_CHIP))
    return both_cores([arrays[0], near, across, far])


def to_earlier(array):
    groups = lax.axis_size("block")
    return lax.ppermute(array, "block", [(i, (i - 1) % groups) for i in range(groups)])


def chain_to_block(array, source, target, by):
    size = lax.axis_size("tok")
    places = [(chip, core) for chip in (LOW, HIGH_CHIP) for core in range(2)]
    return lax.ppermute(
        array,
        ("block", "tok"),
        [(source * size + 2 * chip + core, target * size + 2 * (chip ^ by) + core) for chip, core in places],
    )


def to_later(array):
    groups = lax.axis_size("block")
    return lax.ppermute(array, "block", [(i, (i + 1) % groups) for i in range(groups)])


def per_device(queries, keys, values, rates, states, out_cot, final_cot):
    groups, size = lax.axis_size("block"), lax.axis_size("tok")
    depth, width = keys.shape
    own_rows = states[0]
    rows = own_rows.shape[1]
    if not (size == 2 * CHIPS and 4 * rows == 128 and depth == 128 and width == 8 * rows):
        return per_device_general(queries, keys, values, rates, states, out_cot, final_cot)
    span, tokens = 2 * rows, depth * size
    position, place = lax.axis_index("block"), lax.axis_index("tok")
    chip = place // 2
    in_chain = (chip == LOW) | (chip == HIGH_CHIP)
    flags = jnp.stack([chip, place % 2, in_chain, position == groups - 1, position]).astype(jnp.int32)
    rates_row = rates.reshape(1, depth)
    state, square, wide = f32(3, span, width), f32(depth, width), f32(3 * span, width)
    sources = (keys, values, rates_row, own_rows, final_cot, queries, out_cot)
    longer, shorter = f32(2 * depth + 4 * rows, width), f32(2 * depth + 2 * rows, width)
    *packs, ahead = kernel_call(
        pack_body,
        [longer, longer, shorter, shorter, f32(2 * depth, width)],
        *sources,
        flags=flags,
        scratch=[pltpu.VMEM(array.shape, array.dtype) for array in sources] + [pltpu.SemaphoreType.DMA((len(sources),))],
        raw=True,
        limit=PACK_LIMIT,
    )
    pieces = to_chain(packs)
    half = bf16(tokens, width)
    ahead_pieces = to_chain([ahead] * CHIPS)
    own, last, *halved, kept, shifted, sums = kernel_call(
        forward_body,
        [state, state, half, half, half, half, f32(5, span, tokens), state, f32(8, width)],
        *pieces,
        flags=flags,
        scratch=[pltpu.VMEM((width, 4 * span), jnp.float32)],
    )
    across = by_xor(sums, 3)
    all_sums = [sums, core_swap(sums), across, core_swap(across)]
    earlier = to_later(shifted)
    weights = from_chain([own.reshape(3 * span, width)] * CHIPS)
    (applied,) = kernel_call(apply_body, [wide], own, *ahead_pieces, flags=flags)

    inners, arrived = [], []
    common = [own, shifted, last, *all_sums]
    kept_arrays = [*halved, kept, applied]
    for section in range(groups - 1):
        source = groups - 1 - section
        body = functools.partial(section_body, min(section, 1), source)
        payload, partial = kernel_call(
            body, [state, f32(8, width)], *common, *inners[-4:], *arrived[-1:], *kept_arrays, earlier, flags=flags
        )
        arrived.append(to_earlier(payload))
        cross = chain_to_block(partial, source, source - 1, 3)
        straight = chain_to_block(partial, source, source - 1, 0)
        inners += [straight, cross, core_swap(straight), core_swap(cross)]
    ends = kernel_call(
        functools.partial(final_body, groups - 1),
        [f32(4 * span, width)] * CHIPS,
        *common,
        *inners,
        *arrived,
        *kept_arrays,
        flags=flags,
        scratch=[pltpu.VMEM((width, 128), jnp.float32)],
    )
    cots = from_chain(ends)
    (d_queries,) = kernel_call(query_body, [square], queries, out_cot, *weights, spill=True)
    d_keys, d_values, d_rates, d_rows = kernel_call(
        token_body,
        [square, square, f32(1, depth), f32(3, rows, width)],
        keys,
        values,
        rates_row,
        *weights,
        *cots,
        flags=flags,
        spill=True,
    )
    return (d_queries, d_keys, d_values, d_rates.reshape(depth), d_rows[None])


def solution(mesh):
    return jax.shard_map(
        per_device,
        mesh=mesh,
        in_specs=(
            P(("block", "tok"), None),
            P(("block", "tok"), None),
            P(("block", "tok"), None),
            P(("block", "tok")),
            P("block", None, "tok", None),
            P(("block", "tok"), None),
            P(None, "tok", None),
        ),
        out_specs=(
            P(("block", "tok"), None),
            P(("block", "tok"), None),
            P(("block", "tok"), None),
            P(("block", "tok")),
            P("block", None, "tok", None),
        ),
        check_vma=False,
    )
```

```python
import functools

import jax
import jax.numpy as jnp
from jax import lax
from jax.experimental import pallas as pl
from jax.experimental.pallas import tpu as pltpu
from jax.sharding import PartitionSpec as P


EPS = 1e-06
HIGH = lax.Precision.HIGHEST


def mm(left, right):
    return lax.dot_general(left, right, (((1,), (0,)), ((), ())), precision=HIGH, preferred_element_type=jnp.float32)


def mm_nt(left, right):
    return lax.dot_general(left, right, (((1,), (1,)), ((), ())), precision=HIGH, preferred_element_type=jnp.float32)


def mm_tn(left, right):
    return lax.dot_general(left, right, (((0,), (0,)), ((), ())), precision=HIGH, preferred_element_type=jnp.float32)


def silu_parts(first):
    sig = 1.0 / (1.0 + jnp.exp(-first))
    slope = sig * (1.0 - sig)
    value = first * sig
    d_one = sig + first * slope
    d_two = slope * (2.0 + first * (1.0 - 2.0 * sig))
    return value, d_one, d_two


def direct(size):
    return size % 2 == 0 and size <= 16


def chip_shift(array, by):
    size = lax.axis_size("tok")
    return lax.ppermute(array, "tok", [(j, (j + 2 * by) % size) for j in range(size)])


def core_swap(array):
    size = lax.axis_size("tok")
    return lax.ppermute(array, "tok", [(j, j ^ 1) for j in range(size)])


def gather_pieces(array):
    size = lax.axis_size("tok")
    if not direct(size):
        return lax.all_gather(array, "tok")
    mine = jnp.stack([array] + [chip_shift(array, by) for by in range(1, size // 2)])
    return jnp.concatenate([mine, core_swap(mine)])


def spread_sum(pieces):
    size = lax.axis_size("tok")
    if not direct(size):
        return lax.psum_scatter(pieces, "tok")
    half = size // 2
    mine = pieces[:half] + core_swap(pieces[half:])
    total = mine[0]
    for by in range(1, half):
        total = total + chip_shift(mine[by], -by)
    return total


def sum_all(array):
    size = lax.axis_size("tok")
    if not direct(size):
        return jnp.sum(lax.all_gather(array, "tok"), axis=0)
    array = array + core_swap(array)
    total = array
    for by in range(1, size // 2):
        total = total + chip_shift(array, by)
    return total


def rows_to_hidden(rows):
    size = lax.axis_size("tok")
    count, depth, width = rows.shape
    parts = rows.reshape(count, depth, size, width // size).transpose(2, 0, 3, 1)
    parts = lax.all_to_all(parts, "tok", 0, 0)
    return parts.transpose(1, 2, 0, 3).reshape(count, width // size, depth * size)


def hidden_to_rows(slices):
    size = lax.axis_size("tok")
    count, depth, width = slices.shape
    parts = slices.reshape(count, depth, size, width // size).transpose(2, 0, 1, 3)
    parts = lax.all_to_all(parts, "tok", 0, 0)
    return parts.transpose(1, 3, 0, 2).reshape(count, width // size, depth * size)


def to_block(array, source, target, by=0):
    size = lax.axis_size("tok")
    pairs = [(source * size + j, target * size + (j + by) % size) for j in range(size)]
    return lax.ppermute(array, ("block", "tok"), pairs)


def up_one(array):
    groups = lax.axis_size("block")
    return lax.ppermute(array, "block", [(i, i + 1) for i in range(groups - 1)])


def slice_forward(weights, keys, scaled):
    first, gate = mm_nt(weights[0], keys), mm_nt(weights[1], keys)
    value, d_one, d_two = silu_parts(first)
    d_mixed = mm_nt(weights[2], scaled)
    mixed = value * gate
    d_gate = d_mixed * value
    d_first = d_mixed * gate * d_one
    grads = jnp.stack([mm(d_first, keys), mm(d_gate, keys), mm(mixed, scaled)])
    return grads, (gate, value, d_one, d_two, d_mixed)


def slice_adjoint(cot, kept, keys, scaled):
    gate, value, d_one, d_two, d_mixed = kept
    t_first, t_gate, p_mixed = mm_nt(cot[0], keys), mm_nt(cot[1], keys), mm_nt(cot[2], scaled)
    t_mixed = d_one * t_first * gate + value * t_gate
    c_gate = p_mixed * value + d_mixed * d_one * t_first
    c_first = p_mixed * gate * d_one + d_mixed * (d_two * t_first * gate + d_one * t_gate)
    return jnp.stack([mm(c_first, keys), mm(c_gate, keys), mm(t_mixed, scaled)])


def query_adjoint(weights, queries, out_cot):
    first, gate = mm_nt(queries, weights[0]), mm_nt(queries, weights[1])
    value, d_one, _ = silu_parts(first)
    d_mixed = mm_nt(out_cot, weights[2])
    d_gate = d_mixed * value
    d_first = d_mixed * gate * d_one
    d_queries = mm(d_first, weights[0]) + mm(d_gate, weights[1])
    d_weights = jnp.stack([mm_tn(d_first, queries), mm_tn(d_gate, queries), mm_tn(value * gate, out_cot)])
    return d_queries, d_weights


def token_adjoint(weights, cot, keys, scaled):
    first, gate = mm_nt(keys, weights[0]), mm_nt(keys, weights[1])
    value, d_one, d_two = silu_parts(first)
    d_mixed = mm_nt(scaled, weights[2])
    mixed = value * gate
    d_gate = d_mixed * value
    d_first = d_mixed * gate * d_one
    t_first, t_gate, p_mixed = mm_nt(keys, cot[0]), mm_nt(keys, cot[1]), mm_nt(scaled, cot[2])
    t_mixed = d_one * t_first * gate + value * t_gate
    c_gate = p_mixed * value + d_mixed * d_one * t_first
    c_first = p_mixed * gate * d_one + d_mixed * (d_two * t_first * gate + d_one * t_gate)
    d_keys = mm(c_first, weights[0]) + mm(c_gate, weights[1]) + mm(d_first, cot[0]) + mm(d_gate, cot[1])
    t_out = mm(t_mixed, weights[2]) + mm(mixed, cot[2])
    return d_keys, t_out


def over_hidden(array):
    return jnp.sum(array[:2], axis=1)


def per_device_general(queries, keys, values, rates, states, out_cot, final_cot):
    groups, size = lax.axis_size("block"), lax.axis_size("tok")
    position = lax.axis_index("block")
    own_rows = states[0]
    scaled = -rates[:, None] * values
    both = gather_pieces(jnp.stack([keys, scaled]))
    width = keys.shape[1]
    all_keys = both[:, 0].reshape(-1, width)
    all_scaled = both[:, 1].reshape(-1, width)
    split = rows_to_hidden(jnp.concatenate([own_rows[:2], final_cot[:2]]))
    own = jnp.concatenate([split[:2], own_rows[2:]])
    last = jnp.concatenate([split[2:], final_cot[2:]])
    grads, kept = slice_forward(own, all_keys, all_scaled)
    shifted = own - grads
    earlier = up_one(shifted[:2])
    sums = sum_all(jnp.concatenate([over_hidden(own * own), over_hidden(shifted * shifted), over_hidden(last * shifted)]))
    row_norm = [jnp.sqrt(sums[0:2, None, :] + EPS), jnp.sqrt(jnp.sum(own[2:] ** 2, axis=-1, keepdims=True) + EPS)]
    new_norm = [jnp.sqrt(sums[2:4, None, :] + EPS), jnp.sqrt(jnp.sum(shifted[2:] ** 2, axis=-1, keepdims=True) + EPS)]

    pieces = gather_pieces(own)
    whole = pieces.transpose(1, 0, 2, 3).reshape(3, -1, width)
    d_queries, d_weights = query_adjoint(whole, queries, out_cot)
    apply_state = spread_sum(d_weights.reshape(3, size, -1, width).transpose(1, 0, 2, 3))

    is_last = position == groups - 1
    incoming = jnp.where(is_last, last, 0.0)
    inner = jnp.where(is_last, sums[4:6], 0.0)
    for section in range(groups):
        inners = [inner[:, None, :], jnp.sum(incoming[2:] * shifted[2:], axis=-1, keepdims=True)]
        cots, straights = [], []
        for part, dot, old, new in zip((slice(0, 2), slice(2, 3)), inners, row_norm, new_norm):
            d_shifted = old / new * incoming[part] - old * dot / (new * new * new) * shifted[part]
            cots.append(-d_shifted)
            straights.append(d_shifted + dot / new * own[part] / old)
        cot = jnp.concatenate(cots)
        straight = jnp.concatenate(straights)
        rows_now = slice_adjoint(cot, kept, all_keys, all_scaled) + apply_state + straight
        if section + 1 < groups:
            source = groups - 1 - section
            partial = over_hidden(rows_now[:2] * earlier)
            incoming = incoming + to_block(rows_now, source, source - 1)
            if direct(size):
                for by in range(size):
                    inner = inner + to_block(partial, source, source - 1, by)
            else:
                inner = inner + to_block(sum_all(partial), source, source - 1)
    cot_pieces = gather_pieces(cot)
    whole_cot = cot_pieces.transpose(1, 0, 2, 3).reshape(3, -1, width)
    d_keys, t_out = token_adjoint(whole, whole_cot, keys, scaled)
    d_values = -rates[:, None] * t_out
    d_rates = -jnp.sum(values * t_out, axis=-1)
    d_rows = jnp.concatenate([hidden_to_rows(rows_now[:2]), rows_now[2:]])
    return (d_queries, d_keys, d_values, d_rates, d_rows[None])


def halves(array):
    upper = array.astype(jnp.bfloat16)
    return upper, (array - upper.astype(jnp.float32)).astype(jnp.bfloat16)


def product(left, right, contract):
    def one(a, b):
        return lax.dot_general(a, b, (((1,), (contract,)), ((), ())), preferred_element_type=jnp.float32)

    return one(left[0], right[0]) + (one(left[0], right[1]) + one(left[1], right[0]))


def nn(left, right):
    return product(left, right, 0)


def nt(left, right):
    return product(left, right, 1)


def kernel_call(body, outs, *operands, scratch=(), raw=False, spill=False, limit=24 * 1024 * 1024):
    space = pltpu.MemorySpace.HBM if raw else pltpu.VMEM
    return pl.pallas_call(
        body,
        in_specs=[pl.BlockSpec(memory_space=space) for _ in operands],
        out_specs=[pl.BlockSpec(memory_space=pltpu.VMEM) for _ in outs],
        out_shape=[(jax.ShapeDtypeStruct if spill else pltpu.VMEM)(shape, dtype) for shape, dtype in outs],
        scratch_shapes=list(scratch),
        compiler_params=pltpu.CompilerParams(vmem_limit_bytes=limit),
    )(*operands)


def my_chip():
    return lax.div(lax.axis_index("tok"), 2)


def my_core():
    return lax.rem(lax.axis_index("tok"), 2)


def in_chain():
    return (my_chip() == LOW) | (my_chip() == HIGH_CHIP)


def f32(*shape):
    return shape, jnp.float32


def bf16(*shape):
    return shape, jnp.bfloat16


def column(row, width):
    block = jnp.broadcast_to(row, (128, row.shape[1])).T
    return jnp.concatenate([block] * (width // 128), axis=1)


CHIPS = 4
LOW, HIGH_CHIP = 1, 2
CHUNK = 256
PACK_LIMIT = 61 * 1024 * 1024


def rows_at(start, count):
    return pl.ds(pl.multiple_of(start, count), count)


def pack_body(*refs):
    count = 7
    sources, outs = refs[:count], refs[count : count + CHIPS + 1]
    buffers, sems = refs[count + CHIPS + 1 : -1], refs[-1]
    copies = [pltpu.make_async_copy(a, b, sems.at[i]) for i, (a, b) in enumerate(zip(sources, buffers))]
    for copy in copies:
        copy.start()
    for copy in copies:
        copy.wait()
    keys, values, rates, rows, final, queries, cot = buffers
    packs, ahead = outs[:CHIPS], outs[CHIPS]
    tokens = keys.shape[0]
    depth = rows.shape[1]
    scaled = -column(rates[...], values.shape[1]) * values[...]
    sides = []
    for side in range(2):
        parts = []
        for core in range(2):
            lanes = []
            for source in (rows, final):
                for m in range(2):
                    for i in range(2):
                        start = (4 * side + 2 * i + core) * depth
                        lanes.append(source[m, :, start : start + depth])
            parts.append(jnp.concatenate(lanes, axis=1))
        sides.append(jnp.concatenate(parts))
    for by, pack in enumerate(packs):
        pack[:tokens] = keys[...]
        pack[tokens : 2 * tokens] = scaled
        low = jnp.bitwise_xor(my_chip(), by) == LOW
        pack[2 * tokens : 2 * tokens + 2 * depth] = jnp.where(low, sides[0], sides[1])
        if by < 2:
            pack[2 * tokens + 2 * depth : 2 * tokens + 3 * depth] = rows[2]
            pack[2 * tokens + 3 * depth :] = final[2]
    ahead[:tokens] = queries[...]
    ahead[tokens:] = cot[...]


def unpack(packs, mates, own, last, table):
    depth = own.shape[1] // 2
    base = packs[0].shape[0] - 4 * depth
    span = own.shape[1]
    chip, core = my_chip(), my_core()
    for by in range(CHIPS):
        source = jnp.bitwise_xor(chip, by)
        mine = rows_at(base + core * depth, depth)
        table[rows_at((2 * source + core) * depth, depth), :] = packs[by][mine, :]
        table[rows_at((2 * source + 1 - core) * depth, depth), :] = mates[by][mine, :]
    turned = table[...].T
    keep = jnp.where(lax.axis_index("block") == lax.axis_size("block") - 1, 1.0, 0.0)
    own[0], own[1] = turned[:span], turned[span : 2 * span]
    last[0], last[1] = turned[2 * span : 3 * span] * keep, turned[3 * span :] * keep
    low = chip == LOW
    for place, out, scale in ((2 * depth, own, 1.0), (3 * depth, last, keep)):
        cut = slice(base + place, base + place + depth)
        out[2, :depth] = jnp.where(low, packs[1][cut, :], packs[0][cut, :]) * scale
        out[2, depth:] = jnp.where(low, packs[0][cut, :], packs[1][cut, :]) * scale


def forward_body(*refs):
    packs, mates = refs[:CHIPS], refs[CHIPS : 2 * CHIPS]
    own, last, key_high, key_low, scaled_high, scaled_low, kept, shifted, sums, table = refs[2 * CHIPS :]
    pieces = packs + mates
    depth = key_high.shape[0] // len(pieces)
    span = own.shape[1]

    @pl.when(~in_chain())
    def _():
        for out in (own, shifted, sums):
            out[...] = jnp.zeros(out.shape, jnp.float32)

    @pl.when(in_chain())
    def _():
        unpack(packs, mates, own, last, table)
        for index, piece in enumerate(pieces):
            cut = slice(index * depth, (index + 1) * depth)
            key_high[cut, :], key_low[cut, :] = halves(piece[:depth, :])
            scaled_high[cut, :], scaled_low[cut, :] = halves(piece[depth : 2 * depth, :])
        pair = halves(jnp.concatenate([own[0], own[1]]))
        second = halves(own[2])
        grad_pair, grad_second = 0.0, 0.0
        for start in range(0, key_high.shape[0], CHUNK):
            cut = slice(start, start + CHUNK)
            key_cut = key_high[cut, :], key_low[cut, :]
            scaled_cut = scaled_high[cut, :], scaled_low[cut, :]
            both = nt(pair, key_cut)
            d_mixed = nt(second, scaled_cut)
            first, gate = both[:span], both[span:]
            value, d_one, d_two = silu_parts(first)
            for place, array in enumerate((gate, value, d_one, d_two, d_mixed)):
                kept[place, :, cut] = array
            d_pair = jnp.concatenate([d_mixed * gate * d_one, d_mixed * value])
            grad_pair += nn(halves(d_pair), key_cut)
            grad_second += nn(halves(value * gate), scaled_cut)
        moved = own[0] - grad_pair[:span], own[1] - grad_pair[span:], own[2] - grad_second
        rows = []
        for left, right in ((own, own), (moved, moved), (last, moved)):
            rows += [jnp.sum(left[m] * right[m], axis=0, keepdims=True) for m in range(2)]
        sums[...] = jnp.concatenate(rows + [jnp.zeros((2, own.shape[2]), jnp.float32)])
        for m in range(3):
            shifted[m] = moved[m]


def apply_body(source, own, raw, earlier, *refs):
    pieces, (applied, payload, partial) = refs[:-3], refs[-3:]
    span = own.shape[1]
    depth = pieces[0].shape[0] // 2
    active = (lax.axis_index("block") == source) & in_chain()

    @pl.when(~active)
    def _():
        payload[...] = jnp.zeros(payload.shape, jnp.float32)
        partial[...] = jnp.zeros(partial.shape, jnp.float32)

    @pl.when(in_chain())
    def _():
        pair = halves(jnp.concatenate([own[0], own[1]]))
        second = halves(own[2])
        out_pair, out_second = 0.0, 0.0
        for index in range(0, len(pieces), 2):
            one, two = pieces[index], pieces[index + 1]
            query = halves(jnp.concatenate([one[:depth, :], two[:depth, :]]))
            cot = halves(jnp.concatenate([one[depth:, :], two[depth:, :]]))
            both = nt(pair, query)
            d_mixed = nt(second, cot)
            first, gate = both[:span], both[span:]
            value, d_one, _ = silu_parts(first)
            out_pair += nn(halves(jnp.concatenate([d_mixed * gate * d_one, d_mixed * value])), query)
            out_second += nn(halves(value * gate), cot)
        applied[: 2 * span] = out_pair
        applied[2 * span :] = out_second

    @pl.when(active)
    def _():
        rows = [raw[m] + applied[m * span : (m + 1) * span, :] for m in range(3)]
        finish(rows, earlier, payload, partial)


def finish(rows, earlier, payload, partial):
    sums = [jnp.sum(rows[m] * earlier[m], axis=0, keepdims=True) for m in range(2)]
    partial[...] = jnp.concatenate(sums + [jnp.zeros((6, rows[0].shape[1]), jnp.float32)])
    for m in range(3):
        payload[m] = rows[m]


def state_terms(own, shifted, last, sums, inners, arrived):
    total = sums[0][...] + sums[1][...] + (sums[2][...] + sums[3][...])
    inner = total[4:6]
    for array in inners:
        inner = inner + array[0:2]
    cots, straights = [], []
    for m in range(3):
        incoming = last[m]
        for array in arrived:
            incoming = incoming + array[m]
        if m < 2:
            dot, old, new = inner[m : m + 1], jnp.sqrt(total[m : m + 1] + EPS), jnp.sqrt(total[m + 2 : m + 3] + EPS)
        else:
            dot = jnp.sum(incoming * shifted[m], axis=-1, keepdims=True)
            old = jnp.sqrt(jnp.sum(own[m] * own[m], axis=-1, keepdims=True) + EPS)
            new = jnp.sqrt(jnp.sum(shifted[m] * shifted[m], axis=-1, keepdims=True) + EPS)
        d_shifted = old / new * incoming - old * dot / (new * new * new) * shifted[m]
        cots.append(-d_shifted)
        straights.append(d_shifted + dot / new * own[m] / old)
    return cots, straights


def section_rows(count, refs):
    own, shifted, last = refs[:3]
    sums, inners, arrived = refs[3:7], refs[7 : 7 + 4 * count], refs[7 + 4 * count : 7 + 5 * count]
    key_high, key_low, scaled_high, scaled_low, kept = refs[7 + 5 * count : 12 + 5 * count]
    span = own.shape[1]
    cots, straights = state_terms(own, shifted, last, sums, inners, arrived)
    pair = halves(jnp.concatenate(cots[:2]))
    second = halves(cots[2])
    d_pair, d_second = 0.0, 0.0
    for start in range(0, key_high.shape[0], CHUNK):
        cut = slice(start, start + CHUNK)
        key_cut = key_high[cut, :], key_low[cut, :]
        scaled_cut = scaled_high[cut, :], scaled_low[cut, :]
        gate, value, d_one, d_two, d_mixed = [kept[place, :, cut] for place in range(5)]
        both = nt(pair, key_cut)
        p_mixed = nt(second, scaled_cut)
        t_first, t_gate = both[:span], both[span:]
        lift = d_one * t_first
        t_mixed = lift * gate + value * t_gate
        c_gate = p_mixed * value + d_mixed * lift
        c_first = p_mixed * gate * d_one + d_mixed * (d_two * t_first * gate + d_one * t_gate)
        d_pair += nn(halves(jnp.concatenate([c_first, c_gate])), key_cut)
        d_second += nn(halves(t_mixed), scaled_cut)
    return [d_pair[:span] + straights[0], d_pair[span:] + straights[1], d_second + straights[2]]


def first_body(source, *refs):
    raw = refs[-1]

    @pl.when((lax.axis_index("block") == source) & in_chain())
    def _():
        rows = section_rows(0, refs)
        for m in range(3):
            raw[m] = rows[m]


def section_body(source, *refs):
    applied, earlier, payload, partial = refs[-4:]
    active = (lax.axis_index("block") == source) & in_chain()

    @pl.when(~active)
    def _():
        payload[...] = jnp.zeros(payload.shape, jnp.float32)
        partial[...] = jnp.zeros(partial.shape, jnp.float32)

    @pl.when(active)
    def _():
        span = payload.shape[1]
        rows = section_rows(1, refs)
        finish([row + applied[m * span : (m + 1) * span, :] for m, row in enumerate(rows)], earlier, payload, partial)


def terms_body(count, *refs):
    cot = refs[-1]
    span = refs[0].shape[1]

    @pl.when(~in_chain())
    def _():
        cot[...] = jnp.zeros(cot.shape, jnp.float32)

    @pl.when(in_chain())
    def _():
        cots, _ = state_terms(*refs[:3], refs[3:7], refs[7 : 7 + 4 * count], refs[7 + 4 * count : 7 + 5 * count])
        for m in range(3):
            cot[m * span : (m + 1) * span, :] = cots[m]


def final_body(count, *refs):
    applied, outs, table = refs[-6], refs[-5:-1], refs[-1]
    span = refs[0].shape[1]
    depth = span // 2
    chip = my_chip()

    @pl.when(~in_chain())
    def _():
        for out in outs:
            out[...] = jnp.zeros(out.shape, jnp.float32)

    @pl.when(in_chain())
    def _():
        rows = [row + applied[m * span : (m + 1) * span, :] for m, row in enumerate(section_rows(count, refs))]
        table[...] = jnp.concatenate(rows[:2]).T
        low = chip == LOW
        upper, lower = rows[2][:depth], rows[2][depth:]
        picks = jnp.where(low, lower, upper), jnp.where(low, upper, lower), upper, upper
        for by, (out, pick) in enumerate(zip(outs, picks)):
            start = rows_at(jnp.bitwise_xor(chip, by) * 2 * depth, 2 * depth)
            out[:, :128] = table[start, :]
            out[:depth, 128:] = pick[:, :128]
            out[depth:, 128:] = pick[:, 128:]


def joined(refs):
    return [[refs[i], refs[i + 1]] for i in range(0, 8, 2)]


def taken(pair, cut):
    return pair[0][cut, :] + pair[1][cut, :]


def load_halves(pieces, part, span):
    return halves(jnp.concatenate([taken(pair, slice(part * span, (part + 1) * span)) for pair in pieces]))


def query_body(queries, out_cot, *refs):
    pieces, d_queries = joined(refs[:8]), refs[8]
    span = queries.shape[1] // len(pieces)
    one, three, two = [load_halves(pieces, part, span) for part in range(3)]
    query, cot = halves(queries[...]), halves(out_cot[...])
    first, gate = nt(query, one), nt(query, three)
    value, d_one, _ = silu_parts(first)
    d_mixed = nt(cot, two)
    d_gate = d_mixed * value
    d_first = d_mixed * gate * d_one
    d_queries[...] = nn(halves(d_first), one) + nn(halves(d_gate), three)


def token_body(keys, values, rates, *refs):
    weights, cots = joined(refs[:8]), joined(refs[8:16])
    d_keys, d_values, d_rates, d_rows = refs[24:]
    width = keys.shape[1]
    span = width // len(weights)
    one, three, two = [load_halves(weights, part, span) for part in range(3)]
    c_one, c_three, c_two = [load_halves(cots, part, span) for part in range(3)]
    ends = [taken(pair, slice(None)) for pair in joined(refs[16:24])]
    rate = column(rates[...], width)
    key, scaled = halves(keys[...]), halves(-rate * values[...])
    first, gate = nt(key, one), nt(key, three)
    value, d_one, d_two = silu_parts(first)
    d_mixed = nt(scaled, two)
    t_first, t_gate, p_mixed = nt(key, c_one), nt(key, c_three), nt(scaled, c_two)
    mixed = value * gate
    d_gate = d_mixed * value
    d_first = d_mixed * gate * d_one
    lift = d_one * t_first
    t_mixed = lift * gate + value * t_gate
    c_gate = p_mixed * value + d_mixed * lift
    c_first = p_mixed * gate * d_one + d_mixed * (d_two * t_first * gate + d_one * t_gate)
    d_keys[...] = nn(halves(c_first), one) + nn(halves(c_gate), three) + nn(halves(d_first), c_one) + nn(halves(d_gate), c_three)
    t_out = nn(halves(t_mixed), two) + nn(halves(mixed), c_two)
    d_values[...] = -rate * t_out
    d_rates[...] = -jnp.sum((values[...] * t_out).T, axis=0, keepdims=True)
    depth = d_rows.shape[1]
    low_side, upper_core = my_chip() <= LOW, my_core() == 0
    sides = []
    for near, far in ((ends[0], ends[1]), (ends[2], ends[3])):
        pair = jnp.where(low_side, near, far), jnp.where(low_side, far, near)
        sides.append([jnp.where(upper_core, piece[:depth], piece[depth:]) for piece in pair])
    by_core = [[jnp.where(upper_core, a, b) for a, b in zip(*sides)], [jnp.where(upper_core, b, a) for a, b in zip(*sides)]]
    for m in range(2):
        parts = []
        for side in range(2):
            for i in range(2):
                for core in range(2):
                    start = (2 * m + i) * depth
                    parts.append(by_core[core][side][:, start : start + depth])
        d_rows[m] = jnp.concatenate(parts, axis=1)
    d_rows[2] = jnp.concatenate([ends[0][:depth, 128:], ends[0][depth:, 128:]], axis=1)


def by_xor(array, by, chips):
    return lax.ppermute(array, "tok", [(2 * a + core, 2 * (a ^ by) + core) for a in chips for core in range(2)])


def both_cores(pieces):
    swapped = [core_swap(pieces[0])]
    return pieces + swapped + [core_swap(piece) for piece in pieces[1:]]


def hops(arrays, near, far, across):
    first = by_xor(arrays[1], 1, near)
    second = by_xor(arrays[2], 2, far)
    third = by_xor(arrays[3], 3, across)
    return first, second, third


ALL, MIDDLE, OUTER = tuple(range(CHIPS)), (LOW, HIGH_CHIP), (0, CHIPS - 1)


def to_chain(arrays):
    return both_cores([arrays[0], *hops(arrays, ALL, OUTER, MIDDLE)])


def from_chain(arrays, whole):
    near, far, across = hops(arrays, ALL, ALL if whole else MIDDLE, ALL if whole else MIDDLE)
    return both_cores([arrays[0], near, across, far])


def to_earlier(array):
    groups = lax.axis_size("block")
    return lax.ppermute(array, "block", [(i, (i - 1) % groups) for i in range(groups)])


def chain_to_block(array, source, target, by):
    size = lax.axis_size("tok")
    places = [(chip, core) for chip in (LOW, HIGH_CHIP) for core in range(2)]
    return lax.ppermute(
        array,
        ("block", "tok"),
        [(source * size + 2 * chip + core, target * size + 2 * (chip ^ by) + core) for chip, core in places],
    )


def to_later(array):
    groups = lax.axis_size("block")
    return lax.ppermute(array, "block", [(i, (i + 1) % groups) for i in range(groups)])


def per_device(queries, keys, values, rates, states, out_cot, final_cot):
    groups, size = lax.axis_size("block"), lax.axis_size("tok")
    depth, width = keys.shape
    own_rows = states[0]
    rows = own_rows.shape[1]
    if not (size == 2 * CHIPS and 4 * rows == 128 and depth == 128 and width == 8 * rows):
        return per_device_general(queries, keys, values, rates, states, out_cot, final_cot)
    span, tokens = 2 * rows, depth * size
    rates_row = rates.reshape(1, depth)
    state, square, wide = f32(3, span, width), f32(depth, width), f32(3 * span, width)
    sources = (keys, values, rates_row, own_rows, final_cot, queries, out_cot)
    longer, shorter = f32(2 * depth + 4 * rows, width), f32(2 * depth + 2 * rows, width)
    *packs, ahead = kernel_call(
        pack_body,
        [longer, longer, shorter, shorter, f32(2 * depth, width)],
        *sources,
        scratch=[pltpu.VMEM(array.shape, array.dtype) for array in sources] + [pltpu.SemaphoreType.DMA((len(sources),))],
        raw=True,
        limit=PACK_LIMIT,
    )
    pieces = to_chain(packs)
    ahead_pieces = to_chain([ahead] * CHIPS)
    half = bf16(tokens, width)
    own, last, *halved, kept, shifted, sums = kernel_call(
        forward_body,
        [state, state, half, half, half, half, f32(5, span, tokens), state, f32(8, width)],
        *pieces,
        scratch=[pltpu.VMEM((width, 4 * span), jnp.float32)],
    )
    across = by_xor(sums, 3, ALL)
    all_sums = [sums, core_swap(sums), across, core_swap(across)]
    earlier = to_later(shifted)
    weights = from_chain([own.reshape(3 * span, width)] * CHIPS, False)

    inners, arrived = [], []
    common = [own, shifted, last, *all_sums]
    sent = [state, f32(8, width)]
    (raw,) = kernel_call(functools.partial(first_body, groups - 1), [state], *common, *halved, kept)
    for section in range(groups - 1):
        source = groups - 1 - section
        if section == 0:
            body = functools.partial(apply_body, source)
            applied, payload, partial = kernel_call(body, [wide] + sent, own, raw, earlier, *ahead_pieces)
        else:
            body = functools.partial(section_body, source)
            payload, partial = kernel_call(
                body, sent, *common, *inners[-4:], *arrived[-1:], *halved, kept, applied, earlier
            )
        cross = chain_to_block(partial, source, source - 1, 3)
        straight = to_earlier(partial)
        arrived.append(to_earlier(payload))
        inners += [straight, cross, core_swap(straight), core_swap(cross)]
    received = [*common, *inners, *arrived]
    (cot,) = kernel_call(functools.partial(terms_body, groups - 1), [wide], *received)
    cots = from_chain([cot] * CHIPS, False)
    ends = kernel_call(
        functools.partial(final_body, groups - 1),
        [f32(2 * rows, width)] * CHIPS,
        *received,
        *halved,
        kept,
        applied,
        scratch=[pltpu.VMEM((width, 128), jnp.float32)],
    )
    end_pieces = from_chain(ends, True)
    (d_queries,) = kernel_call(query_body, [square], queries, out_cot, *weights, spill=True)
    d_keys, d_values, d_rates, d_rows = kernel_call(
        token_body,
        [square, square, f32(1, depth), f32(3, rows, width)],
        keys,
        values,
        rates_row,
        *weights,
        *cots,
        *end_pieces,
        spill=True,
    )
    return (d_queries, d_keys, d_values, d_rates.reshape(depth), d_rows[None])


def solution(mesh):
    return jax.shard_map(
        per_device,
        mesh=mesh,
        in_specs=(
            P(("block", "tok"), None),
            P(("block", "tok"), None),
            P(("block", "tok"), None),
            P(("block", "tok")),
            P("block", None, "tok", None),
            P(("block", "tok"), None),
            P(None, "tok", None),
        ),
        out_specs=(
            P(("block", "tok"), None),
            P(("block", "tok"), None),
            P(("block", "tok"), None),
            P(("block", "tok")),
            P("block", None, "tok", None),
        ),
        check_vma=False,
    )
```

```python
import functools

import jax
import jax.numpy as jnp
from jax import lax
from jax.experimental import pallas as pl
from jax.experimental.pallas import tpu as pltpu
from jax.sharding import PartitionSpec as P


EPS = 1e-06
HIGH = lax.Precision.HIGHEST


def mm(left, right):
    return lax.dot_general(left, right, (((1,), (0,)), ((), ())), precision=HIGH, preferred_element_type=jnp.float32)


def mm_nt(left, right):
    return lax.dot_general(left, right, (((1,), (1,)), ((), ())), precision=HIGH, preferred_element_type=jnp.float32)


def mm_tn(left, right):
    return lax.dot_general(left, right, (((0,), (0,)), ((), ())), precision=HIGH, preferred_element_type=jnp.float32)


def silu_parts(first):
    sig = 1.0 / (1.0 + jnp.exp(-first))
    slope = sig * (1.0 - sig)
    value = first * sig
    d_one = sig + first * slope
    d_two = slope * (2.0 + first * (1.0 - 2.0 * sig))
    return value, d_one, d_two


def direct(size):
    return size % 2 == 0 and size <= 16


def chip_shift(array, by):
    size = lax.axis_size("tok")
    return lax.ppermute(array, "tok", [(j, (j + 2 * by) % size) for j in range(size)])


def core_swap(array):
    size = lax.axis_size("tok")
    return lax.ppermute(array, "tok", [(j, j ^ 1) for j in range(size)])


def gather_pieces(array):
    size = lax.axis_size("tok")
    if not direct(size):
        return lax.all_gather(array, "tok")
    mine = jnp.stack([array] + [chip_shift(array, by) for by in range(1, size // 2)])
    return jnp.concatenate([mine, core_swap(mine)])


def spread_sum(pieces):
    size = lax.axis_size("tok")
    if not direct(size):
        return lax.psum_scatter(pieces, "tok")
    half = size // 2
    mine = pieces[:half] + core_swap(pieces[half:])
    total = mine[0]
    for by in range(1, half):
        total = total + chip_shift(mine[by], -by)
    return total


def sum_all(array):
    size = lax.axis_size("tok")
    if not direct(size):
        return jnp.sum(lax.all_gather(array, "tok"), axis=0)
    array = array + core_swap(array)
    total = array
    for by in range(1, size // 2):
        total = total + chip_shift(array, by)
    return total


def rows_to_hidden(rows):
    size = lax.axis_size("tok")
    count, depth, width = rows.shape
    parts = rows.reshape(count, depth, size, width // size).transpose(2, 0, 3, 1)
    parts = lax.all_to_all(parts, "tok", 0, 0)
    return parts.transpose(1, 2, 0, 3).reshape(count, width // size, depth * size)


def hidden_to_rows(slices):
    size = lax.axis_size("tok")
    count, depth, width = slices.shape
    parts = slices.reshape(count, depth, size, width // size).transpose(2, 0, 1, 3)
    parts = lax.all_to_all(parts, "tok", 0, 0)
    return parts.transpose(1, 3, 0, 2).reshape(count, width // size, depth * size)


def to_block(array, source, target, by=0):
    size = lax.axis_size("tok")
    pairs = [(source * size + j, target * size + (j + by) % size) for j in range(size)]
    return lax.ppermute(array, ("block", "tok"), pairs)


def up_one(array):
    groups = lax.axis_size("block")
    return lax.ppermute(array, "block", [(i, i + 1) for i in range(groups - 1)])


def slice_forward(weights, keys, scaled):
    first, gate = mm_nt(weights[0], keys), mm_nt(weights[1], keys)
    value, d_one, d_two = silu_parts(first)
    d_mixed = mm_nt(weights[2], scaled)
    mixed = value * gate
    d_gate = d_mixed * value
    d_first = d_mixed * gate * d_one
    grads = jnp.stack([mm(d_first, keys), mm(d_gate, keys), mm(mixed, scaled)])
    return grads, (gate, value, d_one, d_two, d_mixed)


def slice_adjoint(cot, kept, keys, scaled):
    gate, value, d_one, d_two, d_mixed = kept
    t_first, t_gate, p_mixed = mm_nt(cot[0], keys), mm_nt(cot[1], keys), mm_nt(cot[2], scaled)
    t_mixed = d_one * t_first * gate + value * t_gate
    c_gate = p_mixed * value + d_mixed * d_one * t_first
    c_first = p_mixed * gate * d_one + d_mixed * (d_two * t_first * gate + d_one * t_gate)
    return jnp.stack([mm(c_first, keys), mm(c_gate, keys), mm(t_mixed, scaled)])


def query_adjoint(weights, queries, out_cot):
    first, gate = mm_nt(queries, weights[0]), mm_nt(queries, weights[1])
    value, d_one, _ = silu_parts(first)
    d_mixed = mm_nt(out_cot, weights[2])
    d_gate = d_mixed * value
    d_first = d_mixed * gate * d_one
    d_queries = mm(d_first, weights[0]) + mm(d_gate, weights[1])
    d_weights = jnp.stack([mm_tn(d_first, queries), mm_tn(d_gate, queries), mm_tn(value * gate, out_cot)])
    return d_queries, d_weights


def token_adjoint(weights, cot, keys, scaled):
    first, gate = mm_nt(keys, weights[0]), mm_nt(keys, weights[1])
    value, d_one, d_two = silu_parts(first)
    d_mixed = mm_nt(scaled, weights[2])
    mixed = value * gate
    d_gate = d_mixed * value
    d_first = d_mixed * gate * d_one
    t_first, t_gate, p_mixed = mm_nt(keys, cot[0]), mm_nt(keys, cot[1]), mm_nt(scaled, cot[2])
    t_mixed = d_one * t_first * gate + value * t_gate
    c_gate = p_mixed * value + d_mixed * d_one * t_first
    c_first = p_mixed * gate * d_one + d_mixed * (d_two * t_first * gate + d_one * t_gate)
    d_keys = mm(c_first, weights[0]) + mm(c_gate, weights[1]) + mm(d_first, cot[0]) + mm(d_gate, cot[1])
    t_out = mm(t_mixed, weights[2]) + mm(mixed, cot[2])
    return d_keys, t_out


def over_hidden(array):
    return jnp.sum(array[:2], axis=1)


def per_device_general(queries, keys, values, rates, states, out_cot, final_cot):
    groups, size = lax.axis_size("block"), lax.axis_size("tok")
    position = lax.axis_index("block")
    own_rows = states[0]
    scaled = -rates[:, None] * values
    both = gather_pieces(jnp.stack([keys, scaled]))
    width = keys.shape[1]
    all_keys = both[:, 0].reshape(-1, width)
    all_scaled = both[:, 1].reshape(-1, width)
    split = rows_to_hidden(jnp.concatenate([own_rows[:2], final_cot[:2]]))
    own = jnp.concatenate([split[:2], own_rows[2:]])
    last = jnp.concatenate([split[2:], final_cot[2:]])
    grads, kept = slice_forward(own, all_keys, all_scaled)
    shifted = own - grads
    earlier = up_one(shifted[:2])
    sums = sum_all(jnp.concatenate([over_hidden(own * own), over_hidden(shifted * shifted), over_hidden(last * shifted)]))
    row_norm = [jnp.sqrt(sums[0:2, None, :] + EPS), jnp.sqrt(jnp.sum(own[2:] ** 2, axis=-1, keepdims=True) + EPS)]
    new_norm = [jnp.sqrt(sums[2:4, None, :] + EPS), jnp.sqrt(jnp.sum(shifted[2:] ** 2, axis=-1, keepdims=True) + EPS)]

    pieces = gather_pieces(own)
    whole = pieces.transpose(1, 0, 2, 3).reshape(3, -1, width)
    d_queries, d_weights = query_adjoint(whole, queries, out_cot)
    apply_state = spread_sum(d_weights.reshape(3, size, -1, width).transpose(1, 0, 2, 3))

    is_last = position == groups - 1
    incoming = jnp.where(is_last, last, 0.0)
    inner = jnp.where(is_last, sums[4:6], 0.0)
    for section in range(groups):
        inners = [inner[:, None, :], jnp.sum(incoming[2:] * shifted[2:], axis=-1, keepdims=True)]
        cots, straights = [], []
        for part, dot, old, new in zip((slice(0, 2), slice(2, 3)), inners, row_norm, new_norm):
            d_shifted = old / new * incoming[part] - old * dot / (new * new * new) * shifted[part]
            cots.append(-d_shifted)
            straights.append(d_shifted + dot / new * own[part] / old)
        cot = jnp.concatenate(cots)
        straight = jnp.concatenate(straights)
        rows_now = slice_adjoint(cot, kept, all_keys, all_scaled) + apply_state + straight
        if section + 1 < groups:
            source = groups - 1 - section
            partial = over_hidden(rows_now[:2] * earlier)
            incoming = incoming + to_block(rows_now, source, source - 1)
            if direct(size):
                for by in range(size):
                    inner = inner + to_block(partial, source, source - 1, by)
            else:
                inner = inner + to_block(sum_all(partial), source, source - 1)
    cot_pieces = gather_pieces(cot)
    whole_cot = cot_pieces.transpose(1, 0, 2, 3).reshape(3, -1, width)
    d_keys, t_out = token_adjoint(whole, whole_cot, keys, scaled)
    d_values = -rates[:, None] * t_out
    d_rates = -jnp.sum(values * t_out, axis=-1)
    d_rows = jnp.concatenate([hidden_to_rows(rows_now[:2]), rows_now[2:]])
    return (d_queries, d_keys, d_values, d_rates, d_rows[None])


def halves(array):
    upper = array.astype(jnp.bfloat16)
    return upper, (array - upper.astype(jnp.float32)).astype(jnp.bfloat16)


def product(left, right, contract):
    def one(a, b):
        return lax.dot_general(a, b, (((1,), (contract,)), ((), ())), preferred_element_type=jnp.float32)

    return one(left[0], right[0]) + (one(left[0], right[1]) + one(left[1], right[0]))


def nn(left, right):
    return product(left, right, 0)


def nt(left, right):
    return product(left, right, 1)


def kernel_call(body, outs, *operands, scratch=(), raw=False, spill=False, limit=24 * 1024 * 1024):
    space = pltpu.MemorySpace.HBM if raw else pltpu.VMEM
    return pl.pallas_call(
        body,
        in_specs=[pl.BlockSpec(memory_space=space) for _ in operands],
        out_specs=[pl.BlockSpec(memory_space=pltpu.VMEM) for _ in outs],
        out_shape=[(jax.ShapeDtypeStruct if spill else pltpu.VMEM)(shape, dtype) for shape, dtype in outs],
        scratch_shapes=list(scratch),
        compiler_params=pltpu.CompilerParams(vmem_limit_bytes=limit),
    )(*operands)


def my_chip():
    return lax.div(lax.axis_index("tok"), 2)


def my_core():
    return lax.rem(lax.axis_index("tok"), 2)


def in_chain():
    return (my_chip() == LOW) | (my_chip() == HIGH_CHIP)


def f32(*shape):
    return shape, jnp.float32


def bf16(*shape):
    return shape, jnp.bfloat16


def column(row, width):
    block = jnp.broadcast_to(row, (128, row.shape[1])).T
    return jnp.concatenate([block] * (width // 128), axis=1)


CHIPS = 4
LOW, HIGH_CHIP = 1, 2
CHUNK = 256
PACK_LIMIT = 61 * 1024 * 1024


def rows_at(start, count):
    return pl.ds(pl.multiple_of(start, count), count)


def pack_body(*refs):
    count = 7
    sources, outs = refs[:count], refs[count : count + CHIPS + 1]
    buffers, sems = refs[count + CHIPS + 1 : -1], refs[-1]
    copies = [pltpu.make_async_copy(a, b, sems.at[i]) for i, (a, b) in enumerate(zip(sources, buffers))]
    for copy in copies:
        copy.start()
    for copy in copies:
        copy.wait()
    keys, values, rates, rows, final, queries, cot = buffers
    packs, ahead = outs[:CHIPS], outs[CHIPS]
    tokens = keys.shape[0]
    depth = rows.shape[1]
    scaled = -column(rates[...], values.shape[1]) * values[...]
    sides = []
    for side in range(2):
        parts = []
        for core in range(2):
            lanes = []
            for source in (rows, final):
                for m in range(2):
                    for i in range(2):
                        start = (4 * side + 2 * i + core) * depth
                        lanes.append(source[m, :, start : start + depth])
            parts.append(jnp.concatenate(lanes, axis=1))
        sides.append(jnp.concatenate(parts))
    for by, pack in enumerate(packs):
        pack[:tokens] = keys[...]
        pack[tokens : 2 * tokens] = scaled
        low = jnp.bitwise_xor(my_chip(), by) == LOW
        pack[2 * tokens : 2 * tokens + 2 * depth] = jnp.where(low, sides[0], sides[1])
        if by < 2:
            pack[2 * tokens + 2 * depth : 2 * tokens + 3 * depth] = rows[2]
            pack[2 * tokens + 3 * depth :] = final[2]
    ahead[:tokens] = queries[...]
    ahead[tokens:] = cot[...]


def unpack(packs, mates, own, last, table):
    depth = own.shape[1] // 2
    base = packs[0].shape[0] - 4 * depth
    span = own.shape[1]
    chip, core = my_chip(), my_core()
    for by in range(CHIPS):
        source = jnp.bitwise_xor(chip, by)
        mine = rows_at(base + core * depth, depth)
        table[rows_at((2 * source + core) * depth, depth), :] = packs[by][mine, :]
        table[rows_at((2 * source + 1 - core) * depth, depth), :] = mates[by][mine, :]
    turned = table[...].T
    keep = jnp.where(lax.axis_index("block") == lax.axis_size("block") - 1, 1.0, 0.0)
    own[0], own[1] = turned[:span], turned[span : 2 * span]
    last[0], last[1] = turned[2 * span : 3 * span] * keep, turned[3 * span :] * keep
    low = chip == LOW
    for place, out, scale in ((2 * depth, own, 1.0), (3 * depth, last, keep)):
        cut = slice(base + place, base + place + depth)
        out[2, :depth] = jnp.where(low, packs[1][cut, :], packs[0][cut, :]) * scale
        out[2, depth:] = jnp.where(low, packs[0][cut, :], packs[1][cut, :]) * scale


def forward_body(*refs):
    packs, mates = refs[:CHIPS], refs[CHIPS : 2 * CHIPS]
    own, last, key_high, key_low, scaled_high, scaled_low, kept, shifted, sums, table = refs[2 * CHIPS :]
    pieces = packs + mates
    depth = key_high.shape[0] // len(pieces)
    span = own.shape[1]

    @pl.when(~in_chain())
    def _():
        for out in (own, shifted, sums):
            out[...] = jnp.zeros(out.shape, jnp.float32)

    @pl.when(in_chain())
    def _():
        unpack(packs, mates, own, last, table)
        for index, piece in enumerate(pieces):
            cut = slice(index * depth, (index + 1) * depth)
            key_high[cut, :], key_low[cut, :] = halves(piece[:depth, :])
            scaled_high[cut, :], scaled_low[cut, :] = halves(piece[depth : 2 * depth, :])
        pair = halves(jnp.concatenate([own[0], own[1]]))
        second = halves(own[2])
        grad_pair, grad_second = 0.0, 0.0
        for start in range(0, key_high.shape[0], CHUNK):
            cut = slice(start, start + CHUNK)
            key_cut = key_high[cut, :], key_low[cut, :]
            scaled_cut = scaled_high[cut, :], scaled_low[cut, :]
            both = nt(pair, key_cut)
            d_mixed = nt(second, scaled_cut)
            first, gate = both[:span], both[span:]
            value, d_one, d_two = silu_parts(first)
            for place, array in enumerate((gate, value, d_one, d_two, d_mixed)):
                kept[place, :, cut] = array
            d_pair = jnp.concatenate([d_mixed * gate * d_one, d_mixed * value])
            grad_pair += nn(halves(d_pair), key_cut)
            grad_second += nn(halves(value * gate), scaled_cut)
        moved = own[0] - grad_pair[:span], own[1] - grad_pair[span:], own[2] - grad_second
        rows = []
        for left, right in ((own, own), (moved, moved), (last, moved)):
            rows += [jnp.sum(left[m] * right[m], axis=0, keepdims=True) for m in range(2)]
        sums[...] = jnp.concatenate(rows + [jnp.zeros((2, own.shape[2]), jnp.float32)])
        for m in range(3):
            shifted[m] = moved[m]


def apply_body(source, own, raw, earlier, *refs):
    pieces, (applied, payload, partial) = refs[:-3], refs[-3:]
    span = own.shape[1]
    depth = pieces[0].shape[0] // 2
    active = (lax.axis_index("block") == source) & in_chain()

    @pl.when(~active)
    def _():
        payload[...] = jnp.zeros(payload.shape, jnp.float32)
        partial[...] = jnp.zeros(partial.shape, jnp.float32)

    @pl.when(in_chain())
    def _():
        pair = halves(jnp.concatenate([own[0], own[1]]))
        second = halves(own[2])
        out_pair, out_second = 0.0, 0.0
        for index in range(0, len(pieces), 2):
            one, two = pieces[index], pieces[index + 1]
            query = halves(jnp.concatenate([one[:depth, :], two[:depth, :]]))
            cot = halves(jnp.concatenate([one[depth:, :], two[depth:, :]]))
            both = nt(pair, query)
            d_mixed = nt(second, cot)
            first, gate = both[:span], both[span:]
            value, d_one, _ = silu_parts(first)
            out_pair += nn(halves(jnp.concatenate([d_mixed * gate * d_one, d_mixed * value])), query)
            out_second += nn(halves(value * gate), cot)
        applied[: 2 * span] = out_pair
        applied[2 * span :] = out_second

    @pl.when(active)
    def _():
        rows = [raw[m] + applied[m * span : (m + 1) * span, :] for m in range(3)]
        finish(rows, earlier, payload, partial)


def finish(rows, earlier, payload, partial):
    sums = [jnp.sum(rows[m] * earlier[m], axis=0, keepdims=True) for m in range(2)]
    partial[...] = jnp.concatenate(sums + [jnp.zeros((6, rows[0].shape[1]), jnp.float32)])
    for m in range(3):
        payload[m] = rows[m]


def state_terms(own, shifted, last, sums, inners, arrived):
    total = sums[0][...] + sums[1][...] + (sums[2][...] + sums[3][...])
    inner = total[4:6]
    for array in inners:
        inner = inner + array[0:2]
    cots, straights = [], []
    for m in range(3):
        incoming = last[m]
        for array in arrived:
            incoming = incoming + array[m]
        if m < 2:
            dot, old, new = inner[m : m + 1], jnp.sqrt(total[m : m + 1] + EPS), jnp.sqrt(total[m + 2 : m + 3] + EPS)
        else:
            dot = jnp.sum(incoming * shifted[m], axis=-1, keepdims=True)
            old = jnp.sqrt(jnp.sum(own[m] * own[m], axis=-1, keepdims=True) + EPS)
            new = jnp.sqrt(jnp.sum(shifted[m] * shifted[m], axis=-1, keepdims=True) + EPS)
        d_shifted = old / new * incoming - old * dot / (new * new * new) * shifted[m]
        cots.append(-d_shifted)
        straights.append(d_shifted + dot / new * own[m] / old)
    return cots, straights


def section_rows(count, refs):
    own, shifted, last = refs[:3]
    sums, inners, arrived = refs[3:7], refs[7 : 7 + 4 * count], refs[7 + 4 * count : 7 + 5 * count]
    key_high, key_low, scaled_high, scaled_low, kept = refs[7 + 5 * count : 12 + 5 * count]
    span = own.shape[1]
    cots, straights = state_terms(own, shifted, last, sums, inners, arrived)
    pair = halves(jnp.concatenate(cots[:2]))
    second = halves(cots[2])
    d_pair, d_second = 0.0, 0.0
    for start in range(0, key_high.shape[0], CHUNK):
        cut = slice(start, start + CHUNK)
        key_cut = key_high[cut, :], key_low[cut, :]
        scaled_cut = scaled_high[cut, :], scaled_low[cut, :]
        gate, value, d_one, d_two, d_mixed = [kept[place, :, cut] for place in range(5)]
        both = nt(pair, key_cut)
        p_mixed = nt(second, scaled_cut)
        t_first, t_gate = both[:span], both[span:]
        lift = d_one * t_first
        t_mixed = lift * gate + value * t_gate
        c_gate = p_mixed * value + d_mixed * lift
        c_first = p_mixed * gate * d_one + d_mixed * (d_two * t_first * gate + d_one * t_gate)
        d_pair += nn(halves(jnp.concatenate([c_first, c_gate])), key_cut)
        d_second += nn(halves(t_mixed), scaled_cut)
    return [d_pair[:span] + straights[0], d_pair[span:] + straights[1], d_second + straights[2]]


def first_body(source, *refs):
    raw = refs[-1]

    @pl.when((lax.axis_index("block") == source) & in_chain())
    def _():
        rows = section_rows(0, refs)
        for m in range(3):
            raw[m] = rows[m]


def section_body(source, *refs):
    applied, earlier, payload, partial = refs[-4:]
    active = (lax.axis_index("block") == source) & in_chain()

    @pl.when(~active)
    def _():
        payload[...] = jnp.zeros(payload.shape, jnp.float32)
        partial[...] = jnp.zeros(partial.shape, jnp.float32)

    @pl.when(active)
    def _():
        span = payload.shape[1]
        rows = section_rows(1, refs)
        finish([row + applied[m * span : (m + 1) * span, :] for m, row in enumerate(rows)], earlier, payload, partial)


def terms_body(count, *refs):
    cot = refs[-1]
    span = refs[0].shape[1]

    @pl.when(~in_chain())
    def _():
        cot[...] = jnp.zeros(cot.shape, jnp.float32)

    @pl.when(in_chain())
    def _():
        cots, _ = state_terms(*refs[:3], refs[3:7], refs[7 : 7 + 4 * count], refs[7 + 4 * count : 7 + 5 * count])
        for m in range(3):
            cot[m * span : (m + 1) * span, :] = cots[m]


def final_body(count, *refs):
    applied, outs, table = refs[-6], refs[-5:-1], refs[-1]
    span = refs[0].shape[1]
    depth = span // 2
    chip = my_chip()

    @pl.when(~in_chain())
    def _():
        for out in outs:
            out[...] = jnp.zeros(out.shape, jnp.float32)

    @pl.when(in_chain())
    def _():
        rows = [row + applied[m * span : (m + 1) * span, :] for m, row in enumerate(section_rows(count, refs))]
        table[...] = jnp.concatenate(rows[:2]).T
        low = chip == LOW
        upper, lower = rows[2][:depth], rows[2][depth:]
        picks = jnp.where(low, lower, upper), jnp.where(low, upper, lower)
        for by, out in enumerate(outs):
            out[:, :128] = table[rows_at(jnp.bitwise_xor(chip, by) * 2 * depth, 2 * depth), :]
        for out, pick in zip(outs, picks):
            out[:depth, 128:] = pick[:, :128]
            out[depth:, 128:] = pick[:, 128:]


def joined(refs):
    return [[refs[i], refs[i + 1]] for i in range(0, 8, 2)]


def taken(pair, cut):
    return pair[0][cut, :] + pair[1][cut, :]


def load_halves(pieces, part, span):
    return halves(jnp.concatenate([taken(pair, slice(part * span, (part + 1) * span)) for pair in pieces]))


def query_body(queries, out_cot, *refs):
    pieces, d_queries = joined(refs[:8]), refs[8]
    span = queries.shape[1] // len(pieces)
    one, three, two = [load_halves(pieces, part, span) for part in range(3)]
    query, cot = halves(queries[...]), halves(out_cot[...])
    first, gate = nt(query, one), nt(query, three)
    value, d_one, _ = silu_parts(first)
    d_mixed = nt(cot, two)
    d_gate = d_mixed * value
    d_first = d_mixed * gate * d_one
    d_queries[...] = nn(halves(d_first), one) + nn(halves(d_gate), three)


def token_body(keys, values, rates, *refs):
    weights, cots = joined(refs[:8]), joined(refs[8:16])
    d_keys, d_values, d_rates, d_rows = refs[24:]
    width = keys.shape[1]
    span = width // len(weights)
    one, three, two = [load_halves(weights, part, span) for part in range(3)]
    c_one, c_three, c_two = [load_halves(cots, part, span) for part in range(3)]
    ends = [taken(pair, slice(None)) for pair in joined(refs[16:24])]
    rate = column(rates[...], width)
    key, scaled = halves(keys[...]), halves(-rate * values[...])
    first, gate = nt(key, one), nt(key, three)
    value, d_one, d_two = silu_parts(first)
    d_mixed = nt(scaled, two)
    t_first, t_gate, p_mixed = nt(key, c_one), nt(key, c_three), nt(scaled, c_two)
    mixed = value * gate
    d_gate = d_mixed * value
    d_first = d_mixed * gate * d_one
    lift = d_one * t_first
    t_mixed = lift * gate + value * t_gate
    c_gate = p_mixed * value + d_mixed * lift
    c_first = p_mixed * gate * d_one + d_mixed * (d_two * t_first * gate + d_one * t_gate)
    d_keys[...] = nn(halves(c_first), one) + nn(halves(c_gate), three) + nn(halves(d_first), c_one) + nn(halves(d_gate), c_three)
    t_out = nn(halves(t_mixed), two) + nn(halves(mixed), c_two)
    d_values[...] = -rate * t_out
    d_rates[...] = -jnp.sum((values[...] * t_out).T, axis=0, keepdims=True)
    depth = d_rows.shape[1]
    low_side, upper_core = my_chip() <= LOW, my_core() == 0
    sides = []
    for near, far in ((ends[0], ends[1]), (ends[2], ends[3])):
        pair = jnp.where(low_side, near[:, :128], far), jnp.where(low_side, far, near[:, :128])
        sides.append([jnp.where(upper_core, piece[:depth], piece[depth:]) for piece in pair])
    by_core = [[jnp.where(upper_core, a, b) for a, b in zip(*sides)], [jnp.where(upper_core, b, a) for a, b in zip(*sides)]]
    for m in range(2):
        parts = []
        for side in range(2):
            for i in range(2):
                for core in range(2):
                    start = (2 * m + i) * depth
                    parts.append(by_core[core][side][:, start : start + depth])
        d_rows[m] = jnp.concatenate(parts, axis=1)
    d_rows[2] = jnp.concatenate([ends[0][:depth, 128:], ends[0][depth:, 128:]], axis=1)


def by_xor(array, by, chips):
    return lax.ppermute(array, "tok", [(2 * a + core, 2 * (a ^ by) + core) for a in chips for core in range(2)])


def exchanged(array):
    size = lax.axis_size("tok")
    gathered = [array]
    for bits in (2 * (LOW ^ HIGH_CHIP), 2 * (LOW ^ HIGH_CHIP) + 1, 1):
        gathered.append(lax.ppermute(array, "tok", [(j, j ^ bits) for j in range(size)]))
    return gathered


def both_cores(pieces):
    swapped = [core_swap(pieces[0])]
    for piece in pieces[1:]:
        swapped.append(core_swap(piece))
    return pieces + swapped


def hops(arrays, near, far, across):
    first = by_xor(arrays[1], 1, near)
    second = by_xor(arrays[2], 2, far)
    third = by_xor(arrays[3], 3, across)
    return first, second, third


ALL, MIDDLE, OUTER = tuple(range(CHIPS)), (LOW, HIGH_CHIP), (0, CHIPS - 1)


def to_chain(arrays):
    return both_cores([arrays[0], *hops(arrays, ALL, OUTER, MIDDLE)])


def from_chain(arrays, whole):
    near, far, across = hops(arrays, ALL, ALL if whole else MIDDLE, ALL if whole else MIDDLE)
    return both_cores([arrays[0], near, across, far])


def to_earlier(array):
    groups = lax.axis_size("block")
    return lax.ppermute(array, "block", [(i, (i - 1) % groups) for i in range(groups)])


def to_later(array):
    groups = lax.axis_size("block")
    return lax.ppermute(array, "block", [(i, (i + 1) % groups) for i in range(groups)])


def per_device(queries, keys, values, rates, states, out_cot, final_cot):
    groups, size = lax.axis_size("block"), lax.axis_size("tok")
    depth, width = keys.shape
    own_rows = states[0]
    rows = own_rows.shape[1]
    if not (size == 2 * CHIPS and 4 * rows == 128 and depth == 128 and width == 8 * rows):
        return per_device_general(queries, keys, values, rates, states, out_cot, final_cot)
    span, tokens = 2 * rows, depth * size
    rates_row = rates.reshape(1, depth)
    state, square, wide = f32(3, span, width), f32(depth, width), f32(3 * span, width)
    sources = (keys, values, rates_row, own_rows, final_cot, queries, out_cot)
    longer, shorter = f32(2 * depth + 4 * rows, width), f32(2 * depth + 2 * rows, width)
    *packs, ahead = kernel_call(
        pack_body,
        [longer, longer, shorter, shorter, f32(2 * depth, width)],
        *sources,
        scratch=[pltpu.VMEM(array.shape, array.dtype) for array in sources] + [pltpu.SemaphoreType.DMA((len(sources),))],
        raw=True,
        limit=PACK_LIMIT,
    )
    pieces = to_chain(packs)
    ahead_pieces = to_chain([ahead] * CHIPS)
    half = bf16(tokens, width)
    own, last, *halved, kept, shifted, sums = kernel_call(
        forward_body,
        [state, state, half, half, half, half, f32(5, span, tokens), state, f32(8, width)],
        *pieces,
        scratch=[pltpu.VMEM((width, 4 * span), jnp.float32)],
    )
    all_sums = exchanged(sums)
    earlier = to_later(shifted)
    weights = from_chain([own.reshape(3 * span, width)] * CHIPS, False)

    inners, arrived = [], []
    common = [own, shifted, last, *all_sums]
    sent = [state, f32(8, width)]
    (raw,) = kernel_call(functools.partial(first_body, groups - 1), [state], *common, *halved, kept)
    for section in range(groups - 1):
        source = groups - 1 - section
        if section == 0:
            body = functools.partial(apply_body, source)
            applied, payload, partial = kernel_call(body, [wide] + sent, own, raw, earlier, *ahead_pieces)
        else:
            body = functools.partial(section_body, source)
            payload, partial = kernel_call(
                body, sent, *common, *inners[-4:], *arrived[-1:], *halved, kept, applied, earlier
            )
        straight = to_earlier(partial)
        arrived.append(to_earlier(payload))
        inners += exchanged(straight)
    received = [*common, *inners, *arrived]
    (cot,) = kernel_call(functools.partial(terms_body, groups - 1), [wide], *received)
    cots = from_chain([cot] * CHIPS, False)
    ends = kernel_call(
        functools.partial(final_body, groups - 1),
        [f32(2 * rows, width)] * 2 + [f32(2 * rows, 128)] * 2,
        *received,
        *halved,
        kept,
        applied,
        scratch=[pltpu.VMEM((width, 128), jnp.float32)],
    )
    end_pieces = from_chain(ends, True)
    (d_queries,) = kernel_call(query_body, [square], queries, out_cot, *weights, spill=True)
    d_keys, d_values, d_rates, d_rows = kernel_call(
        token_body,
        [square, square, f32(1, depth), f32(3, rows, width)],
        keys,
        values,
        rates_row,
        *weights,
        *cots,
        *end_pieces,
        spill=True,
    )
    return (d_queries, d_keys, d_values, d_rates.reshape(depth), d_rows[None])


def solution(mesh):
    return jax.shard_map(
        per_device,
        mesh=mesh,
        in_specs=(
            P(("block", "tok"), None),
            P(("block", "tok"), None),
            P(("block", "tok"), None),
            P(("block", "tok")),
            P("block", None, "tok", None),
            P(("block", "tok"), None),
            P(None, "tok", None),
        ),
        out_specs=(
            P(("block", "tok"), None),
            P(("block", "tok"), None),
            P(("block", "tok"), None),
            P(("block", "tok")),
            P("block", None, "tok", None),
        ),
        check_vma=False,
    )
```

```python
import functools

import jax
import jax.numpy as jnp
from jax import lax
from jax.experimental import pallas as pl
from jax.experimental.pallas import tpu as pltpu
from jax.sharding import PartitionSpec as P


EPS = 1e-06
HIGH = lax.Precision.HIGHEST


def mm(left, right):
    return lax.dot_general(left, right, (((1,), (0,)), ((), ())), precision=HIGH, preferred_element_type=jnp.float32)


def mm_nt(left, right):
    return lax.dot_general(left, right, (((1,), (1,)), ((), ())), precision=HIGH, preferred_element_type=jnp.float32)


def mm_tn(left, right):
    return lax.dot_general(left, right, (((0,), (0,)), ((), ())), precision=HIGH, preferred_element_type=jnp.float32)


def silu_parts(first):
    sig = 1.0 / (1.0 + jnp.exp(-first))
    slope = sig * (1.0 - sig)
    value = first * sig
    d_one = sig + first * slope
    d_two = slope * (2.0 + first * (1.0 - 2.0 * sig))
    return value, d_one, d_two


def direct(size):
    return size % 2 == 0 and size <= 16


def chip_shift(array, by):
    size = lax.axis_size("tok")
    return lax.ppermute(array, "tok", [(j, (j + 2 * by) % size) for j in range(size)])


def core_swap(array):
    size = lax.axis_size("tok")
    return lax.ppermute(array, "tok", [(j, j ^ 1) for j in range(size)])


def gather_pieces(array):
    size = lax.axis_size("tok")
    if not direct(size):
        return lax.all_gather(array, "tok")
    mine = jnp.stack([array] + [chip_shift(array, by) for by in range(1, size // 2)])
    return jnp.concatenate([mine, core_swap(mine)])


def spread_sum(pieces):
    size = lax.axis_size("tok")
    if not direct(size):
        return lax.psum_scatter(pieces, "tok")
    half = size // 2
    mine = pieces[:half] + core_swap(pieces[half:])
    total = mine[0]
    for by in range(1, half):
        total = total + chip_shift(mine[by], -by)
    return total


def sum_all(array):
    size = lax.axis_size("tok")
    if not direct(size):
        return jnp.sum(lax.all_gather(array, "tok"), axis=0)
    array = array + core_swap(array)
    total = array
    for by in range(1, size // 2):
        total = total + chip_shift(array, by)
    return total


def rows_to_hidden(rows):
    size = lax.axis_size("tok")
    count, depth, width = rows.shape
    parts = rows.reshape(count, depth, size, width // size).transpose(2, 0, 3, 1)
    parts = lax.all_to_all(parts, "tok", 0, 0)
    return parts.transpose(1, 2, 0, 3).reshape(count, width // size, depth * size)


def hidden_to_rows(slices):
    size = lax.axis_size("tok")
    count, depth, width = slices.shape
    parts = slices.reshape(count, depth, size, width // size).transpose(2, 0, 1, 3)
    parts = lax.all_to_all(parts, "tok", 0, 0)
    return parts.transpose(1, 3, 0, 2).reshape(count, width // size, depth * size)


def to_block(array, source, target, by=0):
    size = lax.axis_size("tok")
    pairs = [(source * size + j, target * size + (j + by) % size) for j in range(size)]
    return lax.ppermute(array, ("block", "tok"), pairs)


def up_one(array):
    groups = lax.axis_size("block")
    return lax.ppermute(array, "block", [(i, i + 1) for i in range(groups - 1)])


def slice_forward(weights, keys, scaled):
    first, gate = mm_nt(weights[0], keys), mm_nt(weights[1], keys)
    value, d_one, d_two = silu_parts(first)
    d_mixed = mm_nt(weights[2], scaled)
    mixed = value * gate
    d_gate = d_mixed * value
    d_first = d_mixed * gate * d_one
    grads = jnp.stack([mm(d_first, keys), mm(d_gate, keys), mm(mixed, scaled)])
    return grads, (gate, value, d_one, d_two, d_mixed)


def slice_adjoint(cot, kept, keys, scaled):
    gate, value, d_one, d_two, d_mixed = kept
    t_first, t_gate, p_mixed = mm_nt(cot[0], keys), mm_nt(cot[1], keys), mm_nt(cot[2], scaled)
    t_mixed = d_one * t_first * gate + value * t_gate
    c_gate = p_mixed * value + d_mixed * d_one * t_first
    c_first = p_mixed * gate * d_one + d_mixed * (d_two * t_first * gate + d_one * t_gate)
    return jnp.stack([mm(c_first, keys), mm(c_gate, keys), mm(t_mixed, scaled)])


def query_adjoint(weights, queries, out_cot):
    first, gate = mm_nt(queries, weights[0]), mm_nt(queries, weights[1])
    value, d_one, _ = silu_parts(first)
    d_mixed = mm_nt(out_cot, weights[2])
    d_gate = d_mixed * value
    d_first = d_mixed * gate * d_one
    d_queries = mm(d_first, weights[0]) + mm(d_gate, weights[1])
    d_weights = jnp.stack([mm_tn(d_first, queries), mm_tn(d_gate, queries), mm_tn(value * gate, out_cot)])
    return d_queries, d_weights


def token_adjoint(weights, cot, keys, scaled):
    first, gate = mm_nt(keys, weights[0]), mm_nt(keys, weights[1])
    value, d_one, d_two = silu_parts(first)
    d_mixed = mm_nt(scaled, weights[2])
    mixed = value * gate
    d_gate = d_mixed * value
    d_first = d_mixed * gate * d_one
    t_first, t_gate, p_mixed = mm_nt(keys, cot[0]), mm_nt(keys, cot[1]), mm_nt(scaled, cot[2])
    t_mixed = d_one * t_first * gate + value * t_gate
    c_gate = p_mixed * value + d_mixed * d_one * t_first
    c_first = p_mixed * gate * d_one + d_mixed * (d_two * t_first * gate + d_one * t_gate)
    d_keys = mm(c_first, weights[0]) + mm(c_gate, weights[1]) + mm(d_first, cot[0]) + mm(d_gate, cot[1])
    t_out = mm(t_mixed, weights[2]) + mm(mixed, cot[2])
    return d_keys, t_out


def over_hidden(array):
    return jnp.sum(array[:2], axis=1)


def per_device_general(queries, keys, values, rates, states, out_cot, final_cot):
    groups, size = lax.axis_size("block"), lax.axis_size("tok")
    position = lax.axis_index("block")
    own_rows = states[0]
    scaled = -rates[:, None] * values
    both = gather_pieces(jnp.stack([keys, scaled]))
    width = keys.shape[1]
    all_keys = both[:, 0].reshape(-1, width)
    all_scaled = both[:, 1].reshape(-1, width)
    split = rows_to_hidden(jnp.concatenate([own_rows[:2], final_cot[:2]]))
    own = jnp.concatenate([split[:2], own_rows[2:]])
    last = jnp.concatenate([split[2:], final_cot[2:]])
    grads, kept = slice_forward(own, all_keys, all_scaled)
    shifted = own - grads
    earlier = up_one(shifted[:2])
    sums = sum_all(jnp.concatenate([over_hidden(own * own), over_hidden(shifted * shifted), over_hidden(last * shifted)]))
    row_norm = [jnp.sqrt(sums[0:2, None, :] + EPS), jnp.sqrt(jnp.sum(own[2:] ** 2, axis=-1, keepdims=True) + EPS)]
    new_norm = [jnp.sqrt(sums[2:4, None, :] + EPS), jnp.sqrt(jnp.sum(shifted[2:] ** 2, axis=-1, keepdims=True) + EPS)]

    pieces = gather_pieces(own)
    whole = pieces.transpose(1, 0, 2, 3).reshape(3, -1, width)
    d_queries, d_weights = query_adjoint(whole, queries, out_cot)
    apply_state = spread_sum(d_weights.reshape(3, size, -1, width).transpose(1, 0, 2, 3))

    is_last = position == groups - 1
    incoming = jnp.where(is_last, last, 0.0)
    inner = jnp.where(is_last, sums[4:6], 0.0)
    for section in range(groups):
        inners = [inner[:, None, :], jnp.sum(incoming[2:] * shifted[2:], axis=-1, keepdims=True)]
        cots, straights = [], []
        for part, dot, old, new in zip((slice(0, 2), slice(2, 3)), inners, row_norm, new_norm):
            d_shifted = old / new * incoming[part] - old * dot / (new * new * new) * shifted[part]
            cots.append(-d_shifted)
            straights.append(d_shifted + dot / new * own[part] / old)
        cot = jnp.concatenate(cots)
        straight = jnp.concatenate(straights)
        rows_now = slice_adjoint(cot, kept, all_keys, all_scaled) + apply_state + straight
        if section + 1 < groups:
            source = groups - 1 - section
            partial = over_hidden(rows_now[:2] * earlier)
            incoming = incoming + to_block(rows_now, source, source - 1)
            if direct(size):
                for by in range(size):
                    inner = inner + to_block(partial, source, source - 1, by)
            else:
                inner = inner + to_block(sum_all(partial), source, source - 1)
    cot_pieces = gather_pieces(cot)
    whole_cot = cot_pieces.transpose(1, 0, 2, 3).reshape(3, -1, width)
    d_keys, t_out = token_adjoint(whole, whole_cot, keys, scaled)
    d_values = -rates[:, None] * t_out
    d_rates = -jnp.sum(values * t_out, axis=-1)
    d_rows = jnp.concatenate([hidden_to_rows(rows_now[:2]), rows_now[2:]])
    return (d_queries, d_keys, d_values, d_rates, d_rows[None])


def halves(array):
    upper = array.astype(jnp.bfloat16)
    return upper, (array - upper.astype(jnp.float32)).astype(jnp.bfloat16)


def product(left, right, contract):
    def one(a, b):
        return lax.dot_general(a, b, (((1,), (contract,)), ((), ())), preferred_element_type=jnp.float32)

    return one(left[0], right[0]) + (one(left[0], right[1]) + one(left[1], right[0]))


def nn(left, right):
    return product(left, right, 0)


def nt(left, right):
    return product(left, right, 1)


def kernel_call(body, outs, *operands, scratch=(), raw=False, spill=False, limit=24 * 1024 * 1024):
    space = pltpu.MemorySpace.HBM if raw else pltpu.VMEM
    return pl.pallas_call(
        body,
        in_specs=[pl.BlockSpec(memory_space=space) for _ in operands],
        out_specs=[pl.BlockSpec(memory_space=pltpu.VMEM) for _ in outs],
        out_shape=[(jax.ShapeDtypeStruct if spill else pltpu.VMEM)(shape, dtype) for shape, dtype in outs],
        scratch_shapes=list(scratch),
        compiler_params=pltpu.CompilerParams(vmem_limit_bytes=limit),
    )(*operands)


def my_chip():
    return lax.div(lax.axis_index("tok"), 2)


def my_core():
    return lax.rem(lax.axis_index("tok"), 2)


def in_chain():
    return (my_chip() == LOW) | (my_chip() == HIGH_CHIP)


def f32(*shape):
    return shape, jnp.float32


def bf16(*shape):
    return shape, jnp.bfloat16


def column(row, width):
    block = jnp.broadcast_to(row, (128, row.shape[1])).T
    return jnp.concatenate([block] * (width // 128), axis=1)


CHIPS = 4
LOW, HIGH_CHIP = 1, 2
CHUNK = 256
PACK_LIMIT = 61 * 1024 * 1024


def rows_at(start, count):
    return pl.ds(pl.multiple_of(start, count), count)


def pack_body(*refs):
    count = 7
    sources, outs = refs[:count], refs[count : count + CHIPS + 1]
    buffers, sems = refs[count + CHIPS + 1 : -1], refs[-1]
    copies = [pltpu.make_async_copy(a, b, sems.at[i]) for i, (a, b) in enumerate(zip(sources, buffers))]
    for copy in copies:
        copy.start()
    for copy in copies:
        copy.wait()
    keys, values, rates, rows, final, queries, cot = buffers
    packs, ahead = outs[:CHIPS], outs[CHIPS]
    tokens = keys.shape[0]
    depth = rows.shape[1]
    scaled = -column(rates[...], values.shape[1]) * values[...]
    sides = []
    for side in range(2):
        parts = []
        for core in range(2):
            lanes = []
            for source in (rows, final):
                for m in range(2):
                    for i in range(2):
                        start = (4 * side + 2 * i + core) * depth
                        lanes.append(source[m, :, start : start + depth])
            parts.append(jnp.concatenate(lanes, axis=1))
        sides.append(jnp.concatenate(parts))
    for by, pack in enumerate(packs):
        pack[:tokens] = keys[...]
        pack[tokens : 2 * tokens] = scaled
        low = jnp.bitwise_xor(my_chip(), by) == LOW
        pack[2 * tokens : 2 * tokens + 2 * depth] = jnp.where(low, sides[0], sides[1])
        if by < 2:
            pack[2 * tokens + 2 * depth : 2 * tokens + 3 * depth] = rows[2]
            pack[2 * tokens + 3 * depth :] = final[2]
    ahead[:tokens] = queries[...]
    ahead[tokens:] = cot[...]


def unpack(packs, mates, own, last, table):
    depth = own.shape[1] // 2
    base = packs[0].shape[0] - 4 * depth
    span = own.shape[1]
    chip, core = my_chip(), my_core()
    for by in range(CHIPS):
        source = jnp.bitwise_xor(chip, by)
        mine = rows_at(base + core * depth, depth)
        table[rows_at((2 * source + core) * depth, depth), :] = packs[by][mine, :]
        table[rows_at((2 * source + 1 - core) * depth, depth), :] = mates[by][mine, :]
    turned = table[...].T
    keep = jnp.where(lax.axis_index("block") == lax.axis_size("block") - 1, 1.0, 0.0)
    own[0], own[1] = turned[:span], turned[span : 2 * span]
    last[0], last[1] = turned[2 * span : 3 * span] * keep, turned[3 * span :] * keep
    low = chip == LOW
    for place, out, scale in ((2 * depth, own, 1.0), (3 * depth, last, keep)):
        cut = slice(base + place, base + place + depth)
        out[2, :depth] = jnp.where(low, packs[1][cut, :], packs[0][cut, :]) * scale
        out[2, depth:] = jnp.where(low, packs[0][cut, :], packs[1][cut, :]) * scale


def forward_body(*refs):
    packs, mates = refs[:CHIPS], refs[CHIPS : 2 * CHIPS]
    own, last, key_high, key_low, scaled_high, scaled_low, kept, shifted, sums, table = refs[2 * CHIPS :]
    pieces = packs + mates
    depth = key_high.shape[0] // len(pieces)
    span = own.shape[1]

    @pl.when(~in_chain())
    def _():
        for out in (own, shifted, sums):
            out[...] = jnp.zeros(out.shape, jnp.float32)

    @pl.when(in_chain())
    def _():
        unpack(packs, mates, own, last, table)
        for index, piece in enumerate(pieces):
            cut = slice(index * depth, (index + 1) * depth)
            key_high[cut, :], key_low[cut, :] = halves(piece[:depth, :])
            scaled_high[cut, :], scaled_low[cut, :] = halves(piece[depth : 2 * depth, :])
        pair = halves(jnp.concatenate([own[0], own[1]]))
        second = halves(own[2])
        grad_pair, grad_second = 0.0, 0.0
        for start in range(0, key_high.shape[0], CHUNK):
            cut = slice(start, start + CHUNK)
            key_cut = key_high[cut, :], key_low[cut, :]
            scaled_cut = scaled_high[cut, :], scaled_low[cut, :]
            both = nt(pair, key_cut)
            d_mixed = nt(second, scaled_cut)
            first, gate = both[:span], both[span:]
            value, d_one, d_two = silu_parts(first)
            for place, array in enumerate((gate, value, d_one, d_two, d_mixed)):
                kept[place, :, cut] = array
            d_pair = jnp.concatenate([d_mixed * gate * d_one, d_mixed * value])
            grad_pair += nn(halves(d_pair), key_cut)
            grad_second += nn(halves(value * gate), scaled_cut)
        moved = own[0] - grad_pair[:span], own[1] - grad_pair[span:], own[2] - grad_second
        rows = []
        for left, right in ((own, own), (moved, moved), (last, moved)):
            rows += [jnp.sum(left[m] * right[m], axis=0, keepdims=True) for m in range(2)]
        sums[...] = jnp.concatenate(rows + [jnp.zeros((2, own.shape[2]), jnp.float32)])
        for m in range(3):
            shifted[m] = moved[m]


def apply_body(source, own, raw, earlier, *refs):
    pieces, (applied, payload, partial) = refs[:-3], refs[-3:]
    span = own.shape[1]
    depth = pieces[0].shape[0] // 2
    active = (lax.axis_index("block") == source) & in_chain()

    @pl.when(~active)
    def _():
        payload[...] = jnp.zeros(payload.shape, jnp.float32)
        partial[...] = jnp.zeros(partial.shape, jnp.float32)

    @pl.when(in_chain())
    def _():
        pair = halves(jnp.concatenate([own[0], own[1]]))
        second = halves(own[2])
        out_pair, out_second = 0.0, 0.0
        for index in range(0, len(pieces), 2):
            one, two = pieces[index], pieces[index + 1]
            query = halves(jnp.concatenate([one[:depth, :], two[:depth, :]]))
            cot = halves(jnp.concatenate([one[depth:, :], two[depth:, :]]))
            both = nt(pair, query)
            d_mixed = nt(second, cot)
            first, gate = both[:span], both[span:]
            value, d_one, _ = silu_parts(first)
            out_pair += nn(halves(jnp.concatenate([d_mixed * gate * d_one, d_mixed * value])), query)
            out_second += nn(halves(value * gate), cot)
        applied[: 2 * span] = out_pair
        applied[2 * span :] = out_second

    @pl.when(active)
    def _():
        rows = [raw[m] + applied[m * span : (m + 1) * span, :] for m in range(3)]
        finish(rows, earlier, payload, partial)


def finish(rows, earlier, payload, partial):
    sums = [jnp.sum(rows[m] * earlier[m], axis=0, keepdims=True) for m in range(2)]
    partial[...] = jnp.concatenate(sums + [jnp.zeros((6, rows[0].shape[1]), jnp.float32)])
    for m in range(3):
        payload[m] = rows[m]


def state_terms(own, shifted, last, sums, inners, arrived):
    total = sums[0][...] + sums[1][...] + (sums[2][...] + sums[3][...])
    inner = total[4:6]
    for array in inners:
        inner = inner + array[0:2]
    cots, straights = [], []
    for m in range(3):
        incoming = last[m]
        for array in arrived:
            incoming = incoming + array[m]
        if m < 2:
            dot, old, new = inner[m : m + 1], jnp.sqrt(total[m : m + 1] + EPS), jnp.sqrt(total[m + 2 : m + 3] + EPS)
        else:
            dot = jnp.sum(incoming * shifted[m], axis=-1, keepdims=True)
            old = jnp.sqrt(jnp.sum(own[m] * own[m], axis=-1, keepdims=True) + EPS)
            new = jnp.sqrt(jnp.sum(shifted[m] * shifted[m], axis=-1, keepdims=True) + EPS)
        d_shifted = old / new * incoming - old * dot / (new * new * new) * shifted[m]
        cots.append(-d_shifted)
        straights.append(d_shifted + dot / new * own[m] / old)
    return cots, straights


def section_rows(count, refs):
    own, shifted, last = refs[:3]
    sums, inners, arrived = refs[3:7], refs[7 : 7 + 4 * count], refs[7 + 4 * count : 7 + 5 * count]
    key_high, key_low, scaled_high, scaled_low, kept = refs[7 + 5 * count : 12 + 5 * count]
    span = own.shape[1]
    cots, straights = state_terms(own, shifted, last, sums, inners, arrived)
    pair = halves(jnp.concatenate(cots[:2]))
    second = halves(cots[2])
    d_pair, d_second = 0.0, 0.0
    for start in range(0, key_high.shape[0], CHUNK):
        cut = slice(start, start + CHUNK)
        key_cut = key_high[cut, :], key_low[cut, :]
        scaled_cut = scaled_high[cut, :], scaled_low[cut, :]
        gate, value, d_one, d_two, d_mixed = [kept[place, :, cut] for place in range(5)]
        both = nt(pair, key_cut)
        p_mixed = nt(second, scaled_cut)
        t_first, t_gate = both[:span], both[span:]
        lift = d_one * t_first
        t_mixed = lift * gate + value * t_gate
        c_gate = p_mixed * value + d_mixed * lift
        c_first = p_mixed * gate * d_one + d_mixed * (d_two * t_first * gate + d_one * t_gate)
        d_pair += nn(halves(jnp.concatenate([c_first, c_gate])), key_cut)
        d_second += nn(halves(t_mixed), scaled_cut)
    return cots, [d_pair[:span] + straights[0], d_pair[span:] + straights[1], d_second + straights[2]]


def first_body(source, *refs):
    raw = refs[-1]

    @pl.when((lax.axis_index("block") == source) & in_chain())
    def _():
        _, rows = section_rows(0, refs)
        for m in range(3):
            raw[m] = rows[m]


def section_body(source, *refs):
    applied, earlier, payload, partial = refs[-4:]
    active = (lax.axis_index("block") == source) & in_chain()

    @pl.when(~active)
    def _():
        payload[...] = jnp.zeros(payload.shape, jnp.float32)
        partial[...] = jnp.zeros(partial.shape, jnp.float32)

    @pl.when(active)
    def _():
        span = payload.shape[1]
        _, rows = section_rows(1, refs)
        finish([row + applied[m * span : (m + 1) * span, :] for m, row in enumerate(rows)], earlier, payload, partial)


def final_body(count, *refs):
    applied, outs, table = refs[-6], refs[-5:-1], refs[-1]
    span = refs[0].shape[1]
    depth = span // 2
    chip = my_chip()

    @pl.when(~in_chain())
    def _():
        for out in outs:
            out[...] = jnp.zeros(out.shape, jnp.float32)

    @pl.when(in_chain())
    def _():
        cots, rows = section_rows(count, refs)
        for out in outs:
            for m in range(3):
                out[m * span : (m + 1) * span, :] = cots[m]
        rows = [row + applied[m * span : (m + 1) * span, :] for m, row in enumerate(rows)]
        table[...] = jnp.concatenate(rows[:2]).T
        for by, out in enumerate(outs):
            start = jnp.bitwise_xor(chip, by) * 2 * depth
            for core in range(2):
                lanes = slice(core * 128, (core + 1) * 128)
                out[3 * span : 3 * span + depth, lanes] = table[rows_at(start + core * depth, depth), :]
        low = chip == LOW
        upper, lower = rows[2][:depth], rows[2][depth:]
        outs[0][3 * span + depth :] = jnp.where(low, lower, upper)
        outs[1][3 * span + depth :] = jnp.where(low, upper, lower)


def joined(refs):
    return [[refs[i], refs[i + 1]] for i in range(0, 8, 2)]


def taken(pair, cut):
    return pair[0][cut, :] + pair[1][cut, :]


def load_halves(pieces, part, span):
    return halves(jnp.concatenate([taken(pair, slice(part * span, (part + 1) * span)) for pair in pieces]))


def query_body(queries, out_cot, *refs):
    pieces, d_queries = joined(refs[:8]), refs[8]
    span = queries.shape[1] // len(pieces)
    one, three, two = [load_halves(pieces, part, span) for part in range(3)]
    query, cot = halves(queries[...]), halves(out_cot[...])
    first, gate = nt(query, one), nt(query, three)
    value, d_one, _ = silu_parts(first)
    d_mixed = nt(cot, two)
    d_gate = d_mixed * value
    d_first = d_mixed * gate * d_one
    d_queries[...] = nn(halves(d_first), one) + nn(halves(d_gate), three)


def token_body(keys, values, rates, *refs):
    weights, cots = joined(refs[:8]), joined(refs[8:16])
    d_keys, d_values, d_rates, d_rows = refs[16:]
    width = keys.shape[1]
    span = width // len(weights)
    one, three, two = [load_halves(weights, part, span) for part in range(3)]
    c_one, c_three, c_two = [load_halves(cots, part, span) for part in range(3)]
    rate = column(rates[...], width)
    key, scaled = halves(keys[...]), halves(-rate * values[...])
    first, gate = nt(key, one), nt(key, three)
    value, d_one, d_two = silu_parts(first)
    d_mixed = nt(scaled, two)
    t_first, t_gate, p_mixed = nt(key, c_one), nt(key, c_three), nt(scaled, c_two)
    mixed = value * gate
    d_gate = d_mixed * value
    d_first = d_mixed * gate * d_one
    lift = d_one * t_first
    t_mixed = lift * gate + value * t_gate
    c_gate = p_mixed * value + d_mixed * lift
    c_first = p_mixed * gate * d_one + d_mixed * (d_two * t_first * gate + d_one * t_gate)
    d_keys[...] = nn(halves(c_first), one) + nn(halves(c_gate), three) + nn(halves(d_first), c_one) + nn(halves(d_gate), c_three)
    t_out = nn(halves(t_mixed), two) + nn(halves(mixed), c_two)
    d_values[...] = -rate * t_out
    d_rates[...] = -jnp.sum((values[...] * t_out).T, axis=0, keepdims=True)
    depth = d_rows.shape[1]
    low_side, upper_core = my_chip() <= LOW, my_core() == 0
    block = slice(3 * span, 3 * span + depth)
    sides = []
    for near, far in (cots[:2], cots[2:]):
        near, far = taken(near, block), taken(far, block)
        near, far = [jnp.where(upper_core, piece[:, :128], piece[:, 128:]) for piece in (near, far)]
        sides.append([jnp.where(low_side, near, far), jnp.where(low_side, far, near)])
    by_core = [[jnp.where(upper_core, a, b) for a, b in zip(*sides)], [jnp.where(upper_core, b, a) for a, b in zip(*sides)]]
    for m in range(2):
        parts = []
        for side in range(2):
            for i in range(2):
                for core in range(2):
                    start = (2 * m + i) * depth
                    parts.append(by_core[core][side][:, start : start + depth])
        d_rows[m] = jnp.concatenate(parts, axis=1)
    d_rows[2] = taken(cots[0], slice(3 * span + depth, None))


def by_xor(array, by, chips):
    return lax.ppermute(array, "tok", [(2 * a + core, 2 * (a ^ by) + core) for a in chips for core in range(2)])


def exchanged(array):
    size = lax.axis_size("tok")
    gathered = [array]
    for bits in (2 * (LOW ^ HIGH_CHIP), 2 * (LOW ^ HIGH_CHIP) + 1, 1):
        gathered.append(lax.ppermute(array, "tok", [(j, j ^ bits) for j in range(size)]))
    return gathered


def both_cores(pieces):
    swapped = [core_swap(pieces[0])]
    for piece in pieces[1:]:
        swapped.append(core_swap(piece))
    return pieces + swapped


def hops(arrays, near, far, across):
    first = by_xor(arrays[1], 1, near)
    second = by_xor(arrays[2], 2, far)
    third = by_xor(arrays[3], 3, across)
    return first, second, third


ALL, MIDDLE, OUTER = tuple(range(CHIPS)), (LOW, HIGH_CHIP), (0, CHIPS - 1)


def to_chain(arrays):
    return both_cores([arrays[0], *hops(arrays, ALL, OUTER, MIDDLE)])


def from_chain(arrays):
    near, far, across = hops(arrays, ALL, MIDDLE, MIDDLE)
    return both_cores([arrays[0], near, across, far])


def from_chain_relayed(array):
    near = by_xor(array, 1, ALL)
    across = by_xor(array, 3, MIDDLE)
    far = by_xor(across, 1, ALL)
    return both_cores([array, near, across, far])


def to_earlier(array):
    groups = lax.axis_size("block")
    return lax.ppermute(array, "block", [(i, (i - 1) % groups) for i in range(groups)])


def to_later(array):
    groups = lax.axis_size("block")
    return lax.ppermute(array, "block", [(i, (i + 1) % groups) for i in range(groups)])


def per_device(queries, keys, values, rates, states, out_cot, final_cot):
    groups, size = lax.axis_size("block"), lax.axis_size("tok")
    depth, width = keys.shape
    own_rows = states[0]
    rows = own_rows.shape[1]
    if not (size == 2 * CHIPS and 4 * rows == 128 and depth == 128 and width == 8 * rows):
        return per_device_general(queries, keys, values, rates, states, out_cot, final_cot)
    span, tokens = 2 * rows, depth * size
    rates_row = rates.reshape(1, depth)
    state, square, wide = f32(3, span, width), f32(depth, width), f32(3 * span, width)
    sources = (keys, values, rates_row, own_rows, final_cot, queries, out_cot)
    longer, shorter = f32(2 * depth + 4 * rows, width), f32(2 * depth + 2 * rows, width)
    *packs, ahead = kernel_call(
        pack_body,
        [longer, longer, shorter, shorter, f32(2 * depth, width)],
        *sources,
        scratch=[pltpu.VMEM(array.shape, array.dtype) for array in sources] + [pltpu.SemaphoreType.DMA((len(sources),))],
        raw=True,
        limit=PACK_LIMIT,
    )
    pieces = to_chain(packs)
    ahead_pieces = to_chain([ahead] * CHIPS)
    half = bf16(tokens, width)
    own, last, *halved, kept, shifted, sums = kernel_call(
        forward_body,
        [state, state, half, half, half, half, f32(5, span, tokens), state, f32(8, width)],
        *pieces,
        scratch=[pltpu.VMEM((width, 4 * span), jnp.float32)],
    )
    all_sums = exchanged(sums)
    earlier = to_later(shifted)
    weights = from_chain_relayed(own.reshape(3 * span, width))

    inners, arrived = [], []
    common = [own, shifted, last, *all_sums]
    sent = [state, f32(8, width)]
    (raw,) = kernel_call(functools.partial(first_body, groups - 1), [state], *common, *halved, kept)
    for section in range(groups - 1):
        source = groups - 1 - section
        if section == 0:
            body = functools.partial(apply_body, source)
            applied, payload, partial = kernel_call(body, [wide] + sent, own, raw, earlier, *ahead_pieces)
        else:
            body = functools.partial(section_body, source)
            payload, partial = kernel_call(
                body, sent, *common, *inners[-4:], *arrived[-1:], *halved, kept, applied, earlier
            )
        straight = to_earlier(partial)
        arrived.append(to_earlier(payload))
        inners += exchanged(straight)
    received = [*common, *inners, *arrived]
    long, short = f32(4 * span, width), f32(3 * span + rows, width)
    ends = kernel_call(
        functools.partial(final_body, groups - 1),
        [long, long, short, short],
        *received,
        *halved,
        kept,
        applied,
        scratch=[pltpu.VMEM((width, 128), jnp.float32)],
    )
    cots = from_chain(ends)
    (d_queries,) = kernel_call(query_body, [square], queries, out_cot, *weights, spill=True)
    d_keys, d_values, d_rates, d_rows = kernel_call(
        token_body,
        [square, square, f32(1, depth), f32(3, rows, width)],
        keys,
        values,
        rates_row,
        *weights,
        *cots,
        spill=True,
    )
    return (d_queries, d_keys, d_values, d_rates.reshape(depth), d_rows[None])


def solution(mesh):
    return jax.shard_map(
        per_device,
        mesh=mesh,
        in_specs=(
            P(("block", "tok"), None),
            P(("block", "tok"), None),
            P(("block", "tok"), None),
            P(("block", "tok")),
            P("block", None, "tok", None),
            P(("block", "tok"), None),
            P(None, "tok", None),
        ),
        out_specs=(
            P(("block", "tok"), None),
            P(("block", "tok"), None),
            P(("block", "tok"), None),
            P(("block", "tok")),
            P("block", None, "tok", None),
        ),
        check_vma=False,
    )
```

```python
import functools

import jax
import jax.numpy as jnp
from jax import lax
from jax.experimental import pallas as pl
from jax.experimental.pallas import tpu as pltpu
from jax.sharding import PartitionSpec as P


EPS = 1e-06
HIGH = lax.Precision.HIGHEST


def mm(left, right):
    return lax.dot_general(left, right, (((1,), (0,)), ((), ())), precision=HIGH, preferred_element_type=jnp.float32)


def mm_nt(left, right):
    return lax.dot_general(left, right, (((1,), (1,)), ((), ())), precision=HIGH, preferred_element_type=jnp.float32)


def mm_tn(left, right):
    return lax.dot_general(left, right, (((0,), (0,)), ((), ())), precision=HIGH, preferred_element_type=jnp.float32)


def silu_parts(first):
    sig = 1.0 / (1.0 + jnp.exp(-first))
    slope = sig * (1.0 - sig)
    value = first * sig
    d_one = sig + first * slope
    d_two = slope * (2.0 + first * (1.0 - 2.0 * sig))
    return value, d_one, d_two


def direct(size):
    return size % 2 == 0 and size <= 16


def chip_shift(array, by):
    size = lax.axis_size("tok")
    return lax.ppermute(array, "tok", [(j, (j + 2 * by) % size) for j in range(size)])


def core_swap(array):
    size = lax.axis_size("tok")
    return lax.ppermute(array, "tok", [(j, j ^ 1) for j in range(size)])


def gather_pieces(array):
    size = lax.axis_size("tok")
    if not direct(size):
        return lax.all_gather(array, "tok")
    mine = jnp.stack([array] + [chip_shift(array, by) for by in range(1, size // 2)])
    return jnp.concatenate([mine, core_swap(mine)])


def spread_sum(pieces):
    size = lax.axis_size("tok")
    if not direct(size):
        return lax.psum_scatter(pieces, "tok")
    half = size // 2
    mine = pieces[:half] + core_swap(pieces[half:])
    total = mine[0]
    for by in range(1, half):
        total = total + chip_shift(mine[by], -by)
    return total


def sum_all(array):
    size = lax.axis_size("tok")
    if not direct(size):
        return jnp.sum(lax.all_gather(array, "tok"), axis=0)
    array = array + core_swap(array)
    total = array
    for by in range(1, size // 2):
        total = total + chip_shift(array, by)
    return total


def rows_to_hidden(rows):
    size = lax.axis_size("tok")
    count, depth, width = rows.shape
    parts = rows.reshape(count, depth, size, width // size).transpose(2, 0, 3, 1)
    parts = lax.all_to_all(parts, "tok", 0, 0)
    return parts.transpose(1, 2, 0, 3).reshape(count, width // size, depth * size)


def hidden_to_rows(slices):
    size = lax.axis_size("tok")
    count, depth, width = slices.shape
    parts = slices.reshape(count, depth, size, width // size).transpose(2, 0, 1, 3)
    parts = lax.all_to_all(parts, "tok", 0, 0)
    return parts.transpose(1, 3, 0, 2).reshape(count, width // size, depth * size)


def to_block(array, source, target, by=0):
    size = lax.axis_size("tok")
    pairs = [(source * size + j, target * size + (j + by) % size) for j in range(size)]
    return lax.ppermute(array, ("block", "tok"), pairs)


def up_one(array):
    groups = lax.axis_size("block")
    return lax.ppermute(array, "block", [(i, i + 1) for i in range(groups - 1)])


def slice_forward(weights, keys, scaled):
    first, gate = mm_nt(weights[0], keys), mm_nt(weights[1], keys)
    value, d_one, d_two = silu_parts(first)
    d_mixed = mm_nt(weights[2], scaled)
    mixed = value * gate
    d_gate = d_mixed * value
    d_first = d_mixed * gate * d_one
    grads = jnp.stack([mm(d_first, keys), mm(d_gate, keys), mm(mixed, scaled)])
    return grads, (gate, value, d_one, d_two, d_mixed)


def slice_adjoint(cot, kept, keys, scaled):
    gate, value, d_one, d_two, d_mixed = kept
    t_first, t_gate, p_mixed = mm_nt(cot[0], keys), mm_nt(cot[1], keys), mm_nt(cot[2], scaled)
    t_mixed = d_one * t_first * gate + value * t_gate
    c_gate = p_mixed * value + d_mixed * d_one * t_first
    c_first = p_mixed * gate * d_one + d_mixed * (d_two * t_first * gate + d_one * t_gate)
    return jnp.stack([mm(c_first, keys), mm(c_gate, keys), mm(t_mixed, scaled)])


def query_adjoint(weights, queries, out_cot):
    first, gate = mm_nt(queries, weights[0]), mm_nt(queries, weights[1])
    value, d_one, _ = silu_parts(first)
    d_mixed = mm_nt(out_cot, weights[2])
    d_gate = d_mixed * value
    d_first = d_mixed * gate * d_one
    d_queries = mm(d_first, weights[0]) + mm(d_gate, weights[1])
    d_weights = jnp.stack([mm_tn(d_first, queries), mm_tn(d_gate, queries), mm_tn(value * gate, out_cot)])
    return d_queries, d_weights


def token_adjoint(weights, cot, keys, scaled):
    first, gate = mm_nt(keys, weights[0]), mm_nt(keys, weights[1])
    value, d_one, d_two = silu_parts(first)
    d_mixed = mm_nt(scaled, weights[2])
    mixed = value * gate
    d_gate = d_mixed * value
    d_first = d_mixed * gate * d_one
    t_first, t_gate, p_mixed = mm_nt(keys, cot[0]), mm_nt(keys, cot[1]), mm_nt(scaled, cot[2])
    t_mixed = d_one * t_first * gate + value * t_gate
    c_gate = p_mixed * value + d_mixed * d_one * t_first
    c_first = p_mixed * gate * d_one + d_mixed * (d_two * t_first * gate + d_one * t_gate)
    d_keys = mm(c_first, weights[0]) + mm(c_gate, weights[1]) + mm(d_first, cot[0]) + mm(d_gate, cot[1])
    t_out = mm(t_mixed, weights[2]) + mm(mixed, cot[2])
    return d_keys, t_out


def over_hidden(array):
    return jnp.sum(array[:2], axis=1)


def per_device_general(queries, keys, values, rates, states, out_cot, final_cot):
    groups, size = lax.axis_size("block"), lax.axis_size("tok")
    position = lax.axis_index("block")
    own_rows = states[0]
    scaled = -rates[:, None] * values
    both = gather_pieces(jnp.stack([keys, scaled]))
    width = keys.shape[1]
    all_keys = both[:, 0].reshape(-1, width)
    all_scaled = both[:, 1].reshape(-1, width)
    split = rows_to_hidden(jnp.concatenate([own_rows[:2], final_cot[:2]]))
    own = jnp.concatenate([split[:2], own_rows[2:]])
    last = jnp.concatenate([split[2:], final_cot[2:]])
    grads, kept = slice_forward(own, all_keys, all_scaled)
    shifted = own - grads
    earlier = up_one(shifted[:2])
    sums = sum_all(jnp.concatenate([over_hidden(own * own), over_hidden(shifted * shifted), over_hidden(last * shifted)]))
    row_norm = [jnp.sqrt(sums[0:2, None, :] + EPS), jnp.sqrt(jnp.sum(own[2:] ** 2, axis=-1, keepdims=True) + EPS)]
    new_norm = [jnp.sqrt(sums[2:4, None, :] + EPS), jnp.sqrt(jnp.sum(shifted[2:] ** 2, axis=-1, keepdims=True) + EPS)]

    pieces = gather_pieces(own)
    whole = pieces.transpose(1, 0, 2, 3).reshape(3, -1, width)
    d_queries, d_weights = query_adjoint(whole, queries, out_cot)
    apply_state = spread_sum(d_weights.reshape(3, size, -1, width).transpose(1, 0, 2, 3))

    is_last = position == groups - 1
    incoming = jnp.where(is_last, last, 0.0)
    inner = jnp.where(is_last, sums[4:6], 0.0)
    for section in range(groups):
        inners = [inner[:, None, :], jnp.sum(incoming[2:] * shifted[2:], axis=-1, keepdims=True)]
        cots, straights = [], []
        for part, dot, old, new in zip((slice(0, 2), slice(2, 3)), inners, row_norm, new_norm):
            d_shifted = old / new * incoming[part] - old * dot / (new * new * new) * shifted[part]
            cots.append(-d_shifted)
            straights.append(d_shifted + dot / new * own[part] / old)
        cot = jnp.concatenate(cots)
        straight = jnp.concatenate(straights)
        rows_now = slice_adjoint(cot, kept, all_keys, all_scaled) + apply_state + straight
        if section + 1 < groups:
            source = groups - 1 - section
            partial = over_hidden(rows_now[:2] * earlier)
            incoming = incoming + to_block(rows_now, source, source - 1)
            if direct(size):
                for by in range(size):
                    inner = inner + to_block(partial, source, source - 1, by)
            else:
                inner = inner + to_block(sum_all(partial), source, source - 1)
    cot_pieces = gather_pieces(cot)
    whole_cot = cot_pieces.transpose(1, 0, 2, 3).reshape(3, -1, width)
    d_keys, t_out = token_adjoint(whole, whole_cot, keys, scaled)
    d_values = -rates[:, None] * t_out
    d_rates = -jnp.sum(values * t_out, axis=-1)
    d_rows = jnp.concatenate([hidden_to_rows(rows_now[:2]), rows_now[2:]])
    return (d_queries, d_keys, d_values, d_rates, d_rows[None])


def halves(array):
    upper = array.astype(jnp.bfloat16)
    return upper, (array - upper.astype(jnp.float32)).astype(jnp.bfloat16)


def product(left, right, contract):
    def one(a, b):
        return lax.dot_general(a, b, (((1,), (contract,)), ((), ())), preferred_element_type=jnp.float32)

    return one(left[0], right[0]) + (one(left[0], right[1]) + one(left[1], right[0]))


def nn(left, right):
    return product(left, right, 0)


def nt(left, right):
    return product(left, right, 1)


def kernel_call(body, outs, *operands, scratch=(), raw=False, spill=False, limit=24 * 1024 * 1024):
    space = pltpu.MemorySpace.HBM if raw else pltpu.VMEM
    return pl.pallas_call(
        body,
        in_specs=[pl.BlockSpec(memory_space=space) for _ in operands],
        out_specs=[pl.BlockSpec(memory_space=pltpu.VMEM) for _ in outs],
        out_shape=[(jax.ShapeDtypeStruct if spill else pltpu.VMEM)(shape, dtype) for shape, dtype in outs],
        scratch_shapes=list(scratch),
        compiler_params=pltpu.CompilerParams(vmem_limit_bytes=limit),
    )(*operands)


def my_chip():
    return lax.div(lax.axis_index("tok"), 2)


def my_core():
    return lax.rem(lax.axis_index("tok"), 2)


def in_chain():
    return (my_chip() == LOW) | (my_chip() == HIGH_CHIP)


def f32(*shape):
    return shape, jnp.float32


def bf16(*shape):
    return shape, jnp.bfloat16


def column(row, width):
    block = jnp.broadcast_to(row, (128, row.shape[1])).T
    return jnp.concatenate([block] * (width // 128), axis=1)


CHIPS = 4
LOW, HIGH_CHIP = 1, 2
CHUNK = 256
PACK_LIMIT = 61 * 1024 * 1024


def rows_at(start, count):
    return pl.ds(pl.multiple_of(start, count), count)


def pack_body(*refs):
    count = 7
    sources, outs = refs[:count], refs[count : count + CHIPS + 1]
    buffers, sems = refs[count + CHIPS + 1 : -1], refs[-1]
    copies = [pltpu.make_async_copy(a, b, sems.at[i]) for i, (a, b) in enumerate(zip(sources, buffers))]
    for copy in copies:
        copy.start()
    for copy in copies:
        copy.wait()
    keys, values, rates, rows, final, queries, cot = buffers
    packs, ahead = outs[:CHIPS], outs[CHIPS]
    tokens = keys.shape[0]
    depth = rows.shape[1]
    scaled = -column(rates[...], values.shape[1]) * values[...]
    sides = []
    for side in range(2):
        parts = []
        for core in range(2):
            lanes = []
            for source in (rows, final):
                for m in range(2):
                    for i in range(2):
                        start = (4 * side + 2 * i + core) * depth
                        lanes.append(source[m, :, start : start + depth])
            parts.append(jnp.concatenate(lanes, axis=1))
        sides.append(jnp.concatenate(parts))
    for by, pack in enumerate(packs):
        pack[:tokens] = keys[...]
        pack[tokens : 2 * tokens] = scaled
        low = jnp.bitwise_xor(my_chip(), by) == LOW
        pack[2 * tokens : 2 * tokens + 2 * depth] = jnp.where(low, sides[0], sides[1])
        if by < 2:
            pack[2 * tokens + 2 * depth : 2 * tokens + 3 * depth] = rows[2]
            pack[2 * tokens + 3 * depth :] = final[2]
    ahead[:tokens] = queries[...]
    ahead[tokens:] = cot[...]


def unpack(packs, mates, own, last, table):
    depth = own.shape[1] // 2
    base = packs[0].shape[0] - 4 * depth
    span = own.shape[1]
    chip, core = my_chip(), my_core()
    for by in range(CHIPS):
        source = jnp.bitwise_xor(chip, by)
        mine = rows_at(base + core * depth, depth)
        table[rows_at((2 * source + core) * depth, depth), :] = packs[by][mine, :]
        table[rows_at((2 * source + 1 - core) * depth, depth), :] = mates[by][mine, :]
    turned = table[...].T
    keep = jnp.where(lax.axis_index("block") == lax.axis_size("block") - 1, 1.0, 0.0)
    own[0], own[1] = turned[:span], turned[span : 2 * span]
    last[0], last[1] = turned[2 * span : 3 * span] * keep, turned[3 * span :] * keep
    low = chip == LOW
    for place, out, scale in ((2 * depth, own, 1.0), (3 * depth, last, keep)):
        cut = slice(base + place, base + place + depth)
        out[2, :depth] = jnp.where(low, packs[1][cut, :], packs[0][cut, :]) * scale
        out[2, depth:] = jnp.where(low, packs[0][cut, :], packs[1][cut, :]) * scale


def forward_body(*refs):
    packs, mates = refs[:CHIPS], refs[CHIPS : 2 * CHIPS]
    own, last, key_high, key_low, scaled_high, scaled_low, kept, shifted, sums, table = refs[2 * CHIPS :]
    pieces = packs + mates
    depth = key_high.shape[0] // len(pieces)
    span = own.shape[1]

    @pl.when(~in_chain())
    def _():
        for out in (own, shifted, sums):
            out[...] = jnp.zeros(out.shape, jnp.float32)

    @pl.when(in_chain())
    def _():
        unpack(packs, mates, own, last, table)
        for index, piece in enumerate(pieces):
            cut = slice(index * depth, (index + 1) * depth)
            key_high[cut, :], key_low[cut, :] = halves(piece[:depth, :])
            scaled_high[cut, :], scaled_low[cut, :] = halves(piece[depth : 2 * depth, :])
        pair = halves(jnp.concatenate([own[0], own[1]]))
        second = halves(own[2])
        grad_pair, grad_second = 0.0, 0.0
        for start in range(0, key_high.shape[0], CHUNK):
            cut = slice(start, start + CHUNK)
            key_cut = key_high[cut, :], key_low[cut, :]
            scaled_cut = scaled_high[cut, :], scaled_low[cut, :]
            both = nt(pair, key_cut)
            d_mixed = nt(second, scaled_cut)
            first, gate = both[:span], both[span:]
            value, d_one, d_two = silu_parts(first)
            for place, array in enumerate((gate, value, d_one, d_two, d_mixed)):
                kept[place, :, cut] = array
            d_pair = jnp.concatenate([d_mixed * gate * d_one, d_mixed * value])
            grad_pair += nn(halves(d_pair), key_cut)
            grad_second += nn(halves(value * gate), scaled_cut)
        moved = own[0] - grad_pair[:span], own[1] - grad_pair[span:], own[2] - grad_second
        rows = []
        for left, right in ((own, own), (moved, moved), (last, moved)):
            rows += [jnp.sum(left[m] * right[m], axis=0, keepdims=True) for m in range(2)]
        sums[...] = jnp.concatenate(rows + [jnp.zeros((2, own.shape[2]), jnp.float32)])
        for m in range(3):
            shifted[m] = moved[m]


def apply_body(source, own, raw, earlier, *refs):
    pieces, (applied, payload, partial) = refs[:-3], refs[-3:]
    span = own.shape[1]
    depth = pieces[0].shape[0] // 2
    active = (lax.axis_index("block") == source) & in_chain()

    @pl.when(~active)
    def _():
        payload[...] = jnp.zeros(payload.shape, jnp.float32)
        partial[...] = jnp.zeros(partial.shape, jnp.float32)

    @pl.when(in_chain())
    def _():
        pair = halves(jnp.concatenate([own[0], own[1]]))
        second = halves(own[2])
        out_pair, out_second = 0.0, 0.0
        for index in range(0, len(pieces), 2):
            one, two = pieces[index], pieces[index + 1]
            query = halves(jnp.concatenate([one[:depth, :], two[:depth, :]]))
            cot = halves(jnp.concatenate([one[depth:, :], two[depth:, :]]))
            both = nt(pair, query)
            d_mixed = nt(second, cot)
            first, gate = both[:span], both[span:]
            value, d_one, _ = silu_parts(first)
            out_pair += nn(halves(jnp.concatenate([d_mixed * gate * d_one, d_mixed * value])), query)
            out_second += nn(halves(value * gate), cot)
        applied[: 2 * span] = out_pair
        applied[2 * span :] = out_second

    @pl.when(active)
    def _():
        rows = [raw[m] + applied[m * span : (m + 1) * span, :] for m in range(3)]
        finish(rows, earlier, payload, partial)


def finish(rows, earlier, payload, partial):
    sums = [jnp.sum(rows[m] * earlier[m], axis=0, keepdims=True) for m in range(2)]
    partial[...] = jnp.concatenate(sums + [jnp.zeros((6, rows[0].shape[1]), jnp.float32)])
    for m in range(3):
        payload[m] = rows[m]


def state_terms(own, shifted, last, sums, inners, arrived):
    total = sums[0][...] + sums[1][...] + (sums[2][...] + sums[3][...])
    inner = total[4:6]
    for array in inners:
        inner = inner + array[0:2]
    cots, straights = [], []
    for m in range(3):
        incoming = last[m]
        for array in arrived:
            incoming = incoming + array[m]
        if m < 2:
            dot, old, new = inner[m : m + 1], jnp.sqrt(total[m : m + 1] + EPS), jnp.sqrt(total[m + 2 : m + 3] + EPS)
        else:
            dot = jnp.sum(incoming * shifted[m], axis=-1, keepdims=True)
            old = jnp.sqrt(jnp.sum(own[m] * own[m], axis=-1, keepdims=True) + EPS)
            new = jnp.sqrt(jnp.sum(shifted[m] * shifted[m], axis=-1, keepdims=True) + EPS)
        d_shifted = old / new * incoming - old * dot / (new * new * new) * shifted[m]
        cots.append(-d_shifted)
        straights.append(d_shifted + dot / new * own[m] / old)
    return cots, straights


def section_rows(count, refs):
    own, shifted, last = refs[:3]
    sums, inners, arrived = refs[3:7], refs[7 : 7 + 4 * count], refs[7 + 4 * count : 7 + 5 * count]
    key_high, key_low, scaled_high, scaled_low, kept = refs[7 + 5 * count : 12 + 5 * count]
    span = own.shape[1]
    cots, straights = state_terms(own, shifted, last, sums, inners, arrived)
    pair = halves(jnp.concatenate(cots[:2]))
    second = halves(cots[2])
    d_pair, d_second = 0.0, 0.0
    for start in range(0, key_high.shape[0], CHUNK):
        cut = slice(start, start + CHUNK)
        key_cut = key_high[cut, :], key_low[cut, :]
        scaled_cut = scaled_high[cut, :], scaled_low[cut, :]
        gate, value, d_one, d_two, d_mixed = [kept[place, :, cut] for place in range(5)]
        both = nt(pair, key_cut)
        p_mixed = nt(second, scaled_cut)
        t_first, t_gate = both[:span], both[span:]
        lift = d_one * t_first
        t_mixed = lift * gate + value * t_gate
        c_gate = p_mixed * value + d_mixed * lift
        c_first = p_mixed * gate * d_one + d_mixed * (d_two * t_first * gate + d_one * t_gate)
        d_pair += nn(halves(jnp.concatenate([c_first, c_gate])), key_cut)
        d_second += nn(halves(t_mixed), scaled_cut)
    return cots, [d_pair[:span] + straights[0], d_pair[span:] + straights[1], d_second + straights[2]]


def first_body(source, *refs):
    raw = refs[-1]

    @pl.when((lax.axis_index("block") == source) & in_chain())
    def _():
        _, rows = section_rows(0, refs)
        for m in range(3):
            raw[m] = rows[m]


def section_body(source, *refs):
    applied, earlier, payload, partial = refs[-4:]
    active = (lax.axis_index("block") == source) & in_chain()

    @pl.when(~active)
    def _():
        payload[...] = jnp.zeros(payload.shape, jnp.float32)
        partial[...] = jnp.zeros(partial.shape, jnp.float32)

    @pl.when(active)
    def _():
        span = payload.shape[1]
        _, rows = section_rows(1, refs)
        finish([row + applied[m * span : (m + 1) * span, :] for m, row in enumerate(rows)], earlier, payload, partial)


def final_body(count, *refs):
    applied, outs, table = refs[-6], refs[-5:-1], refs[-1]
    span = refs[0].shape[1]
    depth = span // 2
    chip = my_chip()

    @pl.when(~in_chain())
    def _():
        for out in outs:
            out[...] = jnp.zeros(out.shape, jnp.float32)

    @pl.when(in_chain())
    def _():
        cots, rows = section_rows(count, refs)
        for out in outs:
            for m in range(3):
                out[m * span : (m + 1) * span, :] = cots[m]
        rows = [row + applied[m * span : (m + 1) * span, :] for m, row in enumerate(rows)]
        table[...] = jnp.concatenate(rows[:2]).T
        for by, out in enumerate(outs):
            start = jnp.bitwise_xor(chip, by) * 2 * depth
            for core in range(2):
                lanes = slice(core * 128, (core + 1) * 128)
                out[3 * span : 3 * span + depth, lanes] = table[rows_at(start + core * depth, depth), :]
        low = chip == LOW
        upper, lower = rows[2][:depth], rows[2][depth:]
        outs[0][3 * span + depth :] = jnp.where(low, lower, upper)
        outs[1][3 * span + depth :] = jnp.where(low, upper, lower)


def joined(refs):
    return [[refs[i], refs[i + 1]] for i in range(0, 8, 2)]


def taken(pair, cut):
    return pair[0][cut, :] + pair[1][cut, :]


def load_halves(pieces, part, span):
    return halves(jnp.concatenate([taken(pair, slice(part * span, (part + 1) * span)) for pair in pieces]))


def query_body(queries, out_cot, *refs):
    pieces, d_queries = joined(refs[:8]), refs[8]
    span = queries.shape[1] // len(pieces)
    one, three, two = [load_halves(pieces, part, span) for part in range(3)]
    query, cot = halves(queries[...]), halves(out_cot[...])
    first, gate = nt(query, one), nt(query, three)
    value, d_one, _ = silu_parts(first)
    d_mixed = nt(cot, two)
    d_gate = d_mixed * value
    d_first = d_mixed * gate * d_one
    d_queries[...] = nn(halves(d_first), one) + nn(halves(d_gate), three)


def token_body(keys, values, rates, *refs):
    weights, cots = joined(refs[:8]), joined(refs[8:16])
    d_keys, d_values, d_rates, d_rows = refs[16:]
    width = keys.shape[1]
    span = width // len(weights)
    one, three, two = [load_halves(weights, part, span) for part in range(3)]
    c_one, c_three, c_two = [load_halves(cots, part, span) for part in range(3)]
    rate = column(rates[...], width)
    key, scaled = halves(keys[...]), halves(-rate * values[...])
    first, gate = nt(key, one), nt(key, three)
    value, d_one, d_two = silu_parts(first)
    d_mixed = nt(scaled, two)
    t_first, t_gate, p_mixed = nt(key, c_one), nt(key, c_three), nt(scaled, c_two)
    mixed = value * gate
    d_gate = d_mixed * value
    d_first = d_mixed * gate * d_one
    lift = d_one * t_first
    t_mixed = lift * gate + value * t_gate
    c_gate = p_mixed * value + d_mixed * lift
    c_first = p_mixed * gate * d_one + d_mixed * (d_two * t_first * gate + d_one * t_gate)
    d_keys[...] = nn(halves(c_first), one) + nn(halves(c_gate), three) + nn(halves(d_first), c_one) + nn(halves(d_gate), c_three)
    t_out = nn(halves(t_mixed), two) + nn(halves(mixed), c_two)
    d_values[...] = -rate * t_out
    d_rates[...] = -jnp.sum((values[...] * t_out).T, axis=0, keepdims=True)
    depth = d_rows.shape[1]
    low_side, upper_core = my_chip() <= LOW, my_core() == 0
    block = slice(3 * span, 3 * span + depth)
    sides = []
    for near, far in (cots[:2], cots[2:]):
        near, far = taken(near, block), taken(far, block)
        near, far = [jnp.where(upper_core, piece[:, :128], piece[:, 128:]) for piece in (near, far)]
        sides.append([jnp.where(low_side, near, far), jnp.where(low_side, far, near)])
    by_core = [[jnp.where(upper_core, a, b) for a, b in zip(*sides)], [jnp.where(upper_core, b, a) for a, b in zip(*sides)]]
    for m in range(2):
        parts = []
        for side in range(2):
            for i in range(2):
                for core in range(2):
                    start = (2 * m + i) * depth
                    parts.append(by_core[core][side][:, start : start + depth])
        d_rows[m] = jnp.concatenate(parts, axis=1)
    d_rows[2] = taken(cots[0], slice(3 * span + depth, None))


def over_chips(array, moves):
    pairs = [(2 * a + core, 2 * b + (core if a != b else 1 - core)) for a, b in enumerate(moves) for core in range(2)]
    return lax.ppermute(array, "tok", pairs)


def by_xor(array, by):
    return over_chips(array, [chip ^ by for chip in range(CHIPS)])


ACROSS = (0, 2, 1, 3)
INWARD = (2, 0, 3, 1)
OUTWARD = (1, 3, 0, 2)


def exchanged(array):
    turned = [(2 * a + core, 2 * b + 1 - core) for a, b in enumerate(ACROSS) for core in range(2)]
    return [array, over_chips(array, ACROSS), lax.ppermute(array, "tok", turned), core_swap(array)]


def both_cores(pieces):
    swapped = [core_swap(pieces[0])]
    for piece in pieces[1:]:
        swapped.append(core_swap(piece))
    return pieces + swapped


def hops(arrays, far):
    first = by_xor(arrays[1], 1)
    second = over_chips(arrays[2], far)
    third = over_chips(arrays[3], ACROSS)
    return first, second, third


def to_chain(arrays):
    return both_cores([arrays[0], *hops(arrays, INWARD)])


def from_chain(arrays):
    near, far, across = hops(arrays, OUTWARD)
    return both_cores([arrays[0], near, across, far])


def from_chain_relayed(array):
    near = by_xor(array, 1)
    across = over_chips(array, ACROSS)
    far = by_xor(across, 1)
    return both_cores([array, near, across, far])


def to_earlier(array):
    groups = lax.axis_size("block")
    return lax.ppermute(array, "block", [(i, (i - 1) % groups) for i in range(groups)])


def to_later(array):
    groups = lax.axis_size("block")
    return lax.ppermute(array, "block", [(i, (i + 1) % groups) for i in range(groups)])


def per_device(queries, keys, values, rates, states, out_cot, final_cot):
    groups, size = lax.axis_size("block"), lax.axis_size("tok")
    depth, width = keys.shape
    own_rows = states[0]
    rows = own_rows.shape[1]
    if not (size == 2 * CHIPS and 4 * rows == 128 and depth == 128 and width == 8 * rows):
        return per_device_general(queries, keys, values, rates, states, out_cot, final_cot)
    span, tokens = 2 * rows, depth * size
    rates_row = rates.reshape(1, depth)
    state, square, wide = f32(3, span, width), f32(depth, width), f32(3 * span, width)
    sources = (keys, values, rates_row, own_rows, final_cot, queries, out_cot)
    longer, shorter = f32(2 * depth + 4 * rows, width), f32(2 * depth + 2 * rows, width)
    *packs, ahead = kernel_call(
        pack_body,
        [longer, longer, shorter, shorter, f32(2 * depth, width)],
        *sources,
        scratch=[pltpu.VMEM(array.shape, array.dtype) for array in sources] + [pltpu.SemaphoreType.DMA((len(sources),))],
        raw=True,
        limit=PACK_LIMIT,
    )
    pieces = to_chain(packs)
    ahead_pieces = to_chain([ahead] * CHIPS)
    half = bf16(tokens, width)
    own, last, *halved, kept, shifted, sums = kernel_call(
        forward_body,
        [state, state, half, half, half, half, f32(5, span, tokens), state, f32(8, width)],
        *pieces,
        scratch=[pltpu.VMEM((width, 4 * span), jnp.float32)],
    )
    all_sums = exchanged(sums)
    earlier = to_later(shifted)
    weights = from_chain_relayed(own.reshape(3 * span, width))

    inners, arrived = [], []
    common = [own, shifted, last, *all_sums]
    sent = [state, f32(8, width)]
    (raw,) = kernel_call(functools.partial(first_body, groups - 1), [state], *common, *halved, kept)
    for section in range(groups - 1):
        source = groups - 1 - section
        if section == 0:
            body = functools.partial(apply_body, source)
            applied, payload, partial = kernel_call(body, [wide] + sent, own, raw, earlier, *ahead_pieces)
        else:
            body = functools.partial(section_body, source)
            payload, partial = kernel_call(
                body, sent, *common, *inners[-4:], *arrived[-1:], *halved, kept, applied, earlier
            )
        straight = to_earlier(partial)
        arrived.append(to_earlier(payload))
        inners += exchanged(straight)
    received = [*common, *inners, *arrived]
    long, short = f32(4 * span, width), f32(3 * span + rows, width)
    ends = kernel_call(
        functools.partial(final_body, groups - 1),
        [long, long, short, short],
        *received,
        *halved,
        kept,
        applied,
        scratch=[pltpu.VMEM((width, 128), jnp.float32)],
    )
    cots = from_chain(ends)
    (d_queries,) = kernel_call(query_body, [square], queries, out_cot, *weights, spill=True)
    d_keys, d_values, d_rates, d_rows = kernel_call(
        token_body,
        [square, square, f32(1, depth), f32(3, rows, width)],
        keys,
        values,
        rates_row,
        *weights,
        *cots,
        spill=True,
    )
    return (d_queries, d_keys, d_values, d_rates.reshape(depth), d_rows[None])


def solution(mesh):
    return jax.shard_map(
        per_device,
        mesh=mesh,
        in_specs=(
            P(("block", "tok"), None),
            P(("block", "tok"), None),
            P(("block", "tok"), None),
            P(("block", "tok")),
            P("block", None, "tok", None),
            P(("block", "tok"), None),
            P(None, "tok", None),
        ),
        out_specs=(
            P(("block", "tok"), None),
            P(("block", "tok"), None),
            P(("block", "tok"), None),
            P(("block", "tok")),
            P("block", None, "tok", None),
        ),
        check_vma=False,
    )
```

```python
import functools

import jax
import jax.numpy as jnp
from jax import lax
from jax.experimental import pallas as pl
from jax.experimental.pallas import tpu as pltpu
from jax.sharding import PartitionSpec as P


EPS = 1e-06
HIGH = lax.Precision.HIGHEST


def mm(left, right):
    return lax.dot_general(left, right, (((1,), (0,)), ((), ())), precision=HIGH, preferred_element_type=jnp.float32)


def mm_nt(left, right):
    return lax.dot_general(left, right, (((1,), (1,)), ((), ())), precision=HIGH, preferred_element_type=jnp.float32)


def mm_tn(left, right):
    return lax.dot_general(left, right, (((0,), (0,)), ((), ())), precision=HIGH, preferred_element_type=jnp.float32)


def silu_parts(first):
    sig = 1.0 / (1.0 + jnp.exp(-first))
    slope = sig * (1.0 - sig)
    value = first * sig
    d_one = sig + first * slope
    d_two = slope * (2.0 + first * (1.0 - 2.0 * sig))
    return value, d_one, d_two


def direct(size):
    return size % 2 == 0 and size <= 16


def chip_shift(array, by):
    size = lax.axis_size("tok")
    return lax.ppermute(array, "tok", [(j, (j + 2 * by) % size) for j in range(size)])


def core_swap(array):
    size = lax.axis_size("tok")
    return lax.ppermute(array, "tok", [(j, j ^ 1) for j in range(size)])


def gather_pieces(array):
    size = lax.axis_size("tok")
    if not direct(size):
        return lax.all_gather(array, "tok")
    mine = jnp.stack([array] + [chip_shift(array, by) for by in range(1, size // 2)])
    return jnp.concatenate([mine, core_swap(mine)])


def spread_sum(pieces):
    size = lax.axis_size("tok")
    if not direct(size):
        return lax.psum_scatter(pieces, "tok")
    half = size // 2
    mine = pieces[:half] + core_swap(pieces[half:])
    total = mine[0]
    for by in range(1, half):
        total = total + chip_shift(mine[by], -by)
    return total


def sum_all(array):
    size = lax.axis_size("tok")
    if not direct(size):
        return jnp.sum(lax.all_gather(array, "tok"), axis=0)
    array = array + core_swap(array)
    total = array
    for by in range(1, size // 2):
        total = total + chip_shift(array, by)
    return total


def rows_to_hidden(rows):
    size = lax.axis_size("tok")
    count, depth, width = rows.shape
    parts = rows.reshape(count, depth, size, width // size).transpose(2, 0, 3, 1)
    parts = lax.all_to_all(parts, "tok", 0, 0)
    return parts.transpose(1, 2, 0, 3).reshape(count, width // size, depth * size)


def hidden_to_rows(slices):
    size = lax.axis_size("tok")
    count, depth, width = slices.shape
    parts = slices.reshape(count, depth, size, width // size).transpose(2, 0, 1, 3)
    parts = lax.all_to_all(parts, "tok", 0, 0)
    return parts.transpose(1, 3, 0, 2).reshape(count, width // size, depth * size)


def to_block(array, source, target, by=0):
    size = lax.axis_size("tok")
    pairs = [(source * size + j, target * size + (j + by) % size) for j in range(size)]
    return lax.ppermute(array, ("block", "tok"), pairs)


def up_one(array):
    groups = lax.axis_size("block")
    return lax.ppermute(array, "block", [(i, i + 1) for i in range(groups - 1)])


def slice_forward(weights, keys, scaled):
    first, gate = mm_nt(weights[0], keys), mm_nt(weights[1], keys)
    value, d_one, d_two = silu_parts(first)
    d_mixed = mm_nt(weights[2], scaled)
    mixed = value * gate
    d_gate = d_mixed * value
    d_first = d_mixed * gate * d_one
    grads = jnp.stack([mm(d_first, keys), mm(d_gate, keys), mm(mixed, scaled)])
    return grads, (gate, value, d_one, d_two, d_mixed)


def slice_adjoint(cot, kept, keys, scaled):
    gate, value, d_one, d_two, d_mixed = kept
    t_first, t_gate, p_mixed = mm_nt(cot[0], keys), mm_nt(cot[1], keys), mm_nt(cot[2], scaled)
    t_mixed = d_one * t_first * gate + value * t_gate
    c_gate = p_mixed * value + d_mixed * d_one * t_first
    c_first = p_mixed * gate * d_one + d_mixed * (d_two * t_first * gate + d_one * t_gate)
    return jnp.stack([mm(c_first, keys), mm(c_gate, keys), mm(t_mixed, scaled)])


def query_adjoint(weights, queries, out_cot):
    first, gate = mm_nt(queries, weights[0]), mm_nt(queries, weights[1])
    value, d_one, _ = silu_parts(first)
    d_mixed = mm_nt(out_cot, weights[2])
    d_gate = d_mixed * value
    d_first = d_mixed * gate * d_one
    d_queries = mm(d_first, weights[0]) + mm(d_gate, weights[1])
    d_weights = jnp.stack([mm_tn(d_first, queries), mm_tn(d_gate, queries), mm_tn(value * gate, out_cot)])
    return d_queries, d_weights


def token_adjoint(weights, cot, keys, scaled):
    first, gate = mm_nt(keys, weights[0]), mm_nt(keys, weights[1])
    value, d_one, d_two = silu_parts(first)
    d_mixed = mm_nt(scaled, weights[2])
    mixed = value * gate
    d_gate = d_mixed * value
    d_first = d_mixed * gate * d_one
    t_first, t_gate, p_mixed = mm_nt(keys, cot[0]), mm_nt(keys, cot[1]), mm_nt(scaled, cot[2])
    t_mixed = d_one * t_first * gate + value * t_gate
    c_gate = p_mixed * value + d_mixed * d_one * t_first
    c_first = p_mixed * gate * d_one + d_mixed * (d_two * t_first * gate + d_one * t_gate)
    d_keys = mm(c_first, weights[0]) + mm(c_gate, weights[1]) + mm(d_first, cot[0]) + mm(d_gate, cot[1])
    t_out = mm(t_mixed, weights[2]) + mm(mixed, cot[2])
    return d_keys, t_out


def over_hidden(array):
    return jnp.sum(array[:2], axis=1)


def per_device_general(queries, keys, values, rates, states, out_cot, final_cot):
    groups, size = lax.axis_size("block"), lax.axis_size("tok")
    position = lax.axis_index("block")
    own_rows = states[0]
    scaled = -rates[:, None] * values
    both = gather_pieces(jnp.stack([keys, scaled]))
    width = keys.shape[1]
    all_keys = both[:, 0].reshape(-1, width)
    all_scaled = both[:, 1].reshape(-1, width)
    split = rows_to_hidden(jnp.concatenate([own_rows[:2], final_cot[:2]]))
    own = jnp.concatenate([split[:2], own_rows[2:]])
    last = jnp.concatenate([split[2:], final_cot[2:]])
    grads, kept = slice_forward(own, all_keys, all_scaled)
    shifted = own - grads
    earlier = up_one(shifted[:2])
    sums = sum_all(jnp.concatenate([over_hidden(own * own), over_hidden(shifted * shifted), over_hidden(last * shifted)]))
    row_norm = [jnp.sqrt(sums[0:2, None, :] + EPS), jnp.sqrt(jnp.sum(own[2:] ** 2, axis=-1, keepdims=True) + EPS)]
    new_norm = [jnp.sqrt(sums[2:4, None, :] + EPS), jnp.sqrt(jnp.sum(shifted[2:] ** 2, axis=-1, keepdims=True) + EPS)]

    pieces = gather_pieces(own)
    whole = pieces.transpose(1, 0, 2, 3).reshape(3, -1, width)
    d_queries, d_weights = query_adjoint(whole, queries, out_cot)
    apply_state = spread_sum(d_weights.reshape(3, size, -1, width).transpose(1, 0, 2, 3))

    is_last = position == groups - 1
    incoming = jnp.where(is_last, last, 0.0)
    inner = jnp.where(is_last, sums[4:6], 0.0)
    for section in range(groups):
        inners = [inner[:, None, :], jnp.sum(incoming[2:] * shifted[2:], axis=-1, keepdims=True)]
        cots, straights = [], []
        for part, dot, old, new in zip((slice(0, 2), slice(2, 3)), inners, row_norm, new_norm):
            d_shifted = old / new * incoming[part] - old * dot / (new * new * new) * shifted[part]
            cots.append(-d_shifted)
            straights.append(d_shifted + dot / new * own[part] / old)
        cot = jnp.concatenate(cots)
        straight = jnp.concatenate(straights)
        rows_now = slice_adjoint(cot, kept, all_keys, all_scaled) + apply_state + straight
        if section + 1 < groups:
            source = groups - 1 - section
            partial = over_hidden(rows_now[:2] * earlier)
            incoming = incoming + to_block(rows_now, source, source - 1)
            if direct(size):
                for by in range(size):
                    inner = inner + to_block(partial, source, source - 1, by)
            else:
                inner = inner + to_block(sum_all(partial), source, source - 1)
    cot_pieces = gather_pieces(cot)
    whole_cot = cot_pieces.transpose(1, 0, 2, 3).reshape(3, -1, width)
    d_keys, t_out = token_adjoint(whole, whole_cot, keys, scaled)
    d_values = -rates[:, None] * t_out
    d_rates = -jnp.sum(values * t_out, axis=-1)
    d_rows = jnp.concatenate([hidden_to_rows(rows_now[:2]), rows_now[2:]])
    return (d_queries, d_keys, d_values, d_rates, d_rows[None])


def halves(array):
    upper = array.astype(jnp.bfloat16)
    return upper, (array - upper.astype(jnp.float32)).astype(jnp.bfloat16)


def product(left, right, contract):
    def one(a, b):
        return lax.dot_general(a, b, (((1,), (contract,)), ((), ())), preferred_element_type=jnp.float32)

    return one(left[0], right[0]) + (one(left[0], right[1]) + one(left[1], right[0]))


def nn(left, right):
    return product(left, right, 0)


def nt(left, right):
    return product(left, right, 1)


def kernel_call(body, outs, *operands, scratch=(), raw=False, spill=False, limit=24 * 1024 * 1024):
    space = pltpu.MemorySpace.HBM if raw else pltpu.VMEM
    return pl.pallas_call(
        body,
        in_specs=[pl.BlockSpec(memory_space=space) for _ in operands],
        out_specs=[pl.BlockSpec(memory_space=pltpu.VMEM) for _ in outs],
        out_shape=[(jax.ShapeDtypeStruct if spill else pltpu.VMEM)(shape, dtype) for shape, dtype in outs],
        scratch_shapes=list(scratch),
        compiler_params=pltpu.CompilerParams(vmem_limit_bytes=limit),
    )(*operands)


def my_chip():
    return lax.div(lax.axis_index("tok"), 2)


def my_core():
    return lax.rem(lax.axis_index("tok"), 2)


def in_chain():
    return (my_chip() == LOW) | (my_chip() == HIGH_CHIP)


def f32(*shape):
    return shape, jnp.float32


def bf16(*shape):
    return shape, jnp.bfloat16


def column(row, width):
    block = jnp.broadcast_to(row, (128, row.shape[1])).T
    return jnp.concatenate([block] * (width // 128), axis=1)


CHIPS = 4
LOW, HIGH_CHIP = 1, 2
CHUNK = 256
PACK_LIMIT = 61 * 1024 * 1024


def rows_at(start, count):
    return pl.ds(pl.multiple_of(start, count), count)


def pack_body(*refs):
    count = 7
    sources, outs = refs[:count], refs[count : count + CHIPS + 1]
    buffers, sems = refs[count + CHIPS + 1 : -1], refs[-1]
    copies = [pltpu.make_async_copy(a, b, sems.at[i]) for i, (a, b) in enumerate(zip(sources, buffers))]
    for copy in copies:
        copy.start()
    for copy in copies:
        copy.wait()
    keys, values, rates, rows, final, queries, cot = buffers
    packs, ahead = outs[:CHIPS], outs[CHIPS]
    tokens = keys.shape[0]
    depth = rows.shape[1]
    scaled = -column(rates[...], values.shape[1]) * values[...]
    sides = []
    for side in range(2):
        parts = []
        for core in range(2):
            lanes = []
            for source in (rows, final):
                for m in range(2):
                    for i in range(2):
                        start = (4 * side + 2 * i + core) * depth
                        lanes.append(source[m, :, start : start + depth])
            parts.append(jnp.concatenate(lanes, axis=1))
        sides.append(jnp.concatenate(parts))
    for by, pack in enumerate(packs):
        pack[:tokens] = keys[...]
        pack[tokens : 2 * tokens] = scaled
        low = jnp.bitwise_xor(my_chip(), by) == LOW
        pack[2 * tokens : 2 * tokens + 2 * depth] = jnp.where(low, sides[0], sides[1])
        if by < 2:
            pack[2 * tokens + 2 * depth : 2 * tokens + 3 * depth] = rows[2]
            pack[2 * tokens + 3 * depth :] = final[2]
    ahead[:tokens] = queries[...]
    ahead[tokens:] = cot[...]


def unpack(packs, mates, own, last, table):
    depth = own.shape[1] // 2
    base = packs[0].shape[0] - 4 * depth
    span = own.shape[1]
    chip, core = my_chip(), my_core()
    for by in range(CHIPS):
        source = jnp.bitwise_xor(chip, by)
        mine = rows_at(base + core * depth, depth)
        table[rows_at((2 * source + core) * depth, depth), :] = packs[by][mine, :]
        table[rows_at((2 * source + 1 - core) * depth, depth), :] = mates[by][mine, :]
    turned = table[...].T
    keep = jnp.where(lax.axis_index("block") == lax.axis_size("block") - 1, 1.0, 0.0)
    own[0], own[1] = turned[:span], turned[span : 2 * span]
    last[0], last[1] = turned[2 * span : 3 * span] * keep, turned[3 * span :] * keep
    low = chip == LOW
    for place, out, scale in ((2 * depth, own, 1.0), (3 * depth, last, keep)):
        cut = slice(base + place, base + place + depth)
        out[2, :depth] = jnp.where(low, packs[1][cut, :], packs[0][cut, :]) * scale
        out[2, depth:] = jnp.where(low, packs[0][cut, :], packs[1][cut, :]) * scale


def forward_body(*refs):
    packs, mates = refs[:CHIPS], refs[CHIPS : 2 * CHIPS]
    own, last, key_high, key_low, scaled_high, scaled_low, kept, shifted, sums, table = refs[2 * CHIPS :]
    pieces = packs + mates
    depth = key_high.shape[0] // len(pieces)
    span = own.shape[1]

    @pl.when(~in_chain())
    def _():
        for out in (own, shifted, sums):
            out[...] = jnp.zeros(out.shape, jnp.float32)

    @pl.when(in_chain())
    def _():
        unpack(packs, mates, own, last, table)
        for index, piece in enumerate(pieces):
            cut = slice(index * depth, (index + 1) * depth)
            key_high[cut, :], key_low[cut, :] = halves(piece[:depth, :])
            scaled_high[cut, :], scaled_low[cut, :] = halves(piece[depth : 2 * depth, :])
        pair = halves(jnp.concatenate([own[0], own[1]]))
        second = halves(own[2])
        grad_pair, grad_second = 0.0, 0.0
        for start in range(0, key_high.shape[0], CHUNK):
            cut = slice(start, start + CHUNK)
            key_cut = key_high[cut, :], key_low[cut, :]
            scaled_cut = scaled_high[cut, :], scaled_low[cut, :]
            both = nt(pair, key_cut)
            d_mixed = nt(second, scaled_cut)
            first, gate = both[:span], both[span:]
            value, d_one, d_two = silu_parts(first)
            for place, array in enumerate((gate, value, d_one, d_two, d_mixed)):
                kept[place, :, cut] = array
            d_pair = jnp.concatenate([d_mixed * gate * d_one, d_mixed * value])
            grad_pair += nn(halves(d_pair), key_cut)
            grad_second += nn(halves(value * gate), scaled_cut)
        moved = own[0] - grad_pair[:span], own[1] - grad_pair[span:], own[2] - grad_second
        rows = []
        for left, right in ((own, own), (moved, moved), (last, moved)):
            rows += [jnp.sum(left[m] * right[m], axis=0, keepdims=True) for m in range(2)]
        sums[...] = jnp.concatenate(rows + [jnp.zeros((2, own.shape[2]), jnp.float32)])
        for m in range(3):
            shifted[m] = moved[m]


def apply_body(source, own, raw, earlier, *refs):
    pieces, (applied, payload, partial) = refs[:-3], refs[-3:]
    span = own.shape[1]
    depth = pieces[0].shape[0] // 2
    active = (lax.axis_index("block") == source) & in_chain()

    @pl.when(~active)
    def _():
        payload[...] = jnp.zeros(payload.shape, jnp.float32)
        partial[...] = jnp.zeros(partial.shape, jnp.float32)

    @pl.when(in_chain())
    def _():
        pair = halves(jnp.concatenate([own[0], own[1]]))
        second = halves(own[2])
        out_pair, out_second = 0.0, 0.0
        for index in range(0, len(pieces), 2):
            one, two = pieces[index], pieces[index + 1]
            query = halves(jnp.concatenate([one[:depth, :], two[:depth, :]]))
            cot = halves(jnp.concatenate([one[depth:, :], two[depth:, :]]))
            both = nt(pair, query)
            d_mixed = nt(second, cot)
            first, gate = both[:span], both[span:]
            value, d_one, _ = silu_parts(first)
            out_pair += nn(halves(jnp.concatenate([d_mixed * gate * d_one, d_mixed * value])), query)
            out_second += nn(halves(value * gate), cot)
        applied[: 2 * span] = out_pair
        applied[2 * span :] = out_second

    @pl.when(active)
    def _():
        rows = [raw[m] + applied[m * span : (m + 1) * span, :] for m in range(3)]
        finish(rows, earlier, payload, partial)


def finish(rows, earlier, payload, partial):
    sums = [jnp.sum(rows[m] * earlier[m], axis=0, keepdims=True) for m in range(2)]
    partial[...] = jnp.concatenate(sums + [jnp.zeros((6, rows[0].shape[1]), jnp.float32)])
    for m in range(3):
        payload[m] = rows[m]


def state_terms(own, shifted, last, sums, inners, arrived):
    total = sums[0][...] + sums[1][...] + (sums[2][...] + sums[3][...])
    inner = total[4:6]
    for array in inners:
        inner = inner + array[0:2]
    cots, straights = [], []
    for m in range(3):
        incoming = last[m]
        for array in arrived:
            incoming = incoming + array[m]
        if m < 2:
            dot, old, new = inner[m : m + 1], jnp.sqrt(total[m : m + 1] + EPS), jnp.sqrt(total[m + 2 : m + 3] + EPS)
        else:
            dot = jnp.sum(incoming * shifted[m], axis=-1, keepdims=True)
            old = jnp.sqrt(jnp.sum(own[m] * own[m], axis=-1, keepdims=True) + EPS)
            new = jnp.sqrt(jnp.sum(shifted[m] * shifted[m], axis=-1, keepdims=True) + EPS)
        d_shifted = old / new * incoming - old * dot / (new * new * new) * shifted[m]
        cots.append(-d_shifted)
        straights.append(d_shifted + dot / new * own[m] / old)
    return cots, straights


def section_rows(count, refs):
    own, shifted, last = refs[:3]
    sums, inners, arrived = refs[3:7], refs[7 : 7 + 4 * count], refs[7 + 4 * count : 7 + 5 * count]
    key_high, key_low, scaled_high, scaled_low, kept = refs[7 + 5 * count : 12 + 5 * count]
    span = own.shape[1]
    cots, straights = state_terms(own, shifted, last, sums, inners, arrived)
    pair = halves(jnp.concatenate(cots[:2]))
    second = halves(cots[2])
    d_pair, d_second = 0.0, 0.0
    for start in range(0, key_high.shape[0], CHUNK):
        cut = slice(start, start + CHUNK)
        key_cut = key_high[cut, :], key_low[cut, :]
        scaled_cut = scaled_high[cut, :], scaled_low[cut, :]
        gate, value, d_one, d_two, d_mixed = [kept[place, :, cut] for place in range(5)]
        both = nt(pair, key_cut)
        p_mixed = nt(second, scaled_cut)
        t_first, t_gate = both[:span], both[span:]
        lift = d_one * t_first
        t_mixed = lift * gate + value * t_gate
        c_gate = p_mixed * value + d_mixed * lift
        c_first = p_mixed * gate * d_one + d_mixed * (d_two * t_first * gate + d_one * t_gate)
        d_pair += nn(halves(jnp.concatenate([c_first, c_gate])), key_cut)
        d_second += nn(halves(t_mixed), scaled_cut)
    return cots, [d_pair[:span] + straights[0], d_pair[span:] + straights[1], d_second + straights[2]]


def first_body(source, *refs):
    raw = refs[-1]

    @pl.when((lax.axis_index("block") == source) & in_chain())
    def _():
        _, rows = section_rows(0, refs)
        for m in range(3):
            raw[m] = rows[m]


def section_body(source, *refs):
    applied, earlier, payload, partial = refs[-4:]
    active = (lax.axis_index("block") == source) & in_chain()

    @pl.when(~active)
    def _():
        payload[...] = jnp.zeros(payload.shape, jnp.float32)
        partial[...] = jnp.zeros(partial.shape, jnp.float32)

    @pl.when(active)
    def _():
        span = payload.shape[1]
        _, rows = section_rows(1, refs)
        finish([row + applied[m * span : (m + 1) * span, :] for m, row in enumerate(rows)], earlier, payload, partial)


def terms_body(count, *refs):
    cot = refs[-1]
    span = refs[0].shape[1]

    @pl.when(~in_chain())
    def _():
        cot[...] = jnp.zeros(cot.shape, jnp.float32)

    @pl.when(in_chain())
    def _():
        cots, _ = state_terms(*refs[:3], refs[3:7], refs[7 : 7 + 4 * count], refs[7 + 4 * count : 7 + 5 * count])
        for m in range(3):
            cot[m * span : (m + 1) * span, :] = cots[m]


def final_body(count, *refs):
    applied, outs, table = refs[-6], refs[-5:-1], refs[-1]
    span = refs[0].shape[1]
    depth = span // 2
    chip = my_chip()

    @pl.when(~in_chain())
    def _():
        for out in outs:
            out[...] = jnp.zeros(out.shape, jnp.float32)

    @pl.when(in_chain())
    def _():
        _, rows = section_rows(count, refs)
        rows = [row + applied[m * span : (m + 1) * span, :] for m, row in enumerate(rows)]
        table[...] = jnp.concatenate(rows[:2]).T
        for by, out in enumerate(outs):
            start = jnp.bitwise_xor(chip, by) * 2 * depth
            for core in range(2):
                out[:depth, core * 128 : (core + 1) * 128] = table[rows_at(start + core * depth, depth), :]
        low = chip == LOW
        upper, lower = rows[2][:depth], rows[2][depth:]
        outs[0][depth:] = jnp.where(low, lower, upper)
        outs[1][depth:] = jnp.where(low, upper, lower)


def joined(refs):
    return [[refs[i], refs[i + 1]] for i in range(0, 8, 2)]


def taken(pair, cut):
    return pair[0][cut, :] + pair[1][cut, :]


def load_halves(pieces, part, span):
    return halves(jnp.concatenate([taken(pair, slice(part * span, (part + 1) * span)) for pair in pieces]))


def query_body(queries, out_cot, *refs):
    pieces, d_queries = joined(refs[:8]), refs[8]
    span = queries.shape[1] // len(pieces)
    one, three, two = [load_halves(pieces, part, span) for part in range(3)]
    query, cot = halves(queries[...]), halves(out_cot[...])
    first, gate = nt(query, one), nt(query, three)
    value, d_one, _ = silu_parts(first)
    d_mixed = nt(cot, two)
    d_gate = d_mixed * value
    d_first = d_mixed * gate * d_one
    d_queries[...] = nn(halves(d_first), one) + nn(halves(d_gate), three)


def token_body(keys, values, rates, *refs):
    weights, cots = joined(refs[:8]), joined(refs[8:16])
    ends = joined(refs[16:24])
    d_keys, d_values, d_rates, d_rows = refs[24:]
    width = keys.shape[1]
    span = width // len(weights)
    one, three, two = [load_halves(weights, part, span) for part in range(3)]
    c_one, c_three, c_two = [load_halves(cots, part, span) for part in range(3)]
    rate = column(rates[...], width)
    key, scaled = halves(keys[...]), halves(-rate * values[...])
    first, gate = nt(key, one), nt(key, three)
    value, d_one, d_two = silu_parts(first)
    d_mixed = nt(scaled, two)
    t_first, t_gate, p_mixed = nt(key, c_one), nt(key, c_three), nt(scaled, c_two)
    mixed = value * gate
    d_gate = d_mixed * value
    d_first = d_mixed * gate * d_one
    lift = d_one * t_first
    t_mixed = lift * gate + value * t_gate
    c_gate = p_mixed * value + d_mixed * lift
    c_first = p_mixed * gate * d_one + d_mixed * (d_two * t_first * gate + d_one * t_gate)
    d_keys[...] = nn(halves(c_first), one) + nn(halves(c_gate), three) + nn(halves(d_first), c_one) + nn(halves(d_gate), c_three)
    t_out = nn(halves(t_mixed), two) + nn(halves(mixed), c_two)
    d_values[...] = -rate * t_out
    d_rates[...] = -jnp.sum((values[...] * t_out).T, axis=0, keepdims=True)
    depth = d_rows.shape[1]
    low_side, upper_core = my_chip() <= LOW, my_core() == 0
    block = slice(0, depth)
    sides = []
    for near, far in (ends[:2], ends[2:]):
        near, far = taken(near, block), taken(far, block)
        near, far = [jnp.where(upper_core, piece[:, :128], piece[:, 128:]) for piece in (near, far)]
        sides.append([jnp.where(low_side, near, far), jnp.where(low_side, far, near)])
    by_core = [[jnp.where(upper_core, a, b) for a, b in zip(*sides)], [jnp.where(upper_core, b, a) for a, b in zip(*sides)]]
    for m in range(2):
        parts = []
        for side in range(2):
            for i in range(2):
                for core in range(2):
                    start = (2 * m + i) * depth
                    parts.append(by_core[core][side][:, start : start + depth])
        d_rows[m] = jnp.concatenate(parts, axis=1)
    d_rows[2] = taken(ends[0], slice(depth, None))


def over_chips(array, moves):
    pairs = [(2 * a + core, 2 * b + (core if a != b else 1 - core)) for a, b in enumerate(moves) for core in range(2)]
    return lax.ppermute(array, "tok", pairs)


def by_xor(array, by):
    return over_chips(array, [chip ^ by for chip in range(CHIPS)])


ACROSS = (0, 2, 1, 3)
INWARD = (2, 0, 3, 1)
OUTWARD = (1, 3, 0, 2)


def exchanged(array):
    turned = [(2 * a + core, 2 * b + 1 - core) for a, b in enumerate(ACROSS) for core in range(2)]
    return [array, over_chips(array, ACROSS), lax.ppermute(array, "tok", turned), core_swap(array)]


def both_cores(pieces):
    swapped = [core_swap(pieces[0])]
    for piece in pieces[1:]:
        swapped.append(core_swap(piece))
    return pieces + swapped


def hops(arrays, far):
    first = by_xor(arrays[1], 1)
    second = over_chips(arrays[2], far)
    third = over_chips(arrays[3], ACROSS)
    return first, second, third


def to_chain(arrays):
    return both_cores([arrays[0], *hops(arrays, INWARD)])


def from_chain(arrays):
    near, far, across = hops(arrays, OUTWARD)
    return both_cores([arrays[0], near, across, far])


def from_chain_relayed(array):
    near = by_xor(array, 1)
    across = over_chips(array, ACROSS)
    far = by_xor(across, 1)
    return both_cores([array, near, across, far])


def to_earlier(array):
    groups = lax.axis_size("block")
    return lax.ppermute(array, "block", [(i, (i - 1) % groups) for i in range(groups)])


def to_later(array):
    groups = lax.axis_size("block")
    return lax.ppermute(array, "block", [(i, (i + 1) % groups) for i in range(groups)])


def per_device(queries, keys, values, rates, states, out_cot, final_cot):
    groups, size = lax.axis_size("block"), lax.axis_size("tok")
    depth, width = keys.shape
    own_rows = states[0]
    rows = own_rows.shape[1]
    if not (size == 2 * CHIPS and 4 * rows == 128 and depth == 128 and width == 8 * rows):
        return per_device_general(queries, keys, values, rates, states, out_cot, final_cot)
    span, tokens = 2 * rows, depth * size
    rates_row = rates.reshape(1, depth)
    state, square, wide = f32(3, span, width), f32(depth, width), f32(3 * span, width)
    sources = (keys, values, rates_row, own_rows, final_cot, queries, out_cot)
    longer, shorter = f32(2 * depth + 4 * rows, width), f32(2 * depth + 2 * rows, width)
    *packs, ahead = kernel_call(
        pack_body,
        [longer, longer, shorter, shorter, f32(2 * depth, width)],
        *sources,
        scratch=[pltpu.VMEM(array.shape, array.dtype) for array in sources] + [pltpu.SemaphoreType.DMA((len(sources),))],
        raw=True,
        limit=PACK_LIMIT,
    )
    pieces = to_chain(packs)
    ahead_pieces = to_chain([ahead] * CHIPS)
    half = bf16(tokens, width)
    own, last, *halved, kept, shifted, sums = kernel_call(
        forward_body,
        [state, state, half, half, half, half, f32(5, span, tokens), state, f32(8, width)],
        *pieces,
        scratch=[pltpu.VMEM((width, 4 * span), jnp.float32)],
    )
    all_sums = exchanged(sums)
    earlier = to_later(shifted)
    weights = from_chain_relayed(own.reshape(3 * span, width))

    inners, arrived = [], []
    common = [own, shifted, last, *all_sums]
    sent = [state, f32(8, width)]
    (raw,) = kernel_call(functools.partial(first_body, groups - 1), [state], *common, *halved, kept)
    for section in range(groups - 1):
        source = groups - 1 - section
        if section == 0:
            body = functools.partial(apply_body, source)
            applied, payload, partial = kernel_call(body, [wide] + sent, own, raw, earlier, *ahead_pieces)
        else:
            body = functools.partial(section_body, source)
            payload, partial = kernel_call(
                body, sent, *common, *inners[-4:], *arrived[-1:], *halved, kept, applied, earlier
            )
        straight = to_earlier(partial)
        arrived.append(to_earlier(payload))
        inners += exchanged(straight)
    received = [*common, *inners, *arrived]
    (cot,) = kernel_call(functools.partial(terms_body, groups - 1), [wide], *received)
    cots = from_chain([cot] * CHIPS)
    ends = kernel_call(
        functools.partial(final_body, groups - 1),
        [f32(2 * rows, width)] * 2 + [f32(rows, width)] * 2,
        *received,
        *halved,
        kept,
        applied,
        scratch=[pltpu.VMEM((width, 128), jnp.float32)],
    )
    end_pieces = from_chain(ends)
    (d_queries,) = kernel_call(query_body, [square], queries, out_cot, *weights, spill=True)
    d_keys, d_values, d_rates, d_rows = kernel_call(
        token_body,
        [square, square, f32(1, depth), f32(3, rows, width)],
        keys,
        values,
        rates_row,
        *weights,
        *cots,
        *end_pieces,
        spill=True,
    )
    return (d_queries, d_keys, d_values, d_rates.reshape(depth), d_rows[None])


def solution(mesh):
    return jax.shard_map(
        per_device,
        mesh=mesh,
        in_specs=(
            P(("block", "tok"), None),
            P(("block", "tok"), None),
            P(("block", "tok"), None),
            P(("block", "tok")),
            P("block", None, "tok", None),
            P(("block", "tok"), None),
            P(None, "tok", None),
        ),
        out_specs=(
            P(("block", "tok"), None),
            P(("block", "tok"), None),
            P(("block", "tok"), None),
            P(("block", "tok")),
            P("block", None, "tok", None),
        ),
        check_vma=False,
    )
```

```python
import functools

import jax
import jax.numpy as jnp
from jax import lax
from jax.experimental import pallas as pl
from jax.experimental.pallas import tpu as pltpu
from jax.sharding import PartitionSpec as P


EPS = 1e-06
HIGH = lax.Precision.HIGHEST


def mm(left, right):
    return lax.dot_general(left, right, (((1,), (0,)), ((), ())), precision=HIGH, preferred_element_type=jnp.float32)


def mm_nt(left, right):
    return lax.dot_general(left, right, (((1,), (1,)), ((), ())), precision=HIGH, preferred_element_type=jnp.float32)


def mm_tn(left, right):
    return lax.dot_general(left, right, (((0,), (0,)), ((), ())), precision=HIGH, preferred_element_type=jnp.float32)


def silu_parts(first):
    sig = 1.0 / (1.0 + jnp.exp(-first))
    slope = sig * (1.0 - sig)
    value = first * sig
    d_one = sig + first * slope
    d_two = slope * (2.0 + first * (1.0 - 2.0 * sig))
    return value, d_one, d_two


def direct(size):
    return size % 2 == 0 and size <= 16


def chip_shift(array, by):
    size = lax.axis_size("tok")
    return lax.ppermute(array, "tok", [(j, (j + 2 * by) % size) for j in range(size)])


def core_swap(array):
    size = lax.axis_size("tok")
    return lax.ppermute(array, "tok", [(j, j ^ 1) for j in range(size)])


def gather_pieces(array):
    size = lax.axis_size("tok")
    if not direct(size):
        return lax.all_gather(array, "tok")
    mine = jnp.stack([array] + [chip_shift(array, by) for by in range(1, size // 2)])
    return jnp.concatenate([mine, core_swap(mine)])


def spread_sum(pieces):
    size = lax.axis_size("tok")
    if not direct(size):
        return lax.psum_scatter(pieces, "tok")
    half = size // 2
    mine = pieces[:half] + core_swap(pieces[half:])
    total = mine[0]
    for by in range(1, half):
        total = total + chip_shift(mine[by], -by)
    return total


def sum_all(array):
    size = lax.axis_size("tok")
    if not direct(size):
        return jnp.sum(lax.all_gather(array, "tok"), axis=0)
    array = array + core_swap(array)
    total = array
    for by in range(1, size // 2):
        total = total + chip_shift(array, by)
    return total


def rows_to_hidden(rows):
    size = lax.axis_size("tok")
    count, depth, width = rows.shape
    parts = rows.reshape(count, depth, size, width // size).transpose(2, 0, 3, 1)
    parts = lax.all_to_all(parts, "tok", 0, 0)
    return parts.transpose(1, 2, 0, 3).reshape(count, width // size, depth * size)


def hidden_to_rows(slices):
    size = lax.axis_size("tok")
    count, depth, width = slices.shape
    parts = slices.reshape(count, depth, size, width // size).transpose(2, 0, 1, 3)
    parts = lax.all_to_all(parts, "tok", 0, 0)
    return parts.transpose(1, 3, 0, 2).reshape(count, width // size, depth * size)


def to_block(array, source, target, by=0):
    size = lax.axis_size("tok")
    pairs = [(source * size + j, target * size + (j + by) % size) for j in range(size)]
    return lax.ppermute(array, ("block", "tok"), pairs)


def up_one(array):
    groups = lax.axis_size("block")
    return lax.ppermute(array, "block", [(i, i + 1) for i in range(groups - 1)])


def slice_forward(weights, keys, scaled):
    first, gate = mm_nt(weights[0], keys), mm_nt(weights[1], keys)
    value, d_one, d_two = silu_parts(first)
    d_mixed = mm_nt(weights[2], scaled)
    mixed = value * gate
    d_gate = d_mixed * value
    d_first = d_mixed * gate * d_one
    grads = jnp.stack([mm(d_first, keys), mm(d_gate, keys), mm(mixed, scaled)])
    return grads, (gate, value, d_one, d_two, d_mixed)


def slice_adjoint(cot, kept, keys, scaled):
    gate, value, d_one, d_two, d_mixed = kept
    t_first, t_gate, p_mixed = mm_nt(cot[0], keys), mm_nt(cot[1], keys), mm_nt(cot[2], scaled)
    t_mixed = d_one * t_first * gate + value * t_gate
    c_gate = p_mixed * value + d_mixed * d_one * t_first
    c_first = p_mixed * gate * d_one + d_mixed * (d_two * t_first * gate + d_one * t_gate)
    return jnp.stack([mm(c_first, keys), mm(c_gate, keys), mm(t_mixed, scaled)])


def query_adjoint(weights, queries, out_cot):
    first, gate = mm_nt(queries, weights[0]), mm_nt(queries, weights[1])
    value, d_one, _ = silu_parts(first)
    d_mixed = mm_nt(out_cot, weights[2])
    d_gate = d_mixed * value
    d_first = d_mixed * gate * d_one
    d_queries = mm(d_first, weights[0]) + mm(d_gate, weights[1])
    d_weights = jnp.stack([mm_tn(d_first, queries), mm_tn(d_gate, queries), mm_tn(value * gate, out_cot)])
    return d_queries, d_weights


def token_adjoint(weights, cot, keys, scaled):
    first, gate = mm_nt(keys, weights[0]), mm_nt(keys, weights[1])
    value, d_one, d_two = silu_parts(first)
    d_mixed = mm_nt(scaled, weights[2])
    mixed = value * gate
    d_gate = d_mixed * value
    d_first = d_mixed * gate * d_one
    t_first, t_gate, p_mixed = mm_nt(keys, cot[0]), mm_nt(keys, cot[1]), mm_nt(scaled, cot[2])
    t_mixed = d_one * t_first * gate + value * t_gate
    c_gate = p_mixed * value + d_mixed * d_one * t_first
    c_first = p_mixed * gate * d_one + d_mixed * (d_two * t_first * gate + d_one * t_gate)
    d_keys = mm(c_first, weights[0]) + mm(c_gate, weights[1]) + mm(d_first, cot[0]) + mm(d_gate, cot[1])
    t_out = mm(t_mixed, weights[2]) + mm(mixed, cot[2])
    return d_keys, t_out


def over_hidden(array):
    return jnp.sum(array[:2], axis=1)


def per_device_general(queries, keys, values, rates, states, out_cot, final_cot):
    groups, size = lax.axis_size("block"), lax.axis_size("tok")
    position = lax.axis_index("block")
    own_rows = states[0]
    scaled = -rates[:, None] * values
    both = gather_pieces(jnp.stack([keys, scaled]))
    width = keys.shape[1]
    all_keys = both[:, 0].reshape(-1, width)
    all_scaled = both[:, 1].reshape(-1, width)
    split = rows_to_hidden(jnp.concatenate([own_rows[:2], final_cot[:2]]))
    own = jnp.concatenate([split[:2], own_rows[2:]])
    last = jnp.concatenate([split[2:], final_cot[2:]])
    grads, kept = slice_forward(own, all_keys, all_scaled)
    shifted = own - grads
    earlier = up_one(shifted[:2])
    sums = sum_all(jnp.concatenate([over_hidden(own * own), over_hidden(shifted * shifted), over_hidden(last * shifted)]))
    row_norm = [jnp.sqrt(sums[0:2, None, :] + EPS), jnp.sqrt(jnp.sum(own[2:] ** 2, axis=-1, keepdims=True) + EPS)]
    new_norm = [jnp.sqrt(sums[2:4, None, :] + EPS), jnp.sqrt(jnp.sum(shifted[2:] ** 2, axis=-1, keepdims=True) + EPS)]

    pieces = gather_pieces(own)
    whole = pieces.transpose(1, 0, 2, 3).reshape(3, -1, width)
    d_queries, d_weights = query_adjoint(whole, queries, out_cot)
    apply_state = spread_sum(d_weights.reshape(3, size, -1, width).transpose(1, 0, 2, 3))

    is_last = position == groups - 1
    incoming = jnp.where(is_last, last, 0.0)
    inner = jnp.where(is_last, sums[4:6], 0.0)
    for section in range(groups):
        inners = [inner[:, None, :], jnp.sum(incoming[2:] * shifted[2:], axis=-1, keepdims=True)]
        cots, straights = [], []
        for part, dot, old, new in zip((slice(0, 2), slice(2, 3)), inners, row_norm, new_norm):
            d_shifted = old / new * incoming[part] - old * dot / (new * new * new) * shifted[part]
            cots.append(-d_shifted)
            straights.append(d_shifted + dot / new * own[part] / old)
        cot = jnp.concatenate(cots)
        straight = jnp.concatenate(straights)
        rows_now = slice_adjoint(cot, kept, all_keys, all_scaled) + apply_state + straight
        if section + 1 < groups:
            source = groups - 1 - section
            partial = over_hidden(rows_now[:2] * earlier)
            incoming = incoming + to_block(rows_now, source, source - 1)
            if direct(size):
                for by in range(size):
                    inner = inner + to_block(partial, source, source - 1, by)
            else:
                inner = inner + to_block(sum_all(partial), source, source - 1)
    cot_pieces = gather_pieces(cot)
    whole_cot = cot_pieces.transpose(1, 0, 2, 3).reshape(3, -1, width)
    d_keys, t_out = token_adjoint(whole, whole_cot, keys, scaled)
    d_values = -rates[:, None] * t_out
    d_rates = -jnp.sum(values * t_out, axis=-1)
    d_rows = jnp.concatenate([hidden_to_rows(rows_now[:2]), rows_now[2:]])
    return (d_queries, d_keys, d_values, d_rates, d_rows[None])


def halves(array):
    upper = array.astype(jnp.bfloat16)
    return upper, (array - upper.astype(jnp.float32)).astype(jnp.bfloat16)


def product(left, right, contract):
    def one(a, b):
        return lax.dot_general(a, b, (((1,), (contract,)), ((), ())), preferred_element_type=jnp.float32)

    rows = left[0].shape[0]
    upper = one(jnp.concatenate(left), right[0])
    return upper[:rows] + (upper[rows:] + one(left[0], right[1]))


def nn(left, right):
    return product(left, right, 0)


def nt(left, right):
    return product(left, right, 1)


def kernel_call(body, outs, *operands, scratch=(), raw=False, spill=False, limit=24 * 1024 * 1024):
    space = pltpu.MemorySpace.HBM if raw else pltpu.VMEM
    return pl.pallas_call(
        body,
        in_specs=[pl.BlockSpec(memory_space=space) for _ in operands],
        out_specs=[pl.BlockSpec(memory_space=pltpu.VMEM) for _ in outs],
        out_shape=[(jax.ShapeDtypeStruct if spill else pltpu.VMEM)(shape, dtype) for shape, dtype in outs],
        scratch_shapes=list(scratch),
        compiler_params=pltpu.CompilerParams(vmem_limit_bytes=limit),
    )(*operands)


def my_chip():
    return lax.div(lax.axis_index("tok"), 2)


def my_core():
    return lax.rem(lax.axis_index("tok"), 2)


def in_chain():
    return (my_chip() == LOW) | (my_chip() == HIGH_CHIP)


def f32(*shape):
    return shape, jnp.float32


def bf16(*shape):
    return shape, jnp.bfloat16


def column(row, width):
    block = jnp.broadcast_to(row, (128, row.shape[1])).T
    return jnp.concatenate([block] * (width // 128), axis=1)


CHIPS = 4
LOW, HIGH_CHIP = 1, 2
CHUNK = 512
PACK_LIMIT = 61 * 1024 * 1024


def rows_at(start, count):
    return pl.ds(pl.multiple_of(start, count), count)


def pack_body(*refs):
    count = 7
    sources, outs = refs[:count], refs[count : count + CHIPS + 1]
    buffers, sems = refs[count + CHIPS + 1 : -1], refs[-1]
    copies = [pltpu.make_async_copy(a, b, sems.at[i]) for i, (a, b) in enumerate(zip(sources, buffers))]
    for copy in copies:
        copy.start()
    for copy in copies:
        copy.wait()
    keys, values, rates, rows, final, queries, cot = buffers
    packs, ahead = outs[:CHIPS], outs[CHIPS]
    tokens = keys.shape[0]
    depth = rows.shape[1]
    scaled = -column(rates[...], values.shape[1]) * values[...]
    sides = []
    for side in range(2):
        parts = []
        for core in range(2):
            lanes = []
            for source in (rows, final):
                for m in range(2):
                    for i in range(2):
                        start = (4 * side + 2 * i + core) * depth
                        lanes.append(source[m, :, start : start + depth])
            parts.append(jnp.concatenate(lanes, axis=1))
        sides.append(jnp.concatenate(parts))
    for by, pack in enumerate(packs):
        pack[:tokens] = keys[...]
        pack[tokens : 2 * tokens] = scaled
        low = jnp.bitwise_xor(my_chip(), by) == LOW
        pack[2 * tokens : 2 * tokens + 2 * depth] = jnp.where(low, sides[0], sides[1])
        if by < 2:
            pack[2 * tokens + 2 * depth : 2 * tokens + 3 * depth] = rows[2]
            pack[2 * tokens + 3 * depth :] = final[2]
    ahead[:tokens] = queries[...]
    ahead[tokens:] = cot[...]


def unpack(packs, mates, own, last, table):
    depth = own.shape[1] // 2
    base = packs[0].shape[0] - 4 * depth
    span = own.shape[1]
    chip, core = my_chip(), my_core()
    for by in range(CHIPS):
        source = jnp.bitwise_xor(chip, by)
        mine = rows_at(base + core * depth, depth)
        table[rows_at((2 * source + core) * depth, depth), :] = packs[by][mine, :]
        table[rows_at((2 * source + 1 - core) * depth, depth), :] = mates[by][mine, :]
    turned = table[...].T
    keep = jnp.where(lax.axis_index("block") == lax.axis_size("block") - 1, 1.0, 0.0)
    own[0], own[1] = turned[:span], turned[span : 2 * span]
    last[0], last[1] = turned[2 * span : 3 * span] * keep, turned[3 * span :] * keep
    low = chip == LOW
    for place, out, scale in ((2 * depth, own, 1.0), (3 * depth, last, keep)):
        cut = slice(base + place, base + place + depth)
        out[2, :depth] = jnp.where(low, packs[1][cut, :], packs[0][cut, :]) * scale
        out[2, depth:] = jnp.where(low, packs[0][cut, :], packs[1][cut, :]) * scale


def forward_body(*refs):
    packs, mates = refs[:CHIPS], refs[CHIPS : 2 * CHIPS]
    own, last, key_high, key_low, scaled_high, scaled_low, kept, shifted, sums, table = refs[2 * CHIPS :]
    pieces = packs + mates
    depth = key_high.shape[0] // len(pieces)
    span = own.shape[1]

    @pl.when(~in_chain())
    def _():
        for out in (own, shifted, sums):
            out[...] = jnp.zeros(out.shape, jnp.float32)

    @pl.when(in_chain())
    def _():
        unpack(packs, mates, own, last, table)
        for index, piece in enumerate(pieces):
            cut = slice(index * depth, (index + 1) * depth)
            key_high[cut, :], key_low[cut, :] = halves(piece[:depth, :])
            scaled_high[cut, :], scaled_low[cut, :] = halves(piece[depth : 2 * depth, :])
        pair = halves(jnp.concatenate([own[0], own[1]]))
        second = halves(own[2])
        grad_pair, grad_second = 0.0, 0.0
        for start in range(0, key_high.shape[0], CHUNK):
            cut = slice(start, start + CHUNK)
            key_cut = key_high[cut, :], key_low[cut, :]
            scaled_cut = scaled_high[cut, :], scaled_low[cut, :]
            both = nt(pair, key_cut)
            d_mixed = nt(second, scaled_cut)
            first, gate = both[:span], both[span:]
            value, d_one, d_two = silu_parts(first)
            for place, array in enumerate((gate, value, d_one, d_two, d_mixed)):
                kept[place, :, cut] = array
            d_pair = jnp.concatenate([d_mixed * gate * d_one, d_mixed * value])
            grad_pair += nn(halves(d_pair), key_cut)
            grad_second += nn(halves(value * gate), scaled_cut)
        moved = own[0] - grad_pair[:span], own[1] - grad_pair[span:], own[2] - grad_second
        rows = []
        for left, right in ((own, own), (moved, moved), (last, moved)):
            rows += [jnp.sum(left[m] * right[m], axis=0, keepdims=True) for m in range(2)]
        sums[...] = jnp.concatenate(rows + [jnp.zeros((2, own.shape[2]), jnp.float32)])
        for m in range(3):
            shifted[m] = moved[m]


def apply_body(source, own, raw, earlier, *refs):
    pieces, (applied, payload, partial) = refs[:-3], refs[-3:]
    span = own.shape[1]
    depth = pieces[0].shape[0] // 2
    active = (lax.axis_index("block") == source) & in_chain()

    @pl.when(~active)
    def _():
        payload[...] = jnp.zeros(payload.shape, jnp.float32)
        partial[...] = jnp.zeros(partial.shape, jnp.float32)

    @pl.when(in_chain())
    def _():
        pair = halves(jnp.concatenate([own[0], own[1]]))
        second = halves(own[2])
        out_pair, out_second = 0.0, 0.0
        step = CHUNK // depth
        for index in range(0, len(pieces), step):
            query = halves(jnp.concatenate([piece[:depth, :] for piece in pieces[index : index + step]]))
            cot = halves(jnp.concatenate([piece[depth:, :] for piece in pieces[index : index + step]]))
            both = nt(pair, query)
            d_mixed = nt(second, cot)
            first, gate = both[:span], both[span:]
            value, d_one, _ = silu_parts(first)
            out_pair += nn(halves(jnp.concatenate([d_mixed * gate * d_one, d_mixed * value])), query)
            out_second += nn(halves(value * gate), cot)
        applied[: 2 * span] = out_pair
        applied[2 * span :] = out_second

    @pl.when(active)
    def _():
        rows = [raw[m] + applied[m * span : (m + 1) * span, :] for m in range(3)]
        finish(rows, earlier, payload, partial)


def finish(rows, earlier, payload, partial):
    sums = [jnp.sum(rows[m] * earlier[m], axis=0, keepdims=True) for m in range(2)]
    partial[...] = jnp.concatenate(sums + [jnp.zeros((6, rows[0].shape[1]), jnp.float32)])
    for m in range(3):
        payload[m] = rows[m]


def state_terms(own, shifted, last, sums, inners, arrived):
    total = sums[0][...] + sums[1][...] + (sums[2][...] + sums[3][...])
    inner = total[4:6]
    for array in inners:
        inner = inner + array[0:2]
    cots, straights = [], []
    for m in range(3):
        incoming = last[m]
        for array in arrived:
            incoming = incoming + array[m]
        if m < 2:
            dot, old, new = inner[m : m + 1], jnp.sqrt(total[m : m + 1] + EPS), jnp.sqrt(total[m + 2 : m + 3] + EPS)
        else:
            dot = jnp.sum(incoming * shifted[m], axis=-1, keepdims=True)
            old = jnp.sqrt(jnp.sum(own[m] * own[m], axis=-1, keepdims=True) + EPS)
            new = jnp.sqrt(jnp.sum(shifted[m] * shifted[m], axis=-1, keepdims=True) + EPS)
        d_shifted = old / new * incoming - old * dot / (new * new * new) * shifted[m]
        cots.append(-d_shifted)
        straights.append(d_shifted + dot / new * own[m] / old)
    return cots, straights


def section_rows(count, refs):
    own, shifted, last = refs[:3]
    sums, inners, arrived = refs[3:7], refs[7 : 7 + 4 * count], refs[7 + 4 * count : 7 + 5 * count]
    key_high, key_low, scaled_high, scaled_low, kept = refs[7 + 5 * count : 12 + 5 * count]
    span = own.shape[1]
    cots, straights = state_terms(own, shifted, last, sums, inners, arrived)
    pair = halves(jnp.concatenate(cots[:2]))
    second = halves(cots[2])
    d_pair, d_second = 0.0, 0.0
    for start in range(0, key_high.shape[0], CHUNK):
        cut = slice(start, start + CHUNK)
        key_cut = key_high[cut, :], key_low[cut, :]
        scaled_cut = scaled_high[cut, :], scaled_low[cut, :]
        gate, value, d_one, d_two, d_mixed = [kept[place, :, cut] for place in range(5)]
        both = nt(pair, key_cut)
        p_mixed = nt(second, scaled_cut)
        t_first, t_gate = both[:span], both[span:]
        lift = d_one * t_first
        t_mixed = lift * gate + value * t_gate
        c_gate = p_mixed * value + d_mixed * lift
        c_first = p_mixed * gate * d_one + d_mixed * (d_two * t_first * gate + d_one * t_gate)
        d_pair += nn(halves(jnp.concatenate([c_first, c_gate])), key_cut)
        d_second += nn(halves(t_mixed), scaled_cut)
    return cots, [d_pair[:span] + straights[0], d_pair[span:] + straights[1], d_second + straights[2]]


def first_body(source, *refs):
    raw = refs[-1]

    @pl.when((lax.axis_index("block") == source) & in_chain())
    def _():
        _, rows = section_rows(0, refs)
        for m in range(3):
            raw[m] = rows[m]


def section_body(source, *refs):
    applied, earlier, payload, partial = refs[-4:]
    active = (lax.axis_index("block") == source) & in_chain()

    @pl.when(~active)
    def _():
        payload[...] = jnp.zeros(payload.shape, jnp.float32)
        partial[...] = jnp.zeros(partial.shape, jnp.float32)

    @pl.when(active)
    def _():
        span = payload.shape[1]
        _, rows = section_rows(1, refs)
        finish([row + applied[m * span : (m + 1) * span, :] for m, row in enumerate(rows)], earlier, payload, partial)


def terms_body(count, *refs):
    cot = refs[-1]
    span = refs[0].shape[1]

    @pl.when(~in_chain())
    def _():
        cot[...] = jnp.zeros(cot.shape, jnp.float32)

    @pl.when(in_chain())
    def _():
        cots, _ = state_terms(*refs[:3], refs[3:7], refs[7 : 7 + 4 * count], refs[7 + 4 * count : 7 + 5 * count])
        for m in range(3):
            cot[m * span : (m + 1) * span, :] = cots[m]


def final_body(count, *refs):
    applied, outs, table = refs[-6], refs[-5:-1], refs[-1]
    span = refs[0].shape[1]
    depth = span // 2
    chip = my_chip()

    @pl.when(~in_chain())
    def _():
        for out in outs:
            out[...] = jnp.zeros(out.shape, jnp.float32)

    @pl.when(in_chain())
    def _():
        _, rows = section_rows(count, refs)
        rows = [row + applied[m * span : (m + 1) * span, :] for m, row in enumerate(rows)]
        table[...] = jnp.concatenate(rows[:2]).T
        for by, out in enumerate(outs):
            start = jnp.bitwise_xor(chip, by) * 2 * depth
            for core in range(2):
                out[:depth, core * 128 : (core + 1) * 128] = table[rows_at(start + core * depth, depth), :]
        low = chip == LOW
        upper, lower = rows[2][:depth], rows[2][depth:]
        outs[0][depth:] = jnp.where(low, lower, upper)
        outs[1][depth:] = jnp.where(low, upper, lower)


def joined(refs):
    return [[refs[i], refs[i + 1]] for i in range(0, 8, 2)]


def taken(pair, cut):
    return pair[0][cut, :] + pair[1][cut, :]


def load_halves(pieces, part, span):
    return halves(jnp.concatenate([taken(pair, slice(part * span, (part + 1) * span)) for pair in pieces]))


def query_body(queries, out_cot, *refs):
    pieces, d_queries = joined(refs[:8]), refs[8]
    span = queries.shape[1] // len(pieces)
    one, three, two = [load_halves(pieces, part, span) for part in range(3)]
    query, cot = halves(queries[...]), halves(out_cot[...])
    first, gate = nt(query, one), nt(query, three)
    value, d_one, _ = silu_parts(first)
    d_mixed = nt(cot, two)
    d_gate = d_mixed * value
    d_first = d_mixed * gate * d_one
    d_queries[...] = nn(halves(d_first), one) + nn(halves(d_gate), three)


def token_body(keys, values, rates, *refs):
    weights, cots = joined(refs[:8]), joined(refs[8:16])
    ends = joined(refs[16:24])
    d_keys, d_values, d_rates, d_rows = refs[24:]
    width = keys.shape[1]
    span = width // len(weights)
    one, three, two = [load_halves(weights, part, span) for part in range(3)]
    c_one, c_three, c_two = [load_halves(cots, part, span) for part in range(3)]
    rate = column(rates[...], width)
    key, scaled = halves(keys[...]), halves(-rate * values[...])
    first, gate = nt(key, one), nt(key, three)
    value, d_one, d_two = silu_parts(first)
    d_mixed = nt(scaled, two)
    t_first, t_gate, p_mixed = nt(key, c_one), nt(key, c_three), nt(scaled, c_two)
    mixed = value * gate
    d_gate = d_mixed * value
    d_first = d_mixed * gate * d_one
    lift = d_one * t_first
    t_mixed = lift * gate + value * t_gate
    c_gate = p_mixed * value + d_mixed * lift
    c_first = p_mixed * gate * d_one + d_mixed * (d_two * t_first * gate + d_one * t_gate)
    d_keys[...] = nn(halves(c_first), one) + nn(halves(c_gate), three) + nn(halves(d_first), c_one) + nn(halves(d_gate), c_three)
    t_out = nn(halves(t_mixed), two) + nn(halves(mixed), c_two)
    d_values[...] = -rate * t_out
    d_rates[...] = -jnp.sum((values[...] * t_out).T, axis=0, keepdims=True)
    depth = d_rows.shape[1]
    low_side, upper_core = my_chip() <= LOW, my_core() == 0
    block = slice(0, depth)
    sides = []
    for near, far in (ends[:2], ends[2:]):
        near, far = taken(near, block), taken(far, block)
        near, far = [jnp.where(upper_core, piece[:, :128], piece[:, 128:]) for piece in (near, far)]
        sides.append([jnp.where(low_side, near, far), jnp.where(low_side, far, near)])
    by_core = [[jnp.where(upper_core, a, b) for a, b in zip(*sides)], [jnp.where(upper_core, b, a) for a, b in zip(*sides)]]
    for m in range(2):
        parts = []
        for side in range(2):
            for i in range(2):
                for core in range(2):
                    start = (2 * m + i) * depth
                    parts.append(by_core[core][side][:, start : start + depth])
        d_rows[m] = jnp.concatenate(parts, axis=1)
    d_rows[2] = taken(ends[0], slice(depth, None))


def over_chips(array, moves):
    pairs = [(2 * a + core, 2 * b + (core if a != b else 1 - core)) for a, b in enumerate(moves) for core in range(2)]
    return lax.ppermute(array, "tok", pairs)


def by_xor(array, by):
    return over_chips(array, [chip ^ by for chip in range(CHIPS)])


ACROSS = (0, 2, 1, 3)
INWARD = (2, 0, 3, 1)
OUTWARD = (1, 3, 0, 2)


def exchanged(array):
    turned = [(2 * a + core, 2 * b + 1 - core) for a, b in enumerate(ACROSS) for core in range(2)]
    return [array, over_chips(array, ACROSS), lax.ppermute(array, "tok", turned), core_swap(array)]


def both_cores(pieces):
    swapped = [core_swap(pieces[0])]
    for piece in pieces[1:]:
        swapped.append(core_swap(piece))
    return pieces + swapped


def hops(arrays, far):
    first = by_xor(arrays[1], 1)
    second = over_chips(arrays[2], far)
    third = over_chips(arrays[3], ACROSS)
    return first, second, third


def to_chain(arrays):
    return both_cores([arrays[0], *hops(arrays, INWARD)])


def from_chain(arrays):
    near, far, across = hops(arrays, OUTWARD)
    return both_cores([arrays[0], near, across, far])


def from_chain_relayed(array):
    near = by_xor(array, 1)
    across = over_chips(array, ACROSS)
    far = by_xor(across, 1)
    return both_cores([array, near, across, far])


def to_earlier(array):
    groups = lax.axis_size("block")
    return lax.ppermute(array, "block", [(i, (i - 1) % groups) for i in range(groups)])


def to_later(array):
    groups = lax.axis_size("block")
    return lax.ppermute(array, "block", [(i, (i + 1) % groups) for i in range(groups)])


def per_device(queries, keys, values, rates, states, out_cot, final_cot):
    groups, size = lax.axis_size("block"), lax.axis_size("tok")
    depth, width = keys.shape
    own_rows = states[0]
    rows = own_rows.shape[1]
    if not (size == 2 * CHIPS and 4 * rows == 128 and depth == 128 and width == 8 * rows):
        return per_device_general(queries, keys, values, rates, states, out_cot, final_cot)
    span, tokens = 2 * rows, depth * size
    rates_row = rates.reshape(1, depth)
    state, square, wide = f32(3, span, width), f32(depth, width), f32(3 * span, width)
    sources = (keys, values, rates_row, own_rows, final_cot, queries, out_cot)
    longer, shorter = f32(2 * depth + 4 * rows, width), f32(2 * depth + 2 * rows, width)
    *packs, ahead = kernel_call(
        pack_body,
        [longer, longer, shorter, shorter, f32(2 * depth, width)],
        *sources,
        scratch=[pltpu.VMEM(array.shape, array.dtype) for array in sources] + [pltpu.SemaphoreType.DMA((len(sources),))],
        raw=True,
        limit=PACK_LIMIT,
    )
    pieces = to_chain(packs)
    ahead_pieces = to_chain([ahead] * CHIPS)
    half = bf16(tokens, width)
    own, last, *halved, kept, shifted, sums = kernel_call(
        forward_body,
        [state, state, half, half, half, half, f32(5, span, tokens), state, f32(8, width)],
        *pieces,
        scratch=[pltpu.VMEM((width, 4 * span), jnp.float32)],
    )
    all_sums = exchanged(sums)
    earlier = to_later(shifted)
    weights = from_chain_relayed(own.reshape(3 * span, width))

    inners, arrived = [], []
    common = [own, shifted, last, *all_sums]
    sent = [state, f32(8, width)]
    (raw,) = kernel_call(functools.partial(first_body, groups - 1), [state], *common, *halved, kept)
    for section in range(groups - 1):
        source = groups - 1 - section
        if section == 0:
            body = functools.partial(apply_body, source)
            applied, payload, partial = kernel_call(body, [wide] + sent, own, raw, earlier, *ahead_pieces)
        else:
            body = functools.partial(section_body, source)
            payload, partial = kernel_call(
                body, sent, *common, *inners[-4:], *arrived[-1:], *halved, kept, applied, earlier
            )
        straight = to_earlier(partial)
        arrived.append(to_earlier(payload))
        inners += exchanged(straight)
    received = [*common, *inners, *arrived]
    (cot,) = kernel_call(functools.partial(terms_body, groups - 1), [wide], *received)
    cots = from_chain([cot] * CHIPS)
    ends = kernel_call(
        functools.partial(final_body, groups - 1),
        [f32(2 * rows, width)] * 2 + [f32(rows, width)] * 2,
        *received,
        *halved,
        kept,
        applied,
        scratch=[pltpu.VMEM((width, 128), jnp.float32)],
    )
    end_pieces = from_chain(ends)
    (d_queries,) = kernel_call(query_body, [square], queries, out_cot, *weights, spill=True)
    d_keys, d_values, d_rates, d_rows = kernel_call(
        token_body,
        [square, square, f32(1, depth), f32(3, rows, width)],
        keys,
        values,
        rates_row,
        *weights,
        *cots,
        *end_pieces,
        spill=True,
    )
    return (d_queries, d_keys, d_values, d_rates.reshape(depth), d_rows[None])


def solution(mesh):
    return jax.shard_map(
        per_device,
        mesh=mesh,
        in_specs=(
            P(("block", "tok"), None),
            P(("block", "tok"), None),
            P(("block", "tok"), None),
            P(("block", "tok")),
            P("block", None, "tok", None),
            P(("block", "tok"), None),
            P(None, "tok", None),
        ),
        out_specs=(
            P(("block", "tok"), None),
            P(("block", "tok"), None),
            P(("block", "tok"), None),
            P(("block", "tok")),
            P("block", None, "tok", None),
        ),
        check_vma=False,
    )
```

```python
import functools

import jax
import jax.numpy as jnp
from jax import lax
from jax.experimental import pallas as pl
from jax.experimental.pallas import tpu as pltpu
from jax.sharding import PartitionSpec as P


EPS = 1e-06
HIGH = lax.Precision.HIGHEST


def mm(left, right):
    return lax.dot_general(left, right, (((1,), (0,)), ((), ())), precision=HIGH, preferred_element_type=jnp.float32)


def mm_nt(left, right):
    return lax.dot_general(left, right, (((1,), (1,)), ((), ())), precision=HIGH, preferred_element_type=jnp.float32)


def mm_tn(left, right):
    return lax.dot_general(left, right, (((0,), (0,)), ((), ())), precision=HIGH, preferred_element_type=jnp.float32)


def silu_parts(first):
    sig = 1.0 / (1.0 + jnp.exp(-first))
    slope = sig * (1.0 - sig)
    value = first * sig
    d_one = sig + first * slope
    d_two = slope * (2.0 + first * (1.0 - 2.0 * sig))
    return value, d_one, d_two


def direct(size):
    return size % 2 == 0 and size <= 16


def chip_shift(array, by):
    size = lax.axis_size("tok")
    return lax.ppermute(array, "tok", [(j, (j + 2 * by) % size) for j in range(size)])


def core_swap(array):
    size = lax.axis_size("tok")
    return lax.ppermute(array, "tok", [(j, j ^ 1) for j in range(size)])


def gather_pieces(array):
    size = lax.axis_size("tok")
    if not direct(size):
        return lax.all_gather(array, "tok")
    mine = jnp.stack([array] + [chip_shift(array, by) for by in range(1, size // 2)])
    return jnp.concatenate([mine, core_swap(mine)])


def spread_sum(pieces):
    size = lax.axis_size("tok")
    if not direct(size):
        return lax.psum_scatter(pieces, "tok")
    half = size // 2
    mine = pieces[:half] + core_swap(pieces[half:])
    total = mine[0]
    for by in range(1, half):
        total = total + chip_shift(mine[by], -by)
    return total


def sum_all(array):
    size = lax.axis_size("tok")
    if not direct(size):
        return jnp.sum(lax.all_gather(array, "tok"), axis=0)
    array = array + core_swap(array)
    total = array
    for by in range(1, size // 2):
        total = total + chip_shift(array, by)
    return total


def rows_to_hidden(rows):
    size = lax.axis_size("tok")
    count, depth, width = rows.shape
    parts = rows.reshape(count, depth, size, width // size).transpose(2, 0, 3, 1)
    parts = lax.all_to_all(parts, "tok", 0, 0)
    return parts.transpose(1, 2, 0, 3).reshape(count, width // size, depth * size)


def hidden_to_rows(slices):
    size = lax.axis_size("tok")
    count, depth, width = slices.shape
    parts = slices.reshape(count, depth, size, width // size).transpose(2, 0, 1, 3)
    parts = lax.all_to_all(parts, "tok", 0, 0)
    return parts.transpose(1, 3, 0, 2).reshape(count, width // size, depth * size)


def to_block(array, source, target, by=0):
    size = lax.axis_size("tok")
    pairs = [(source * size + j, target * size + (j + by) % size) for j in range(size)]
    return lax.ppermute(array, ("block", "tok"), pairs)


def up_one(array):
    groups = lax.axis_size("block")
    return lax.ppermute(array, "block", [(i, i + 1) for i in range(groups - 1)])


def slice_forward(weights, keys, scaled):
    first, gate = mm_nt(weights[0], keys), mm_nt(weights[1], keys)
    value, d_one, d_two = silu_parts(first)
    d_mixed = mm_nt(weights[2], scaled)
    mixed = value * gate
    d_gate = d_mixed * value
    d_first = d_mixed * gate * d_one
    grads = jnp.stack([mm(d_first, keys), mm(d_gate, keys), mm(mixed, scaled)])
    return grads, (gate, value, d_one, d_two, d_mixed)


def slice_adjoint(cot, kept, keys, scaled):
    gate, value, d_one, d_two, d_mixed = kept
    t_first, t_gate, p_mixed = mm_nt(cot[0], keys), mm_nt(cot[1], keys), mm_nt(cot[2], scaled)
    t_mixed = d_one * t_first * gate + value * t_gate
    c_gate = p_mixed * value + d_mixed * d_one * t_first
    c_first = p_mixed * gate * d_one + d_mixed * (d_two * t_first * gate + d_one * t_gate)
    return jnp.stack([mm(c_first, keys), mm(c_gate, keys), mm(t_mixed, scaled)])


def query_adjoint(weights, queries, out_cot):
    first, gate = mm_nt(queries, weights[0]), mm_nt(queries, weights[1])
    value, d_one, _ = silu_parts(first)
    d_mixed = mm_nt(out_cot, weights[2])
    d_gate = d_mixed * value
    d_first = d_mixed * gate * d_one
    d_queries = mm(d_first, weights[0]) + mm(d_gate, weights[1])
    d_weights = jnp.stack([mm_tn(d_first, queries), mm_tn(d_gate, queries), mm_tn(value * gate, out_cot)])
    return d_queries, d_weights


def token_adjoint(weights, cot, keys, scaled):
    first, gate = mm_nt(keys, weights[0]), mm_nt(keys, weights[1])
    value, d_one, d_two = silu_parts(first)
    d_mixed = mm_nt(scaled, weights[2])
    mixed = value * gate
    d_gate = d_mixed * value
    d_first = d_mixed * gate * d_one
    t_first, t_gate, p_mixed = mm_nt(keys, cot[0]), mm_nt(keys, cot[1]), mm_nt(scaled, cot[2])
    t_mixed = d_one * t_first * gate + value * t_gate
    c_gate = p_mixed * value + d_mixed * d_one * t_first
    c_first = p_mixed * gate * d_one + d_mixed * (d_two * t_first * gate + d_one * t_gate)
    d_keys = mm(c_first, weights[0]) + mm(c_gate, weights[1]) + mm(d_first, cot[0]) + mm(d_gate, cot[1])
    t_out = mm(t_mixed, weights[2]) + mm(mixed, cot[2])
    return d_keys, t_out


def over_hidden(array):
    return jnp.sum(array[:2], axis=1)


def per_device_general(queries, keys, values, rates, states, out_cot, final_cot):
    groups, size = lax.axis_size("block"), lax.axis_size("tok")
    position = lax.axis_index("block")
    own_rows = states[0]
    scaled = -rates[:, None] * values
    both = gather_pieces(jnp.stack([keys, scaled]))
    width = keys.shape[1]
    all_keys = both[:, 0].reshape(-1, width)
    all_scaled = both[:, 1].reshape(-1, width)
    split = rows_to_hidden(jnp.concatenate([own_rows[:2], final_cot[:2]]))
    own = jnp.concatenate([split[:2], own_rows[2:]])
    last = jnp.concatenate([split[2:], final_cot[2:]])
    grads, kept = slice_forward(own, all_keys, all_scaled)
    shifted = own - grads
    earlier = up_one(shifted[:2])
    sums = sum_all(jnp.concatenate([over_hidden(own * own), over_hidden(shifted * shifted), over_hidden(last * shifted)]))
    row_norm = [jnp.sqrt(sums[0:2, None, :] + EPS), jnp.sqrt(jnp.sum(own[2:] ** 2, axis=-1, keepdims=True) + EPS)]
    new_norm = [jnp.sqrt(sums[2:4, None, :] + EPS), jnp.sqrt(jnp.sum(shifted[2:] ** 2, axis=-1, keepdims=True) + EPS)]

    pieces = gather_pieces(own)
    whole = pieces.transpose(1, 0, 2, 3).reshape(3, -1, width)
    d_queries, d_weights = query_adjoint(whole, queries, out_cot)
    apply_state = spread_sum(d_weights.reshape(3, size, -1, width).transpose(1, 0, 2, 3))

    is_last = position == groups - 1
    incoming = jnp.where(is_last, last, 0.0)
    inner = jnp.where(is_last, sums[4:6], 0.0)
    for section in range(groups):
        inners = [inner[:, None, :], jnp.sum(incoming[2:] * shifted[2:], axis=-1, keepdims=True)]
        cots, straights = [], []
        for part, dot, old, new in zip((slice(0, 2), slice(2, 3)), inners, row_norm, new_norm):
            d_shifted = old / new * incoming[part] - old * dot / (new * new * new) * shifted[part]
            cots.append(-d_shifted)
            straights.append(d_shifted + dot / new * own[part] / old)
        cot = jnp.concatenate(cots)
        straight = jnp.concatenate(straights)
        rows_now = slice_adjoint(cot, kept, all_keys, all_scaled) + apply_state + straight
        if section + 1 < groups:
            source = groups - 1 - section
            partial = over_hidden(rows_now[:2] * earlier)
            incoming = incoming + to_block(rows_now, source, source - 1)
            if direct(size):
                for by in range(size):
                    inner = inner + to_block(partial, source, source - 1, by)
            else:
                inner = inner + to_block(sum_all(partial), source, source - 1)
    cot_pieces = gather_pieces(cot)
    whole_cot = cot_pieces.transpose(1, 0, 2, 3).reshape(3, -1, width)
    d_keys, t_out = token_adjoint(whole, whole_cot, keys, scaled)
    d_values = -rates[:, None] * t_out
    d_rates = -jnp.sum(values * t_out, axis=-1)
    d_rows = jnp.concatenate([hidden_to_rows(rows_now[:2]), rows_now[2:]])
    return (d_queries, d_keys, d_values, d_rates, d_rows[None])


def halves(array):
    upper = array.astype(jnp.bfloat16)
    return upper, (array - upper.astype(jnp.float32)).astype(jnp.bfloat16)


def product(left, right, contract):
    def one(a, b):
        return lax.dot_general(a, b, (((1,), (contract,)), ((), ())), preferred_element_type=jnp.float32)

    rows = left[0].shape[0]
    upper = one(jnp.concatenate(left), right[0])
    return upper[:rows] + (upper[rows:] + one(left[0], right[1]))


def nn(left, right):
    return product(left, right, 0)


def nt(left, right):
    return product(left, right, 1)


def kernel_call(body, outs, *operands, scratch=(), raw=False, spill=0, limit=24 * 1024 * 1024):
    space = pltpu.MemorySpace.HBM if raw else pltpu.VMEM
    return pl.pallas_call(
        body,
        in_specs=[pl.BlockSpec(memory_space=space) for _ in operands],
        out_specs=[pl.BlockSpec(memory_space=pltpu.VMEM) for _ in outs],
        out_shape=[(jax.ShapeDtypeStruct if i < spill else pltpu.VMEM)(*out) for i, out in enumerate(outs)],
        scratch_shapes=list(scratch),
        compiler_params=pltpu.CompilerParams(vmem_limit_bytes=limit),
    )(*operands)


def my_chip():
    return lax.div(lax.axis_index("tok"), 2)


def my_core():
    return lax.rem(lax.axis_index("tok"), 2)


def in_chain():
    return (my_chip() == LOW) | (my_chip() == HIGH_CHIP)


def f32(*shape):
    return shape, jnp.float32


def bf16(*shape):
    return shape, jnp.bfloat16


def column(row, width):
    block = jnp.broadcast_to(row, (128, row.shape[1])).T
    return jnp.concatenate([block] * (width // 128), axis=1)


CHIPS = 4
LOW, HIGH_CHIP = 1, 2
CHUNK = 512
PACK_LIMIT = 61 * 1024 * 1024


def rows_at(start, count):
    return pl.ds(pl.multiple_of(start, count), count)


def pack_body(*refs):
    count = 7
    sources, outs = refs[:count], refs[count : count + CHIPS + 1]
    buffers, sems = refs[count + CHIPS + 1 : -1], refs[-1]
    copies = [pltpu.make_async_copy(a, b, sems.at[i]) for i, (a, b) in enumerate(zip(sources, buffers))]
    for copy in copies:
        copy.start()
    for copy in copies:
        copy.wait()
    keys, values, rates, rows, final, queries, cot = buffers
    packs, ahead = outs[:CHIPS], outs[CHIPS]
    tokens = keys.shape[0]
    depth = rows.shape[1]
    scaled = -column(rates[...], values.shape[1]) * values[...]
    sides = []
    for side in range(2):
        parts = []
        for core in range(2):
            lanes = []
            for source in (rows, final):
                for m in range(2):
                    for i in range(2):
                        start = (4 * side + 2 * i + core) * depth
                        lanes.append(source[m, :, start : start + depth])
            parts.append(jnp.concatenate(lanes, axis=1))
        sides.append(jnp.concatenate(parts))
    for by, pack in enumerate(packs):
        pack[:tokens] = keys[...]
        pack[tokens : 2 * tokens] = scaled
        low = jnp.bitwise_xor(my_chip(), by) == LOW
        pack[2 * tokens : 2 * tokens + 2 * depth] = jnp.where(low, sides[0], sides[1])
        if by < 2:
            pack[2 * tokens + 2 * depth : 2 * tokens + 3 * depth] = rows[2]
            pack[2 * tokens + 3 * depth :] = final[2]
    ahead[:tokens] = queries[...]
    ahead[tokens:] = cot[...]


def unpack(packs, mates, own, last, table):
    depth = own.shape[1] // 2
    base = packs[0].shape[0] - 4 * depth
    span = own.shape[1]
    chip, core = my_chip(), my_core()
    for by in range(CHIPS):
        source = jnp.bitwise_xor(chip, by)
        mine = rows_at(base + core * depth, depth)
        table[rows_at((2 * source + core) * depth, depth), :] = packs[by][mine, :]
        table[rows_at((2 * source + 1 - core) * depth, depth), :] = mates[by][mine, :]
    turned = table[...].T
    keep = jnp.where(lax.axis_index("block") == lax.axis_size("block") - 1, 1.0, 0.0)
    own[0], own[1] = turned[:span], turned[span : 2 * span]
    last[0], last[1] = turned[2 * span : 3 * span] * keep, turned[3 * span :] * keep
    low = chip == LOW
    for place, out, scale in ((2 * depth, own, 1.0), (3 * depth, last, keep)):
        cut = slice(base + place, base + place + depth)
        out[2, :depth] = jnp.where(low, packs[1][cut, :], packs[0][cut, :]) * scale
        out[2, depth:] = jnp.where(low, packs[0][cut, :], packs[1][cut, :]) * scale


def forward_body(*refs):
    packs, mates = refs[:CHIPS], refs[CHIPS : 2 * CHIPS]
    own, last, key_high, key_low, scaled_high, scaled_low, kept, shifted, lead, sums, table = refs[2 * CHIPS :]
    pieces = packs + mates
    depth = key_high.shape[0] // len(pieces)
    span = own.shape[1]

    @pl.when(~in_chain())
    def _():
        for out in (own, shifted, lead, sums):
            out[...] = jnp.zeros(out.shape, jnp.float32)

    @pl.when(in_chain())
    def _():
        unpack(packs, mates, own, last, table)
        for index, piece in enumerate(pieces):
            cut = slice(index * depth, (index + 1) * depth)
            key_high[cut, :], key_low[cut, :] = halves(piece[:depth, :])
            scaled_high[cut, :], scaled_low[cut, :] = halves(piece[depth : 2 * depth, :])
        pair = halves(jnp.concatenate([own[0], own[1]]))
        second = halves(own[2])
        grad_pair, grad_second = 0.0, 0.0
        for start in range(0, key_high.shape[0], CHUNK):
            cut = slice(start, start + CHUNK)
            key_cut = key_high[cut, :], key_low[cut, :]
            scaled_cut = scaled_high[cut, :], scaled_low[cut, :]
            both = nt(pair, key_cut)
            d_mixed = nt(second, scaled_cut)
            first, gate = both[:span], both[span:]
            value, d_one, d_two = silu_parts(first)
            for place, array in enumerate((gate, value, d_one, d_two, d_mixed)):
                kept[place, :, cut] = array
            d_pair = jnp.concatenate([d_mixed * gate * d_one, d_mixed * value])
            grad_pair += nn(halves(d_pair), key_cut)
            grad_second += nn(halves(value * gate), scaled_cut)
        moved = own[0] - grad_pair[:span], own[1] - grad_pair[span:], own[2] - grad_second
        rows = []
        for left, right in ((own, own), (moved, moved), (last, moved)):
            rows += [jnp.sum(left[m] * right[m], axis=0, keepdims=True) for m in range(2)]
        sums[...] = jnp.concatenate(rows + [jnp.zeros((2, own.shape[2]), jnp.float32)])
        for m in range(3):
            shifted[m] = moved[m]
        for m in range(2):
            lead[m] = moved[m]


def apply_body(source, own, raw, earlier, *refs):
    pieces, (applied, payload, partial) = refs[:-3], refs[-3:]
    span = own.shape[1]
    depth = pieces[0].shape[0] // 2
    active = (lax.axis_index("block") == source) & in_chain()

    @pl.when(~active)
    def _():
        payload[...] = jnp.zeros(payload.shape, jnp.float32)
        partial[...] = jnp.zeros(partial.shape, jnp.float32)

    @pl.when(in_chain())
    def _():
        pair = halves(jnp.concatenate([own[0], own[1]]))
        second = halves(own[2])
        out_pair, out_second = 0.0, 0.0
        step = CHUNK // depth
        for index in range(0, len(pieces), step):
            query = halves(jnp.concatenate([piece[:depth, :] for piece in pieces[index : index + step]]))
            cot = halves(jnp.concatenate([piece[depth:, :] for piece in pieces[index : index + step]]))
            both = nt(pair, query)
            d_mixed = nt(second, cot)
            first, gate = both[:span], both[span:]
            value, d_one, _ = silu_parts(first)
            out_pair += nn(halves(jnp.concatenate([d_mixed * gate * d_one, d_mixed * value])), query)
            out_second += nn(halves(value * gate), cot)
        applied[: 2 * span] = out_pair
        applied[2 * span :] = out_second

    @pl.when(active)
    def _():
        rows = [raw[m] + applied[m * span : (m + 1) * span, :] for m in range(3)]
        finish(rows, earlier, payload, partial)


def finish(rows, earlier, payload, partial):
    sums = [jnp.sum(rows[m] * earlier[m], axis=0, keepdims=True) for m in range(2)]
    partial[...] = jnp.concatenate(sums + [jnp.zeros((6, rows[0].shape[1]), jnp.float32)])
    for m in range(3):
        payload[m] = rows[m]


def state_terms(own, shifted, last, sums, inners, arrived):
    total = sums[0][...] + sums[1][...] + (sums[2][...] + sums[3][...])
    inner = total[4:6]
    for array in inners:
        inner = inner + array[0:2]
    cots, straights = [], []
    for m in range(3):
        incoming = last[m]
        for array in arrived:
            incoming = incoming + array[m]
        if m < 2:
            dot, old, new = inner[m : m + 1], jnp.sqrt(total[m : m + 1] + EPS), jnp.sqrt(total[m + 2 : m + 3] + EPS)
        else:
            dot = jnp.sum(incoming * shifted[m], axis=-1, keepdims=True)
            old = jnp.sqrt(jnp.sum(own[m] * own[m], axis=-1, keepdims=True) + EPS)
            new = jnp.sqrt(jnp.sum(shifted[m] * shifted[m], axis=-1, keepdims=True) + EPS)
        d_shifted = old / new * incoming - old * dot / (new * new * new) * shifted[m]
        cots.append(-d_shifted)
        straights.append(d_shifted + dot / new * own[m] / old)
    return cots, straights


def section_rows(count, refs):
    own, shifted, last = refs[:3]
    sums, inners, arrived = refs[3:7], refs[7 : 7 + 4 * count], refs[7 + 4 * count : 7 + 5 * count]
    key_high, key_low, scaled_high, scaled_low, kept = refs[7 + 5 * count : 12 + 5 * count]
    span = own.shape[1]
    cots, straights = state_terms(own, shifted, last, sums, inners, arrived)
    pair = halves(jnp.concatenate(cots[:2]))
    second = halves(cots[2])
    d_pair, d_second = 0.0, 0.0
    for start in range(0, key_high.shape[0], CHUNK):
        cut = slice(start, start + CHUNK)
        key_cut = key_high[cut, :], key_low[cut, :]
        scaled_cut = scaled_high[cut, :], scaled_low[cut, :]
        gate, value, d_one, d_two, d_mixed = [kept[place, :, cut] for place in range(5)]
        both = nt(pair, key_cut)
        p_mixed = nt(second, scaled_cut)
        t_first, t_gate = both[:span], both[span:]
        lift = d_one * t_first
        t_mixed = lift * gate + value * t_gate
        c_gate = p_mixed * value + d_mixed * lift
        c_first = p_mixed * gate * d_one + d_mixed * (d_two * t_first * gate + d_one * t_gate)
        d_pair += nn(halves(jnp.concatenate([c_first, c_gate])), key_cut)
        d_second += nn(halves(t_mixed), scaled_cut)
    return cots, [d_pair[:span] + straights[0], d_pair[span:] + straights[1], d_second + straights[2]]


def first_body(source, *refs):
    raw = refs[-1]

    @pl.when((lax.axis_index("block") == source) & in_chain())
    def _():
        _, rows = section_rows(0, refs)
        for m in range(3):
            raw[m] = rows[m]


def section_body(source, *refs):
    applied, earlier, payload, partial = refs[-4:]
    active = (lax.axis_index("block") == source) & in_chain()

    @pl.when(~active)
    def _():
        payload[...] = jnp.zeros(payload.shape, jnp.float32)
        partial[...] = jnp.zeros(partial.shape, jnp.float32)

    @pl.when(active)
    def _():
        span = payload.shape[1]
        _, rows = section_rows(1, refs)
        finish([row + applied[m * span : (m + 1) * span, :] for m, row in enumerate(rows)], earlier, payload, partial)


def terms_body(count, *refs):
    cot = refs[-1]
    span = refs[0].shape[1]

    @pl.when(~in_chain())
    def _():
        cot[...] = jnp.zeros(cot.shape, jnp.float32)

    @pl.when(in_chain())
    def _():
        cots, _ = state_terms(*refs[:3], refs[3:7], refs[7 : 7 + 4 * count], refs[7 + 4 * count : 7 + 5 * count])
        for m in range(3):
            cot[m * span : (m + 1) * span, :] = cots[m]


def final_body(count, *refs):
    applied, outs, table = refs[-6], refs[-5:-1], refs[-1]
    span = refs[0].shape[1]
    depth = span // 2
    chip = my_chip()

    @pl.when(~in_chain())
    def _():
        for out in outs:
            out[...] = jnp.zeros(out.shape, jnp.float32)

    @pl.when(in_chain())
    def _():
        cots, rows = section_rows(count, refs)
        rows = [row + applied[m * span : (m + 1) * span, :] for m, row in enumerate(rows)]
        table[...] = jnp.concatenate(rows[:2]).T
        for m in range(3):
            outs[2][m * span : (m + 1) * span, :] = cots[m]
        for by, (out, place) in enumerate(zip(outs, (0, 0, 3 * span, 0))):
            start = jnp.bitwise_xor(chip, by) * 2 * depth
            for core in range(2):
                lanes = slice(core * 128, (core + 1) * 128)
                out[place : place + depth, lanes] = table[rows_at(start + core * depth, depth), :]
        low = chip == LOW
        upper, lower = rows[2][:depth], rows[2][depth:]
        outs[0][depth:] = jnp.where(low, lower, upper)
        outs[1][depth:] = jnp.where(low, upper, lower)


def joined(refs):
    return [[refs[i], refs[i + 1]] for i in range(0, 8, 2)]


def taken(pair, cut):
    return pair[0][cut, :] + pair[1][cut, :]


def load_halves(pieces, part, span):
    return halves(jnp.concatenate([taken(pair, slice(part * span, (part + 1) * span)) for pair in pieces]))


def query_body(queries, out_cot, keys, values, rates, *refs):
    pieces = joined(refs[:8])
    d_queries, kept, high, low, key_high, key_low, scaled_high, scaled_low = refs[8:]
    span = queries.shape[1] // len(pieces)
    weights = [load_halves(pieces, part, span) for part in range(3)]
    for part in range(3):
        high[part], low[part] = weights[part]
    one, three, two = weights
    query, cot = halves(queries[...]), halves(out_cot[...])
    first, gate = nt(query, one), nt(query, three)
    value, d_one, _ = silu_parts(first)
    d_mixed = nt(cot, two)
    d_queries[...] = nn(halves(d_mixed * gate * d_one), one) + nn(halves(d_mixed * value), three)
    key, scaled = halves(keys[...]), halves(-column(rates[...], keys.shape[1]) * values[...])
    key_high[...], key_low[...] = key
    scaled_high[...], scaled_low[...] = scaled
    first, gate = nt(key, one), nt(key, three)
    value, d_one, d_two = silu_parts(first)
    for place, array in enumerate((gate, value, d_one, d_two, nt(scaled, two))):
        kept[place] = array


def token_body(values, rates, kept, high, low, key_high, key_low, scaled_high, scaled_low, *refs):
    cots = [[refs[i], refs[i + 1]] for i in (0, 2, 7, 9)]
    ends = [refs[4:7], refs[11:14]]
    d_keys, d_values, d_rates, d_rows = refs[14:]
    width = values.shape[1]
    span = width // len(cots)
    one, three, two = [(high[part], low[part]) for part in range(3)]
    c_one, c_three, c_two = [load_halves(cots, part, span) for part in range(3)]
    key, scaled = (key_high[...], key_low[...]), (scaled_high[...], scaled_low[...])
    gate, value, d_one, d_two, d_mixed = [kept[place] for place in range(5)]
    t_first, t_gate, p_mixed = nt(key, c_one), nt(key, c_three), nt(scaled, c_two)
    d_gate = d_mixed * value
    d_first = d_mixed * gate * d_one
    lift = d_one * t_first
    t_mixed = lift * gate + value * t_gate
    c_gate = p_mixed * value + d_mixed * lift
    c_first = p_mixed * gate * d_one + d_mixed * (d_two * t_first * gate + d_one * t_gate)
    d_keys[...] = nn(halves(c_first), one) + nn(halves(c_gate), three) + nn(halves(d_first), c_one) + nn(halves(d_gate), c_three)
    t_out = nn(halves(t_mixed), two) + nn(halves(value * gate), c_two)
    d_values[...] = -column(rates[...], width) * t_out
    d_rates[...] = -jnp.sum((values[...] * t_out).T, axis=0, keepdims=True)
    depth = d_rows.shape[1]
    low_side, upper_core = my_chip() <= LOW, my_core() == 0
    sides = []
    for (own, beside, across), (_, far) in zip(ends, cots[1::2]):
        near, far = own[:depth] + beside[:depth], across[...] + far[3 * span :]
        near, far = [jnp.where(upper_core, piece[:, :128], piece[:, 128:]) for piece in (near, far)]
        sides.append([jnp.where(low_side, near, far), jnp.where(low_side, far, near)])
    by_core = [[jnp.where(upper_core, a, b) for a, b in zip(*sides)], [jnp.where(upper_core, b, a) for a, b in zip(*sides)]]
    for m in range(2):
        parts = []
        for side in range(2):
            for i in range(2):
                for core in range(2):
                    start = (2 * m + i) * depth
                    parts.append(by_core[core][side][:, start : start + depth])
        d_rows[m] = jnp.concatenate(parts, axis=1)
    d_rows[2] = ends[0][0][depth:] + ends[0][1][depth:]


def over_chips(array, moves):
    pairs = [(2 * a + core, 2 * b + (core if a != b else 1 - core)) for a, b in enumerate(moves) for core in range(2)]
    return lax.ppermute(array, "tok", pairs)


def by_xor(array, by):
    return over_chips(array, [chip ^ by for chip in range(CHIPS)])


ACROSS = (0, 2, 1, 3)
INWARD = (2, 0, 3, 1)
OUTWARD = (1, 3, 0, 2)


def exchanged(array):
    turned = [(2 * a + core, 2 * b + 1 - core) for a, b in enumerate(ACROSS) for core in range(2)]
    return [array, over_chips(array, ACROSS), lax.ppermute(array, "tok", turned), core_swap(array)]


def both_cores(pieces):
    swapped = [core_swap(pieces[0])]
    for piece in pieces[1:]:
        swapped.append(core_swap(piece))
    return pieces + swapped


def hops(arrays, far):
    first = by_xor(arrays[1], 1)
    second = over_chips(arrays[2], far)
    third = over_chips(arrays[3], ACROSS)
    return first, second, third


def to_chain(arrays):
    return both_cores([arrays[0], *hops(arrays, INWARD)])


def from_chain_relayed(array):
    near = by_xor(array, 1)
    across = over_chips(array, ACROSS)
    far = by_xor(across, 1)
    return both_cores([array, near, across, far])


def to_earlier(array):
    groups = lax.axis_size("block")
    return lax.ppermute(array, "block", [(i, (i - 1) % groups) for i in range(groups)])


def to_later(array):
    groups = lax.axis_size("block")
    return lax.ppermute(array, "block", [(i, (i + 1) % groups) for i in range(groups)])


def per_device(queries, keys, values, rates, states, out_cot, final_cot):
    groups, size = lax.axis_size("block"), lax.axis_size("tok")
    depth, width = keys.shape
    own_rows = states[0]
    rows = own_rows.shape[1]
    if not (size == 2 * CHIPS and 4 * rows == 128 and depth == 128 and width == 8 * rows):
        return per_device_general(queries, keys, values, rates, states, out_cot, final_cot)
    span, tokens = 2 * rows, depth * size
    rates_row = rates.reshape(1, depth)
    state, square, wide = f32(3, span, width), f32(depth, width), f32(3 * span, width)
    sources = (keys, values, rates_row, own_rows, final_cot, queries, out_cot)
    longer, shorter = f32(2 * depth + 4 * rows, width), f32(2 * depth + 2 * rows, width)
    *packs, ahead = kernel_call(
        pack_body,
        [longer, longer, shorter, shorter, f32(2 * depth, width)],
        *sources,
        scratch=[pltpu.VMEM(array.shape, array.dtype) for array in sources] + [pltpu.SemaphoreType.DMA((len(sources),))],
        raw=True,
        limit=PACK_LIMIT,
    )
    pieces = to_chain(packs)
    ahead_pieces = to_chain([ahead] * CHIPS)
    half = bf16(tokens, width)
    own, last, *halved, kept, shifted, lead, sums = kernel_call(
        forward_body,
        [state, state, half, half, half, half, f32(5, span, tokens), state, f32(2, span, width), f32(8, width)],
        *pieces,
        scratch=[pltpu.VMEM((width, 4 * span), jnp.float32)],
    )
    all_sums = exchanged(sums)
    earlier = to_later(lead)
    weights = from_chain_relayed(own.reshape(3 * span, width))

    inners, arrived = [], []
    common = [own, shifted, last, *all_sums]
    sent = [state, f32(8, width)]
    (raw,) = kernel_call(functools.partial(first_body, groups - 1), [state], *common, *halved, kept)
    for section in range(groups - 1):
        source = groups - 1 - section
        if section == 0:
            body = functools.partial(apply_body, source)
            applied, payload, partial = kernel_call(body, [wide] + sent, own, raw, earlier, *ahead_pieces)
        else:
            body = functools.partial(section_body, source)
            payload, partial = kernel_call(
                body, sent, *common, *inners[-4:], *arrived[-1:], *halved, kept, applied, earlier
            )
        straight = to_earlier(partial)
        arrived.append(to_earlier(payload))
        inners += exchanged(straight)
    received = [*common, *inners, *arrived]
    (cot,) = kernel_call(functools.partial(terms_body, groups - 1), [wide], *received)
    near = by_xor(cot, 1)
    across = over_chips(cot, ACROSS)
    own_end, near_end, far, across_end = kernel_call(
        functools.partial(final_body, groups - 1),
        [f32(2 * rows, width)] * 2 + [f32(3 * span + rows, width), f32(rows, width)],
        *received,
        *halved,
        kept,
        applied,
        scratch=[pltpu.VMEM((width, 128), jnp.float32)],
    )
    near_end = by_xor(near_end, 1)
    across_end = over_chips(across_end, ACROSS)
    far = over_chips(far, OUTWARD)
    cots = [cot, near, across, far, own_end, near_end, across_end]
    swapped = []
    for piece in cots:
        swapped.append(core_swap(piece))
    cots = cots + swapped
    small, whole = bf16(depth, width), bf16(3, width, width)
    d_queries, *saved = kernel_call(
        query_body,
        [square, f32(5, depth, width), whole, whole, small, small, small, small],
        queries,
        out_cot,
        keys,
        values,
        rates_row,
        *weights,
        spill=1,
    )
    d_keys, d_values, d_rates, d_rows = kernel_call(
        token_body, [square, square, f32(1, depth), f32(3, rows, width)], values, rates_row, *saved, *cots, spill=4
    )
    return (d_queries, d_keys, d_values, d_rates.reshape(depth), d_rows[None])


def solution(mesh):
    return jax.shard_map(
        per_device,
        mesh=mesh,
        in_specs=(
            P(("block", "tok"), None),
            P(("block", "tok"), None),
            P(("block", "tok"), None),
            P(("block", "tok")),
            P("block", None, "tok", None),
            P(("block", "tok"), None),
            P(None, "tok", None),
        ),
        out_specs=(
            P(("block", "tok"), None),
            P(("block", "tok"), None),
            P(("block", "tok"), None),
            P(("block", "tok")),
            P("block", None, "tok", None),
        ),
        check_vma=False,
    )
```

```python
import functools

import jax
import jax.numpy as jnp
from jax import lax
from jax.experimental import pallas as pl
from jax.experimental.pallas import tpu as pltpu
from jax.sharding import PartitionSpec as P


EPS = 1e-06
HIGH = lax.Precision.HIGHEST


def mm(left, right):
    return lax.dot_general(left, right, (((1,), (0,)), ((), ())), precision=HIGH, preferred_element_type=jnp.float32)


def mm_nt(left, right):
    return lax.dot_general(left, right, (((1,), (1,)), ((), ())), precision=HIGH, preferred_element_type=jnp.float32)


def mm_tn(left, right):
    return lax.dot_general(left, right, (((0,), (0,)), ((), ())), precision=HIGH, preferred_element_type=jnp.float32)


def silu_parts(first):
    sig = 1.0 / (1.0 + jnp.exp(-first))
    slope = sig * (1.0 - sig)
    value = first * sig
    d_one = sig + first * slope
    d_two = slope * (2.0 + first * (1.0 - 2.0 * sig))
    return value, d_one, d_two


def direct(size):
    return size % 2 == 0 and size <= 16


def chip_shift(array, by):
    size = lax.axis_size("tok")
    return lax.ppermute(array, "tok", [(j, (j + 2 * by) % size) for j in range(size)])


def core_swap(array):
    size = lax.axis_size("tok")
    return lax.ppermute(array, "tok", [(j, j ^ 1) for j in range(size)])


def gather_pieces(array):
    size = lax.axis_size("tok")
    if not direct(size):
        return lax.all_gather(array, "tok")
    mine = jnp.stack([array] + [chip_shift(array, by) for by in range(1, size // 2)])
    return jnp.concatenate([mine, core_swap(mine)])


def spread_sum(pieces):
    size = lax.axis_size("tok")
    if not direct(size):
        return lax.psum_scatter(pieces, "tok")
    half = size // 2
    mine = pieces[:half] + core_swap(pieces[half:])
    total = mine[0]
    for by in range(1, half):
        total = total + chip_shift(mine[by], -by)
    return total


def sum_all(array):
    size = lax.axis_size("tok")
    if not direct(size):
        return jnp.sum(lax.all_gather(array, "tok"), axis=0)
    array = array + core_swap(array)
    total = array
    for by in range(1, size // 2):
        total = total + chip_shift(array, by)
    return total


def rows_to_hidden(rows):
    size = lax.axis_size("tok")
    count, depth, width = rows.shape
    parts = rows.reshape(count, depth, size, width // size).transpose(2, 0, 3, 1)
    parts = lax.all_to_all(parts, "tok", 0, 0)
    return parts.transpose(1, 2, 0, 3).reshape(count, width // size, depth * size)


def hidden_to_rows(slices):
    size = lax.axis_size("tok")
    count, depth, width = slices.shape
    parts = slices.reshape(count, depth, size, width // size).transpose(2, 0, 1, 3)
    parts = lax.all_to_all(parts, "tok", 0, 0)
    return parts.transpose(1, 3, 0, 2).reshape(count, width // size, depth * size)


def to_block(array, source, target, by=0):
    size = lax.axis_size("tok")
    pairs = [(source * size + j, target * size + (j + by) % size) for j in range(size)]
    return lax.ppermute(array, ("block", "tok"), pairs)


def up_one(array):
    groups = lax.axis_size("block")
    return lax.ppermute(array, "block", [(i, i + 1) for i in range(groups - 1)])


def slice_forward(weights, keys, scaled):
    first, gate = mm_nt(weights[0], keys), mm_nt(weights[1], keys)
    value, d_one, d_two = silu_parts(first)
    d_mixed = mm_nt(weights[2], scaled)
    mixed = value * gate
    d_gate = d_mixed * value
    d_first = d_mixed * gate * d_one
    grads = jnp.stack([mm(d_first, keys), mm(d_gate, keys), mm(mixed, scaled)])
    return grads, (gate, value, d_one, d_two, d_mixed)


def slice_adjoint(cot, kept, keys, scaled):
    gate, value, d_one, d_two, d_mixed = kept
    t_first, t_gate, p_mixed = mm_nt(cot[0], keys), mm_nt(cot[1], keys), mm_nt(cot[2], scaled)
    t_mixed = d_one * t_first * gate + value * t_gate
    c_gate = p_mixed * value + d_mixed * d_one * t_first
    c_first = p_mixed * gate * d_one + d_mixed * (d_two * t_first * gate + d_one * t_gate)
    return jnp.stack([mm(c_first, keys), mm(c_gate, keys), mm(t_mixed, scaled)])


def query_adjoint(weights, queries, out_cot):
    first, gate = mm_nt(queries, weights[0]), mm_nt(queries, weights[1])
    value, d_one, _ = silu_parts(first)
    d_mixed = mm_nt(out_cot, weights[2])
    d_gate = d_mixed * value
    d_first = d_mixed * gate * d_one
    d_queries = mm(d_first, weights[0]) + mm(d_gate, weights[1])
    d_weights = jnp.stack([mm_tn(d_first, queries), mm_tn(d_gate, queries), mm_tn(value * gate, out_cot)])
    return d_queries, d_weights


def token_adjoint(weights, cot, keys, scaled):
    first, gate = mm_nt(keys, weights[0]), mm_nt(keys, weights[1])
    value, d_one, d_two = silu_parts(first)
    d_mixed = mm_nt(scaled, weights[2])
    mixed = value * gate
    d_gate = d_mixed * value
    d_first = d_mixed * gate * d_one
    t_first, t_gate, p_mixed = mm_nt(keys, cot[0]), mm_nt(keys, cot[1]), mm_nt(scaled, cot[2])
    t_mixed = d_one * t_first * gate + value * t_gate
    c_gate = p_mixed * value + d_mixed * d_one * t_first
    c_first = p_mixed * gate * d_one + d_mixed * (d_two * t_first * gate + d_one * t_gate)
    d_keys = mm(c_first, weights[0]) + mm(c_gate, weights[1]) + mm(d_first, cot[0]) + mm(d_gate, cot[1])
    t_out = mm(t_mixed, weights[2]) + mm(mixed, cot[2])
    return d_keys, t_out


def over_hidden(array):
    return jnp.sum(array[:2], axis=1)


def per_device_general(queries, keys, values, rates, states, out_cot, final_cot):
    groups, size = lax.axis_size("block"), lax.axis_size("tok")
    position = lax.axis_index("block")
    own_rows = states[0]
    scaled = -rates[:, None] * values
    both = gather_pieces(jnp.stack([keys, scaled]))
    width = keys.shape[1]
    all_keys = both[:, 0].reshape(-1, width)
    all_scaled = both[:, 1].reshape(-1, width)
    split = rows_to_hidden(jnp.concatenate([own_rows[:2], final_cot[:2]]))
    own = jnp.concatenate([split[:2], own_rows[2:]])
    last = jnp.concatenate([split[2:], final_cot[2:]])
    grads, kept = slice_forward(own, all_keys, all_scaled)
    shifted = own - grads
    earlier = up_one(shifted[:2])
    sums = sum_all(jnp.concatenate([over_hidden(own * own), over_hidden(shifted * shifted), over_hidden(last * shifted)]))
    row_norm = [jnp.sqrt(sums[0:2, None, :] + EPS), jnp.sqrt(jnp.sum(own[2:] ** 2, axis=-1, keepdims=True) + EPS)]
    new_norm = [jnp.sqrt(sums[2:4, None, :] + EPS), jnp.sqrt(jnp.sum(shifted[2:] ** 2, axis=-1, keepdims=True) + EPS)]

    pieces = gather_pieces(own)
    whole = pieces.transpose(1, 0, 2, 3).reshape(3, -1, width)
    d_queries, d_weights = query_adjoint(whole, queries, out_cot)
    apply_state = spread_sum(d_weights.reshape(3, size, -1, width).transpose(1, 0, 2, 3))

    is_last = position == groups - 1
    incoming = jnp.where(is_last, last, 0.0)
    inner = jnp.where(is_last, sums[4:6], 0.0)
    for section in range(groups):
        inners = [inner[:, None, :], jnp.sum(incoming[2:] * shifted[2:], axis=-1, keepdims=True)]
        cots, straights = [], []
        for part, dot, old, new in zip((slice(0, 2), slice(2, 3)), inners, row_norm, new_norm):
            d_shifted = old / new * incoming[part] - old * dot / (new * new * new) * shifted[part]
            cots.append(-d_shifted)
            straights.append(d_shifted + dot / new * own[part] / old)
        cot = jnp.concatenate(cots)
        straight = jnp.concatenate(straights)
        rows_now = slice_adjoint(cot, kept, all_keys, all_scaled) + apply_state + straight
        if section + 1 < groups:
            source = groups - 1 - section
            partial = over_hidden(rows_now[:2] * earlier)
            incoming = incoming + to_block(rows_now, source, source - 1)
            if direct(size):
                for by in range(size):
                    inner = inner + to_block(partial, source, source - 1, by)
            else:
                inner = inner + to_block(sum_all(partial), source, source - 1)
    cot_pieces = gather_pieces(cot)
    whole_cot = cot_pieces.transpose(1, 0, 2, 3).reshape(3, -1, width)
    d_keys, t_out = token_adjoint(whole, whole_cot, keys, scaled)
    d_values = -rates[:, None] * t_out
    d_rates = -jnp.sum(values * t_out, axis=-1)
    d_rows = jnp.concatenate([hidden_to_rows(rows_now[:2]), rows_now[2:]])
    return (d_queries, d_keys, d_values, d_rates, d_rows[None])


def halves(array):
    upper = array.astype(jnp.bfloat16)
    return upper, (array - upper.astype(jnp.float32)).astype(jnp.bfloat16)


def product(left, right, contract):
    def one(a, b):
        return lax.dot_general(a, b, (((1,), (contract,)), ((), ())), preferred_element_type=jnp.float32)

    rows = left[0].shape[0]
    upper = one(jnp.concatenate(left), right[0])
    return upper[:rows] + (upper[rows:] + one(left[0], right[1]))


def nn(left, right):
    return product(left, right, 0)


def nt(left, right):
    return product(left, right, 1)


def kernel_call(body, outs, *operands, scratch=(), raw=False, spill=0, limit=24 * 1024 * 1024):
    space = pltpu.MemorySpace.HBM if raw else pltpu.VMEM
    return pl.pallas_call(
        body,
        in_specs=[pl.BlockSpec(memory_space=space) for _ in operands],
        out_specs=[pl.BlockSpec(memory_space=pltpu.VMEM) for _ in outs],
        out_shape=[(jax.ShapeDtypeStruct if i < spill else pltpu.VMEM)(*out) for i, out in enumerate(outs)],
        scratch_shapes=list(scratch),
        compiler_params=pltpu.CompilerParams(vmem_limit_bytes=limit),
    )(*operands)


def my_chip():
    return lax.div(lax.axis_index("tok"), 2)


def my_core():
    return lax.rem(lax.axis_index("tok"), 2)


def in_chain():
    return (my_chip() == LOW) | (my_chip() == HIGH_CHIP)


def f32(*shape):
    return shape, jnp.float32


def bf16(*shape):
    return shape, jnp.bfloat16


def column(row, width):
    block = jnp.broadcast_to(row, (128, row.shape[1])).T
    return jnp.concatenate([block] * (width // 128), axis=1)


CHIPS = 4
LOW, HIGH_CHIP = 1, 2
CHUNK = 1024
PACK_LIMIT = 61 * 1024 * 1024


def rows_at(start, count):
    return pl.ds(pl.multiple_of(start, count), count)


def pack_body(*refs):
    count = 7
    sources, outs = refs[:count], refs[count : count + CHIPS + 1]
    buffers, sems = refs[count + CHIPS + 1 : -1], refs[-1]
    copies = [pltpu.make_async_copy(a, b, sems.at[i]) for i, (a, b) in enumerate(zip(sources, buffers))]
    for index in (3, 4, 0, 1, 2, 5, 6):
        copies[index].start()
    keys, values, rates, rows, final, queries, cot = buffers
    packs, ahead = outs[:CHIPS], outs[CHIPS]
    tokens = keys.shape[0]
    depth = rows.shape[1]
    for copy in copies[3:5]:
        copy.wait()
    sides = []
    for side in range(2):
        parts = []
        for core in range(2):
            lanes = []
            for source in (rows, final):
                for m in range(2):
                    for i in range(2):
                        start = (4 * side + 2 * i + core) * depth
                        lanes.append(source[m, :, start : start + depth])
            parts.append(jnp.concatenate(lanes, axis=1))
        sides.append(jnp.concatenate(parts))
    for copy in copies[:3]:
        copy.wait()
    scaled = -column(rates[...], values.shape[1]) * values[...]
    for by, pack in enumerate(packs):
        pack[:tokens] = keys[...]
        pack[tokens : 2 * tokens] = scaled
        low = jnp.bitwise_xor(my_chip(), by) == LOW
        pack[2 * tokens : 2 * tokens + 2 * depth] = jnp.where(low, sides[0], sides[1])
        if by < 2:
            pack[2 * tokens + 2 * depth : 2 * tokens + 3 * depth] = rows[2]
            pack[2 * tokens + 3 * depth :] = final[2]
    for copy in copies[5:]:
        copy.wait()
    ahead[:tokens] = queries[...]
    ahead[tokens:] = cot[...]


def unpack(packs, mates, own, last, table):
    depth = own.shape[1] // 2
    base = packs[0].shape[0] - 4 * depth
    span = own.shape[1]
    chip, core = my_chip(), my_core()
    for by in range(CHIPS):
        source = jnp.bitwise_xor(chip, by)
        mine = rows_at(base + core * depth, depth)
        table[rows_at((2 * source + core) * depth, depth), :] = packs[by][mine, :]
        table[rows_at((2 * source + 1 - core) * depth, depth), :] = mates[by][mine, :]
    turned = table[...].T
    keep = jnp.where(lax.axis_index("block") == lax.axis_size("block") - 1, 1.0, 0.0)
    own[0], own[1] = turned[:span], turned[span : 2 * span]
    last[0], last[1] = turned[2 * span : 3 * span] * keep, turned[3 * span :] * keep
    low = chip == LOW
    for place, out, scale in ((2 * depth, own, 1.0), (3 * depth, last, keep)):
        cut = slice(base + place, base + place + depth)
        out[2, :depth] = jnp.where(low, packs[1][cut, :], packs[0][cut, :]) * scale
        out[2, depth:] = jnp.where(low, packs[0][cut, :], packs[1][cut, :]) * scale


def forward_body(*refs):
    packs, mates = refs[:CHIPS], refs[CHIPS : 2 * CHIPS]
    own, last, key_high, key_low, scaled_high, scaled_low, kept, shifted, lead, sums, table = refs[2 * CHIPS :]
    pieces = packs + mates
    depth = key_high.shape[0] // len(pieces)
    span = own.shape[1]

    @pl.when(~in_chain())
    def _():
        for out in (own, shifted, lead, sums):
            out[...] = jnp.zeros(out.shape, jnp.float32)

    @pl.when(in_chain())
    def _():
        unpack(packs, mates, own, last, table)
        for index, piece in enumerate(pieces):
            cut = slice(index * depth, (index + 1) * depth)
            key_high[cut, :], key_low[cut, :] = halves(piece[:depth, :])
            scaled_high[cut, :], scaled_low[cut, :] = halves(piece[depth : 2 * depth, :])
        pair = halves(jnp.concatenate([own[0], own[1]]))
        second = halves(own[2])
        grad_pair, grad_second = 0.0, 0.0
        for start in range(0, key_high.shape[0], CHUNK):
            cut = slice(start, start + CHUNK)
            key_cut = key_high[cut, :], key_low[cut, :]
            scaled_cut = scaled_high[cut, :], scaled_low[cut, :]
            both = nt(pair, key_cut)
            d_mixed = nt(second, scaled_cut)
            first, gate = both[:span], both[span:]
            value, d_one, d_two = silu_parts(first)
            for place, array in enumerate((gate, value, d_one, d_two, d_mixed)):
                kept[place, :, cut] = array
            d_pair = jnp.concatenate([d_mixed * gate * d_one, d_mixed * value])
            grad_pair += nn(halves(d_pair), key_cut)
            grad_second += nn(halves(value * gate), scaled_cut)
        moved = own[0] - grad_pair[:span], own[1] - grad_pair[span:], own[2] - grad_second
        rows = []
        for left, right in ((own, own), (moved, moved), (last, moved)):
            rows += [jnp.sum(left[m] * right[m], axis=0, keepdims=True) for m in range(2)]
        sums[...] = jnp.concatenate(rows + [jnp.zeros((2, own.shape[2]), jnp.float32)])
        for m in range(3):
            shifted[m] = moved[m]
        for m in range(2):
            lead[m] = moved[m]


def apply_body(source, own, raw, earlier, *refs):
    pieces, (applied, payload, partial) = refs[:-3], refs[-3:]
    span = own.shape[1]
    depth = pieces[0].shape[0] // 2
    active = (lax.axis_index("block") == source) & in_chain()

    @pl.when(~active)
    def _():
        payload[...] = jnp.zeros(payload.shape, jnp.float32)
        partial[...] = jnp.zeros(partial.shape, jnp.float32)

    @pl.when(in_chain())
    def _():
        pair = halves(jnp.concatenate([own[0], own[1]]))
        second = halves(own[2])
        out_pair, out_second = 0.0, 0.0
        step = CHUNK // depth
        for index in range(0, len(pieces), step):
            query = halves(jnp.concatenate([piece[:depth, :] for piece in pieces[index : index + step]]))
            cot = halves(jnp.concatenate([piece[depth:, :] for piece in pieces[index : index + step]]))
            both = nt(pair, query)
            d_mixed = nt(second, cot)
            first, gate = both[:span], both[span:]
            value, d_one, _ = silu_parts(first)
            out_pair += nn(halves(jnp.concatenate([d_mixed * gate * d_one, d_mixed * value])), query)
            out_second += nn(halves(value * gate), cot)
        applied[: 2 * span] = out_pair
        applied[2 * span :] = out_second

    @pl.when(active)
    def _():
        rows = [raw[m] + applied[m * span : (m + 1) * span, :] for m in range(3)]
        finish(rows, earlier, payload, partial)


def finish(rows, earlier, payload, partial):
    sums = [jnp.sum(rows[m] * earlier[m], axis=0, keepdims=True) for m in range(2)]
    partial[...] = jnp.concatenate(sums + [jnp.zeros((6, rows[0].shape[1]), jnp.float32)])
    for m in range(3):
        payload[m] = rows[m]


def state_terms(own, shifted, last, sums, inners, arrived):
    total = sums[0][...] + sums[1][...] + (sums[2][...] + sums[3][...])
    inner = total[4:6]
    for array in inners:
        inner = inner + array[0:2]
    cots, straights = [], []
    for m in range(3):
        incoming = last[m]
        for array in arrived:
            incoming = incoming + array[m]
        if m < 2:
            dot, old, new = inner[m : m + 1], jnp.sqrt(total[m : m + 1] + EPS), jnp.sqrt(total[m + 2 : m + 3] + EPS)
        else:
            dot = jnp.sum(incoming * shifted[m], axis=-1, keepdims=True)
            old = jnp.sqrt(jnp.sum(own[m] * own[m], axis=-1, keepdims=True) + EPS)
            new = jnp.sqrt(jnp.sum(shifted[m] * shifted[m], axis=-1, keepdims=True) + EPS)
        d_shifted = old / new * incoming - old * dot / (new * new * new) * shifted[m]
        cots.append(-d_shifted)
        straights.append(d_shifted + dot / new * own[m] / old)
    return cots, straights


def section_rows(count, refs):
    own, shifted, last = refs[:3]
    sums, inners, arrived = refs[3:7], refs[7 : 7 + 4 * count], refs[7 + 4 * count : 7 + 5 * count]
    key_high, key_low, scaled_high, scaled_low, kept = refs[7 + 5 * count : 12 + 5 * count]
    span = own.shape[1]
    cots, straights = state_terms(own, shifted, last, sums, inners, arrived)
    pair = halves(jnp.concatenate(cots[:2]))
    second = halves(cots[2])
    d_pair, d_second = 0.0, 0.0
    for start in range(0, key_high.shape[0], CHUNK):
        cut = slice(start, start + CHUNK)
        key_cut = key_high[cut, :], key_low[cut, :]
        scaled_cut = scaled_high[cut, :], scaled_low[cut, :]
        gate, value, d_one, d_two, d_mixed = [kept[place, :, cut] for place in range(5)]
        both = nt(pair, key_cut)
        p_mixed = nt(second, scaled_cut)
        t_first, t_gate = both[:span], both[span:]
        lift = d_one * t_first
        t_mixed = lift * gate + value * t_gate
        c_gate = p_mixed * value + d_mixed * lift
        c_first = p_mixed * gate * d_one + d_mixed * (d_two * t_first * gate + d_one * t_gate)
        d_pair += nn(halves(jnp.concatenate([c_first, c_gate])), key_cut)
        d_second += nn(halves(t_mixed), scaled_cut)
    return cots, [d_pair[:span] + straights[0], d_pair[span:] + straights[1], d_second + straights[2]]


def first_body(source, *refs):
    raw = refs[-1]

    @pl.when((lax.axis_index("block") == source) & in_chain())
    def _():
        _, rows = section_rows(0, refs)
        for m in range(3):
            raw[m] = rows[m]


def section_body(source, *refs):
    applied, earlier, payload, partial = refs[-4:]
    active = (lax.axis_index("block") == source) & in_chain()

    @pl.when(~active)
    def _():
        payload[...] = jnp.zeros(payload.shape, jnp.float32)
        partial[...] = jnp.zeros(partial.shape, jnp.float32)

    @pl.when(active)
    def _():
        span = payload.shape[1]
        _, rows = section_rows(1, refs)
        finish([row + applied[m * span : (m + 1) * span, :] for m, row in enumerate(rows)], earlier, payload, partial)


def terms_body(count, *refs):
    cot = refs[-1]
    span = refs[0].shape[1]

    @pl.when(~in_chain())
    def _():
        cot[...] = jnp.zeros(cot.shape, jnp.float32)

    @pl.when(in_chain())
    def _():
        cots, _ = state_terms(*refs[:3], refs[3:7], refs[7 : 7 + 4 * count], refs[7 + 4 * count : 7 + 5 * count])
        for m in range(3):
            cot[m * span : (m + 1) * span, :] = cots[m]


def final_body(count, *refs):
    applied, outs, table = refs[-6], refs[-5:-1], refs[-1]
    span = refs[0].shape[1]
    depth = span // 2
    chip = my_chip()

    @pl.when(~in_chain())
    def _():
        for out in outs:
            out[...] = jnp.zeros(out.shape, jnp.float32)

    @pl.when(in_chain())
    def _():
        cots, rows = section_rows(count, refs)
        rows = [row + applied[m * span : (m + 1) * span, :] for m, row in enumerate(rows)]
        table[...] = jnp.concatenate(rows[:2]).T
        for m in range(3):
            outs[2][m * span : (m + 1) * span, :] = cots[m]
        for by, (out, place) in enumerate(zip(outs, (0, 0, 3 * span, 0))):
            start = jnp.bitwise_xor(chip, by) * 2 * depth
            for core in range(2):
                lanes = slice(core * 128, (core + 1) * 128)
                out[place : place + depth, lanes] = table[rows_at(start + core * depth, depth), :]
        low = chip == LOW
        upper, lower = rows[2][:depth], rows[2][depth:]
        outs[0][depth:] = jnp.where(low, lower, upper)
        outs[1][depth:] = jnp.where(low, upper, lower)


def joined(refs):
    return [[refs[i], refs[i + 1]] for i in range(0, 8, 2)]


def taken(pair, cut):
    return pair[0][cut, :] + pair[1][cut, :]


def load_halves(pieces, part, span):
    return halves(jnp.concatenate([taken(pair, slice(part * span, (part + 1) * span)) for pair in pieces]))


def query_body(queries, out_cot, keys, values, rates, *refs):
    pieces = joined(refs[:8])
    d_queries, kept, high, low, key_high, key_low, scaled_high, scaled_low = refs[8:]
    span = queries.shape[1] // len(pieces)
    weights = [load_halves(pieces, part, span) for part in range(3)]
    for part in range(3):
        high[part], low[part] = weights[part]
    one, three, two = weights
    query, cot = halves(queries[...]), halves(out_cot[...])
    first, gate = nt(query, one), nt(query, three)
    value, d_one, _ = silu_parts(first)
    d_mixed = nt(cot, two)
    d_queries[...] = nn(halves(d_mixed * gate * d_one), one) + nn(halves(d_mixed * value), three)
    key, scaled = halves(keys[...]), halves(-column(rates[...], keys.shape[1]) * values[...])
    key_high[...], key_low[...] = key
    scaled_high[...], scaled_low[...] = scaled
    first, gate = nt(key, one), nt(key, three)
    value, d_one, d_two = silu_parts(first)
    for place, array in enumerate((gate, value, d_one, d_two, nt(scaled, two))):
        kept[place] = array


def token_body(values, rates, kept, high, low, key_high, key_low, scaled_high, scaled_low, *refs):
    cots = [[refs[i], refs[i + 1]] for i in (0, 2, 7, 9)]
    ends = [refs[4:7], refs[11:14]]
    d_keys, d_values, d_rates, d_rows = refs[14:]
    width = values.shape[1]
    span = width // len(cots)
    one, three, two = [(high[part], low[part]) for part in range(3)]
    c_one, c_three, c_two = [load_halves(cots, part, span) for part in range(3)]
    key, scaled = (key_high[...], key_low[...]), (scaled_high[...], scaled_low[...])
    gate, value, d_one, d_two, d_mixed = [kept[place] for place in range(5)]
    t_first, t_gate, p_mixed = nt(key, c_one), nt(key, c_three), nt(scaled, c_two)
    d_gate = d_mixed * value
    d_first = d_mixed * gate * d_one
    lift = d_one * t_first
    t_mixed = lift * gate + value * t_gate
    c_gate = p_mixed * value + d_mixed * lift
    c_first = p_mixed * gate * d_one + d_mixed * (d_two * t_first * gate + d_one * t_gate)
    d_keys[...] = nn(halves(c_first), one) + nn(halves(c_gate), three) + nn(halves(d_first), c_one) + nn(halves(d_gate), c_three)
    t_out = nn(halves(t_mixed), two) + nn(halves(value * gate), c_two)
    d_values[...] = -column(rates[...], width) * t_out
    d_rates[...] = -jnp.sum((values[...] * t_out).T, axis=0, keepdims=True)
    depth = d_rows.shape[1]
    low_side, upper_core = my_chip() <= LOW, my_core() == 0
    sides = []
    for (own, beside, across), (_, far) in zip(ends, cots[1::2]):
        near, far = own[:depth] + beside[:depth], across[...] + far[3 * span :]
        near, far = [jnp.where(upper_core, piece[:, :128], piece[:, 128:]) for piece in (near, far)]
        sides.append([jnp.where(low_side, near, far), jnp.where(low_side, far, near)])
    by_core = [[jnp.where(upper_core, a, b) for a, b in zip(*sides)], [jnp.where(upper_core, b, a) for a, b in zip(*sides)]]
    for m in range(2):
        parts = []
        for side in range(2):
            for i in range(2):
                for core in range(2):
                    start = (2 * m + i) * depth
                    parts.append(by_core[core][side][:, start : start + depth])
        d_rows[m] = jnp.concatenate(parts, axis=1)
    d_rows[2] = ends[0][0][depth:] + ends[0][1][depth:]


def over_chips(array, moves):
    pairs = [(2 * a + core, 2 * b + (core if a != b else 1 - core)) for a, b in enumerate(moves) for core in range(2)]
    return lax.ppermute(array, "tok", pairs)


def by_xor(array, by):
    return over_chips(array, [chip ^ by for chip in range(CHIPS)])


ACROSS = (0, 2, 1, 3)
INWARD = (2, 0, 3, 1)
OUTWARD = (1, 3, 0, 2)


def exchanged(array):
    turned = [(2 * a + core, 2 * b + 1 - core) for a, b in enumerate(ACROSS) for core in range(2)]
    return [array, lax.ppermute(array, "tok", turned), over_chips(array, ACROSS), core_swap(array)]


def both_cores(pieces):
    swapped = [core_swap(pieces[0])]
    for piece in pieces[1:]:
        swapped.append(core_swap(piece))
    return pieces + swapped


def hops(arrays, far):
    first = by_xor(arrays[1], 1)
    second = over_chips(arrays[2], far)
    third = over_chips(arrays[3], ACROSS)
    return first, second, third


def to_chain(arrays):
    return both_cores([arrays[0], *hops(arrays, INWARD)])


def from_chain_relayed(array):
    near = by_xor(array, 1)
    across = over_chips(array, ACROSS)
    far = by_xor(across, 1)
    return both_cores([array, near, across, far])


def to_earlier(array):
    groups = lax.axis_size("block")
    return lax.ppermute(array, "block", [(i, (i - 1) % groups) for i in range(groups)])


def to_later(array):
    groups = lax.axis_size("block")
    return lax.ppermute(array, "block", [(i, (i + 1) % groups) for i in range(groups)])


def per_device(queries, keys, values, rates, states, out_cot, final_cot):
    groups, size = lax.axis_size("block"), lax.axis_size("tok")
    depth, width = keys.shape
    own_rows = states[0]
    rows = own_rows.shape[1]
    if not (size == 2 * CHIPS and 4 * rows == 128 and depth == 128 and width == 8 * rows):
        return per_device_general(queries, keys, values, rates, states, out_cot, final_cot)
    span, tokens = 2 * rows, depth * size
    rates_row = rates.reshape(1, depth)
    state, square, wide = f32(3, span, width), f32(depth, width), f32(3 * span, width)
    sources = (keys, values, rates_row, own_rows, final_cot, queries, out_cot)
    longer, shorter = f32(2 * depth + 4 * rows, width), f32(2 * depth + 2 * rows, width)
    *packs, ahead = kernel_call(
        pack_body,
        [longer, longer, shorter, shorter, f32(2 * depth, width)],
        *sources,
        scratch=[pltpu.VMEM(array.shape, array.dtype) for array in sources] + [pltpu.SemaphoreType.DMA((len(sources),))],
        raw=True,
        limit=PACK_LIMIT,
    )
    pieces = to_chain(packs)
    ahead_pieces = to_chain([ahead] * CHIPS)
    half = bf16(tokens, width)
    own, last, *halved, kept, shifted, lead, sums = kernel_call(
        forward_body,
        [state, state, half, half, half, half, f32(5, span, tokens), state, f32(2, span, width), f32(8, width)],
        *pieces,
        scratch=[pltpu.VMEM((width, 4 * span), jnp.float32)],
    )
    all_sums = exchanged(sums)
    earlier = to_later(lead)
    weights = from_chain_relayed(own.reshape(3 * span, width))

    inners, arrived = [], []
    common = [own, shifted, last, *all_sums]
    sent = [state, f32(8, width)]
    (raw,) = kernel_call(functools.partial(first_body, groups - 1), [state], *common, *halved, kept)
    for section in range(groups - 1):
        source = groups - 1 - section
        if section == 0:
            body = functools.partial(apply_body, source)
            applied, payload, partial = kernel_call(body, [wide] + sent, own, raw, earlier, *ahead_pieces)
        else:
            body = functools.partial(section_body, source)
            payload, partial = kernel_call(
                body, sent, *common, *inners[-4:], *arrived[-1:], *halved, kept, applied, earlier
            )
        straight = to_earlier(partial)
        arrived.append(to_earlier(payload))
        inners += exchanged(straight)
    received = [*common, *inners, *arrived]
    (cot,) = kernel_call(functools.partial(terms_body, groups - 1), [wide], *received)
    near = by_xor(cot, 1)
    across = over_chips(cot, ACROSS)
    own_end, near_end, far, across_end = kernel_call(
        functools.partial(final_body, groups - 1),
        [f32(2 * rows, width)] * 2 + [f32(3 * span + rows, width), f32(rows, width)],
        *received,
        *halved,
        kept,
        applied,
        scratch=[pltpu.VMEM((width, 128), jnp.float32)],
    )
    near_end = by_xor(near_end, 1)
    across_end = over_chips(across_end, ACROSS)
    far = over_chips(far, OUTWARD)
    cots = [cot, near, across, far, own_end, near_end, across_end]
    swapped = []
    for piece in cots:
        swapped.append(core_swap(piece))
    cots = cots + swapped
    small, whole = bf16(depth, width), bf16(3, width, width)
    d_queries, *saved = kernel_call(
        query_body,
        [square, f32(5, depth, width), whole, whole, small, small, small, small],
        queries,
        out_cot,
        keys,
        values,
        rates_row,
        *weights,
        spill=1,
    )
    d_keys, d_values, d_rates, d_rows = kernel_call(
        token_body, [square, square, f32(1, depth), f32(3, rows, width)], values, rates_row, *saved, *cots, spill=4
    )
    return (d_queries, d_keys, d_values, d_rates.reshape(depth), d_rows[None])


def solution(mesh):
    return jax.shard_map(
        per_device,
        mesh=mesh,
        in_specs=(
            P(("block", "tok"), None),
            P(("block", "tok"), None),
            P(("block", "tok"), None),
            P(("block", "tok")),
            P("block", None, "tok", None),
            P(("block", "tok"), None),
            P(None, "tok", None),
        ),
        out_specs=(
            P(("block", "tok"), None),
            P(("block", "tok"), None),
            P(("block", "tok"), None),
            P(("block", "tok")),
            P("block", None, "tok", None),
        ),
        check_vma=False,
    )
```
